32 devices in a mesh: row: 8 (over z, y), col: 4 (over x, core).
Axes of the slice: x: 2, y: 2, z: 4, core: 2. Of those that a mesh axis runs over, the one named last changes fastest.
Arguments:
- hidden_in: bfloat16 [16384, 1024], P(('row', 'col')), may hold values from -6 to 6
- teacher: float32 [16384, 1024], P(('row', 'col')), may hold values from -6 to 6
- valid_mask: int32 [16384], replicated, may hold values from 0 to 1, as said below
- first_gain: float32 [1024], replicated, may hold values from 0.1 to 1.9
- second_gain: float32 [1024], replicated, may hold values from 0.1 to 1.9
- attention_in: bfloat16 [3, 1024, 1024], P(None, 'col', 'row'), may hold values from -0.1875 to 0.1875
- attention_out: bfloat16 [1024, 1024], P('row', 'col'), may hold values from -6 to 6
- feed_in: bfloat16 [2, 2624, 1024], P(None, 'col', 'row'), may hold values from -0.1875 to 0.1875
- feed_out: bfloat16 [1024, 2624], P('row', 'col'), may hold values from -0.125 to 0.125
Outputs:
- layer_out: bfloat16 [16384, 1024], P(('row', 'col'))
- loss: float32 [], replicated
- grad_input: float32 [16384, 1024], P(('row', 'col'))
- grad_first_gain: float32 [1024], replicated
- grad_second_gain: float32 [1024], replicated
- grad_attention_in: float32 [3, 1024, 1024], P(None, 'col', 'row')
- grad_attention_out: float32 [1024, 1024], P('row', 'col')
- grad_feed_in: float32 [2, 2624, 1024], P(None, 'col', 'row')
- grad_feed_out: float32 [1024, 2624], P('row', 'col')
The draws below stay inside these ranges and needn't reach their ends.
Inputs may be any that keep to these rules, and one draw needn't show every extreme that they name: `valid_mask`: 1 marks a token that serves as a key and counts in the loss; the first token of every sequence of 2048 is 1.
All inputs are finite; a program needn't handle non-finite values.
Results may differ from the reference program's by a relative error of at most 0.012.
Values may be sent and summed in bfloat16 or wider, within the bound.
No kernel may reach another device: no remote copies, remote signals or barrier semaphores. Data moves between devices by JAX's collectives and lax.ppermute only.
A program may use at most 256 MiB of HBM per device.

```python
import jax
import jax.numpy as jnp
from jax import lax

D = 1024
HEADS = 16
HD = 64
FF = 2624
SEQ_LEN = 2048
TOKENS = 16384


def draw_valid_mask(key, part):
    rolls = jax.random.randint(key, (TOKENS,), 0, 1000, dtype=jnp.int32)
    place = jnp.arange(TOKENS, dtype=jnp.int32)
    limit = 300 + 650 * place // TOKENS
    valid = (rolls < limit).astype(jnp.int32)
    first = place % SEQ_LEN == 0
    return jnp.where(first, 1, valid).astype(jnp.int32)


def block_scale(rng, extent, shards, low, high):
    level = 1.0
    for position, blocks in shards:
        draws = jax.random.uniform(jax.random.fold_in(jax.random.fold_in(rng, 6), position), (blocks,), jnp.float32, low / len(shards), high / len(shards))
        level = level * jnp.repeat(jnp.exp(draws), extent[position] // blocks).reshape((-1,) + (1,) * (len(extent) - 1 - position))
    return level


def bell_draw(own_key, extent, scale, most, pieces=(), kind=jnp.bfloat16):
    factor_of = block_scale(own_key, extent, pieces, -0.22, 0.18) if pieces else 1.0
    drawn = jax.random.normal(own_key, extent, jnp.float32) * scale * factor_of
    return jnp.minimum(jnp.maximum(drawn, -most), most).astype(kind)


def setup_inputs(seed: int = 0) -> dict:
    streams_of = jax.random.split(jax.random.key(seed), 10)
    return {
        "hidden_in": bell_draw(streams_of[0], (TOKENS, D), 1.0, 6.0, ((0, 32),)),
        "teacher": bell_draw(streams_of[1], (TOKENS, D), 1.0, 6.0, ((0, 32),), jnp.float32),
        "valid_mask": draw_valid_mask(jax.random.fold_in(streams_of[9], 71), 0),
        "first_gain": jnp.clip(1.0 + 0.18 * jax.random.normal(streams_of[3], (D,), jnp.float32), 0.1, 1.9),
        "second_gain": jnp.clip(1.0 + 0.18 * jax.random.normal(streams_of[4], (D,), jnp.float32), 0.1, 1.9),
        "attention_in": bell_draw(streams_of[5], (3, D, D), D ** -0.5, 0.1875, ((1, 4), (2, 8))),
        "attention_out": bell_draw(streams_of[6], (D, D), (max(1, 3 * D // SEQ_LEN)) ** -0.5, 6.0, ((0, 8), (1, 4))),
        "feed_in": bell_draw(streams_of[7], (2, FF, D), D ** -0.5, 0.1875, ((1, 4), (2, 8))),
        "feed_out": bell_draw(streams_of[8], (D, FF), FF ** -0.5, 0.125, ((0, 8), (1, 4))),
    }


EPSILON = 1e-05
ROPE_BASE = 160000.0
FLOOR_SCORE = -1e+30
HIGHEST = lax.Precision.HIGHEST

@jax.custom_vjp
def low(v):
    return lax.optimization_barrier(v.astype(jnp.bfloat16)).astype(jnp.float32)

@jax.custom_vjp
def low_back(v):
    return v

def low_keep(v):
    return (low(v), None)

def low_pass(kept, grad):
    return (grad,)

def back_keep(v):
    return (v, None)

def back_low(kept, grad):
    return (low(grad),)
low.defvjp(low_keep, low_pass)
low_back.defvjp(back_keep, back_low)

def layer_norm(values):
    center = values - lax.optimization_barrier(jnp.mean(values, axis=-1, keepdims=True))
    return center * lax.rsqrt(lax.optimization_barrier(jnp.mean(center * center, axis=-1, keepdims=True)) + EPSILON)

def rotary_tables():
    half = HD // 2
    frequency = ROPE_BASE ** (-(jnp.arange(half, dtype=jnp.float32) * 2.0) / HD)
    angle = jnp.arange(SEQ_LEN, dtype=jnp.float32)[:, None] * frequency[None, :]
    angle = jnp.concatenate([angle, angle], axis=1)
    return (jnp.cos(angle), jnp.sin(angle))

def rotate(values, cosine, sine):
    half = values.shape[-1] // 2
    turned = jnp.concatenate([-values[..., half:], values[..., :half]], axis=-1)
    return values * cosine[:, None, :] + turned * sine[:, None, :]

def attend_sequence(parts):
    query, keys, values, live = parts
    scale = query.shape[-1] ** (-0.5)
    scores = low_back(jnp.einsum('qhd,khd->hqk', query, keys, precision=HIGHEST) * scale)
    scores = jnp.where(live[None, None, :] > 0, scores, FLOOR_SCORE)
    top = lax.optimization_barrier(jnp.max(scores, axis=-1, keepdims=True))
    weights = jnp.exp(scores - top)
    probs = weights / lax.optimization_barrier(jnp.sum(weights, axis=-1, keepdims=True))
    return jnp.einsum('hqk,khd->qhd', low(probs), values, precision=HIGHEST)

def forward(inputs, gain_one, gain_two, joint, projection, expand, shrink, target, live):
    tokens = inputs.shape[0]
    seqs = tokens // SEQ_LEN
    low_one = low(layer_norm(inputs) * gain_one)
    projected = jnp.einsum('td,icd->itc', low_one, joint, precision=HIGHEST)
    query = low_back(projected[0])
    keys = low_back(projected[1])
    values = low(low_back(projected[2]))
    shape = (seqs, SEQ_LEN, HEADS, HD)
    cosine, sine = rotary_tables()
    query = low(rotate(query.reshape(shape), cosine, sine))
    keys = low(rotate(keys.reshape(shape), cosine, sine))
    values = values.reshape(shape)
    mixed = lax.map(jax.checkpoint(attend_sequence), (query, keys, values, live.reshape(seqs, SEQ_LEN)))
    heads_out = low(low_back(mixed.reshape(tokens, D)))
    branch = low_back(jnp.einsum('tc,oc->to', heads_out, projection, precision=HIGHEST))
    middle = inputs + branch
    low_two = low(layer_norm(middle) * gain_two)
    hidden = jnp.einsum('td,ifd->itf', low_two, expand, precision=HIGHEST)
    gate = low_back(hidden[0])
    upper = low_back(hidden[1])
    activated = low(jax.nn.gelu(gate, approximate=False) * upper)
    feed = low_back(jnp.einsum('tf,of->to', activated, shrink, precision=HIGHEST))
    result = middle + feed
    error_term = result - target
    loss = jnp.sum(live * lax.optimization_barrier(jnp.sum(error_term * error_term, axis=1))) / (D * jnp.sum(live))
    return (result, loss)

def reference(hidden_in, teacher, valid_mask, first_gain, second_gain, attention_in, attention_out, feed_in, feed_out):
    live = valid_mask.astype(jnp.float32)
    target = teacher.astype(jnp.float32)

    def run(inputs, gain_one, gain_two, joint, projection, expand, shrink):
        return forward(inputs, gain_one, gain_two, joint, projection, expand, shrink, target, live)
    primal = (hidden_in.astype(jnp.float32), first_gain, second_gain, attention_in.astype(jnp.float32), attention_out.astype(jnp.float32), feed_in.astype(jnp.float32), feed_out.astype(jnp.float32))
    (result, loss), pull = jax.vjp(run, *primal)
    scale = jnp.asarray(D * TOKENS / 2.0, jnp.float32)
    grads = pull((jnp.zeros_like(result), scale))
    return (result.astype(jnp.bfloat16), loss, grads[0], grads[1], grads[2], grads[3], grads[4], grads[5], grads[6])
```

```python
import functools

import jax
import jax.numpy as jnp
from jax import lax
from jax.experimental import pallas as pl
from jax.experimental.pallas import tpu as pltpu
from jax.sharding import PartitionSpec as P

D = 1024
HD = 64
SEQ_LEN = 2048


EPSILON = 1e-05
ROPE_BASE = 160000.0
FLOOR_SCORE = -1e30


def layer_norm(values, gain):
    center = values - jnp.mean(values, axis=1, keepdims=True)
    inverse = lax.rsqrt(jnp.mean(center * center, axis=1, keepdims=True) + EPSILON)
    normed = center * inverse
    return (normed, inverse, (normed * gain).astype(jnp.bfloat16))


def norm_back(grad_low, normed, inverse, gain):
    scaled = grad_low * gain
    inner = jnp.mean(scaled * normed, axis=1, keepdims=True)
    centered = scaled - jnp.mean(scaled, axis=1, keepdims=True)
    return (inverse * (centered - normed * inner), jnp.sum(grad_low * normed, axis=0))


def rotary_tables(rows, width):
    half = width // 2
    frequency = ROPE_BASE ** (-(jnp.arange(half, dtype=jnp.float32) * 2.0) / width)
    place = (jnp.arange(rows, dtype=jnp.int32) % SEQ_LEN).astype(jnp.float32)
    angle = place[:, None] * frequency[None, :]
    angle = jnp.concatenate([angle, angle], axis=1)
    return (jnp.cos(angle), jnp.sin(angle))


def rotate(values, cosine, sine):
    half = values.shape[-1] // 2
    turned = jnp.concatenate([-values[..., half:], values[..., :half]], axis=-1)
    return values * cosine[:, None, :] + turned * sine[:, None, :]


def rotate_back(grads, cosine, sine):
    half = grads.shape[-1] // 2
    moved = grads * sine[:, None, :]
    turned = jnp.concatenate([moved[..., half:], -moved[..., :half]], axis=-1)
    return grads * cosine[:, None, :] + turned


def block_scores(query, keys, live, start, block):
    base = start // SEQ_LEN * SEQ_LEN
    picked = lax.dynamic_slice_in_dim(query, start, block, 0)
    window = lax.dynamic_slice_in_dim(keys, base, SEQ_LEN, 0)
    allowed = lax.dynamic_slice_in_dim(live, base, SEQ_LEN, 0)
    scores = jnp.einsum(
        "qhd,khd->hqk", picked, window, preferred_element_type=jnp.float32
    ) * query.shape[2] ** (-0.5)
    return (jnp.where(allowed[None, None, :] > 0, scores, FLOOR_SCORE), picked, window, base)


def attend(query, keys, values, live):
    rows, heads, width = query.shape
    block = min(512, SEQ_LEN)

    def one_block(index):
        start = index * block
        scores, picked, window, base = block_scores(query, keys, live, start, block)
        seq_values = lax.dynamic_slice_in_dim(values, base, SEQ_LEN, 0)
        top = jnp.max(scores, axis=2, keepdims=True)
        weights = jnp.exp(scores - top)
        total = jnp.sum(weights, axis=2, keepdims=True)
        probs = (weights / total).astype(jnp.bfloat16)
        mixed = jnp.einsum("hqk,khd->qhd", probs, seq_values, preferred_element_type=jnp.float32)
        return (mixed.astype(jnp.bfloat16), (top + jnp.log(total))[:, :, 0])

    mixed, log_total = lax.map(one_block, jnp.arange(rows // block, dtype=jnp.int32))
    return (mixed.reshape(rows, heads * width), log_total)


def attend_back(query, keys, values, live, log_total, grad_mixed):
    rows, heads, width = query.shape
    block = min(512, SEQ_LEN)
    scale = width ** (-0.5)
    zeros = jnp.zeros((rows, heads, width), jnp.float32)

    def one_block(index, carry):
        grad_query, grad_keys, grad_values = carry
        start = index * block
        scores, picked, window, base = block_scores(query, keys, live, start, block)
        probs = jnp.exp(scores - log_total[index][:, :, None])
        seq_values = lax.dynamic_slice_in_dim(values, base, SEQ_LEN, 0)
        grad_block = lax.dynamic_slice_in_dim(grad_mixed, start, block, 0)
        grad_probs = jnp.einsum(
            "qhd,khd->hqk", grad_block, seq_values, preferred_element_type=jnp.float32
        )
        inner = jnp.sum(probs * grad_probs, axis=2, keepdims=True)
        grad_scores = (probs * (grad_probs - inner)).astype(jnp.bfloat16)
        part_query = (
            jnp.einsum("hqk,khd->qhd", grad_scores, window, preferred_element_type=jnp.float32)
            * scale
        )
        part_keys = (
            jnp.einsum("hqk,qhd->khd", grad_scores, picked, preferred_element_type=jnp.float32)
            * scale
        )
        part_values = jnp.einsum(
            "hqk,qhd->khd",
            probs.astype(jnp.bfloat16),
            grad_block,
            preferred_element_type=jnp.float32,
        )
        grad_query = lax.dynamic_update_slice_in_dim(grad_query, part_query, start, 0)
        grad_keys = lax.dynamic_update_slice_in_dim(
            grad_keys, lax.dynamic_slice_in_dim(grad_keys, base, SEQ_LEN, 0) + part_keys, base, 0
        )
        grad_values = lax.dynamic_update_slice_in_dim(
            grad_values,
            lax.dynamic_slice_in_dim(grad_values, base, SEQ_LEN, 0) + part_values,
            base,
            0,
        )
        return (grad_query, grad_keys, grad_values)

    return lax.fori_loop(0, rows // block, one_block, (zeros, zeros, zeros))


def general_shards(
    hidden_in,
    teacher,
    valid_mask,
    first_gain,
    second_gain,
    attention_in,
    attention_out,
    feed_in,
    feed_out,
):
    columns = lax.axis_size("col")
    own_rows = hidden_in.shape[0]
    group = own_rows * columns
    own_start = lax.axis_index("col") * own_rows
    group_start = lax.axis_index("row") * group
    total_tokens = group * lax.axis_size("row")
    live_group = lax.dynamic_slice_in_dim(valid_mask, group_start, group, 0)
    live_own = lax.dynamic_slice_in_dim(live_group, own_start, own_rows, 0).astype(jnp.float32)
    valid_total = jnp.sum(valid_mask.astype(jnp.float32))
    joint_rows, attention_rows, feed_in_rows, feed_out_rows = (
        lax.all_gather(attention_in, "row", axis=2, tiled=True),
        lax.all_gather(attention_out, "row", axis=0, tiled=True),
        lax.all_gather(feed_in, "row", axis=2, tiled=True),
        lax.all_gather(feed_out, "row", axis=0, tiled=True),
    )
    inputs = hidden_in.astype(jnp.float32)
    normed_one, inverse_one, low_one = layer_norm(inputs, first_gain)
    joint = jnp.einsum(
        "rd,icd->ric",
        lax.all_gather(low_one, "col", axis=0, tiled=True),
        joint_rows,
        preferred_element_type=jnp.float32,
    )
    local_width = joint.shape[2]
    split = (group, local_width // HD, HD)
    cosine, sine = rotary_tables(group, HD)
    query = rotate(joint[:, 0].reshape(split), cosine, sine).astype(jnp.bfloat16)
    keys = rotate(joint[:, 1].reshape(split), cosine, sine).astype(jnp.bfloat16)
    values = joint[:, 2].reshape(split).astype(jnp.bfloat16)
    mixed, log_total = attend(query, keys, values, live_group)
    part = mixed
    branch = lax.psum_scatter(
        jnp.einsum("rc,oc->ro", part, attention_rows, preferred_element_type=jnp.float32),
        "col",
        scatter_dimension=0,
        tiled=True,
    )
    middle = inputs + branch
    normed_two, inverse_two, low_two = layer_norm(middle, second_gain)
    projected = jnp.einsum(
        "rd,ifd->rif",
        lax.all_gather(low_two, "col", axis=0, tiled=True),
        feed_in_rows,
        preferred_element_type=jnp.float32,
    )
    gate = projected[:, 0]
    upper = projected[:, 1]
    activated = (jax.nn.gelu(gate, approximate=False) * upper).astype(jnp.bfloat16)
    part = activated
    feed_branch = lax.psum_scatter(
        jnp.einsum("rf,of->ro", part, feed_out_rows, preferred_element_type=jnp.float32),
        "col",
        scatter_dimension=0,
        tiled=True,
    )
    result = middle + feed_branch
    error_term = result - teacher
    squares = jnp.sum(live_own * jnp.sum(error_term * error_term, axis=1))
    grad_result = (total_tokens * live_own)[:, None] * error_term / valid_total
    grad_low = grad_result.astype(jnp.bfloat16)
    piece = lax.all_gather(grad_low, "col", axis=0, tiled=True)
    part = activated
    grad_out = jnp.einsum("ro,rf->of", piece, part, preferred_element_type=jnp.float32)
    rows_grad = jnp.einsum("ro,of->rf", piece, feed_out_rows, preferred_element_type=jnp.float32)
    grad_act = rows_grad

    def geglu(first, second):
        return jax.nn.gelu(first, approximate=False) * second

    unused, pull = jax.vjp(geglu, gate, upper)
    grad_gate, grad_upper = pull(grad_act)
    grad_projected = jnp.stack([grad_gate, grad_upper], axis=1).astype(jnp.bfloat16)
    part = grad_projected
    grad_low_two = lax.psum_scatter(
        jnp.einsum("rif,ifd->rd", part, feed_in_rows, preferred_element_type=jnp.float32),
        "col",
        scatter_dimension=0,
        tiled=True,
    )
    grad_middle_norm, grad_second = norm_back(grad_low_two, normed_two, inverse_two, second_gain)
    grad_middle = grad_result + grad_middle_norm
    grad_branch = grad_middle.astype(jnp.bfloat16)
    piece = lax.all_gather(grad_branch, "col", axis=0, tiled=True)
    part = mixed
    grad_weight = jnp.einsum("ro,rc->oc", piece, part, preferred_element_type=jnp.float32)
    rows_grad = jnp.einsum("ro,oc->rc", piece, attention_rows, preferred_element_type=jnp.float32)
    grad_heads = rows_grad
    grad_attention_rows, grad_heads = (grad_weight, grad_heads)
    grad_mixed = grad_heads.astype(jnp.bfloat16)
    grad_query, grad_keys, grad_values = attend_back(
        query, keys, values, live_group, log_total, grad_mixed.reshape(split)
    )
    grad_joint = jnp.stack(
        [rotate_back(grad_query, cosine, sine), rotate_back(grad_keys, cosine, sine), grad_values],
        axis=1,
    )
    grad_joint = grad_joint.astype(jnp.bfloat16).reshape(group, 3, local_width)
    part = grad_joint
    grad_low_one = lax.psum_scatter(
        jnp.einsum("ric,icd->rd", part, joint_rows, preferred_element_type=jnp.float32).astype(
            jnp.bfloat16
        ),
        "col",
        scatter_dimension=0,
        tiled=True,
    ).astype(jnp.float32)
    grad_input_norm, grad_first = norm_back(grad_low_one, normed_one, inverse_one, first_gain)
    grad_input = grad_middle + grad_input_norm
    grad_joint_weight = jnp.einsum(
        "ric,rd->icd",
        grad_joint,
        lax.all_gather(low_one, "col", axis=0, tiled=True),
        preferred_element_type=jnp.float32,
    )
    grad_feed_weight = jnp.einsum(
        "rif,rd->ifd",
        grad_projected,
        lax.all_gather(low_two, "col", axis=0, tiled=True),
        preferred_element_type=jnp.float32,
    )
    grads = (
        lax.psum_scatter(
            grad_joint_weight.astype(jnp.bfloat16), "row", scatter_dimension=2, tiled=True
        ).astype(jnp.float32),
        lax.psum_scatter(
            grad_attention_rows.astype(jnp.bfloat16), "row", scatter_dimension=0, tiled=True
        ).astype(jnp.float32),
        lax.psum_scatter(
            grad_feed_weight.astype(jnp.bfloat16), "row", scatter_dimension=2, tiled=True
        ).astype(jnp.float32),
        lax.psum_scatter(
            grad_out.astype(jnp.bfloat16), "row", scatter_dimension=0, tiled=True
        ).astype(jnp.float32),
    )
    totals = lax.psum((grad_first, grad_second, squares), ("row", "col"))
    loss = totals[2] / (D * valid_total)
    return (
        result.astype(jnp.bfloat16),
        loss,
        grad_input,
        totals[0],
        totals[1],
        grads[0],
        grads[1],
        grads[2],
        grads[3],
    )


BF = jnp.bfloat16
F32 = jnp.float32
MASKED = -1e30
ROW_DIMS = (((1,), (1,)), ((), ()))
HEAD_DIMS = (((0,), (0,)), ((), ()))
PLAIN_DIMS = (((1,), (0,)), ((), ()))


def swap(values, axis, flip):
    size = lax.axis_size(axis)
    return lax.ppermute(values, axis, [(place, place ^ flip) for place in range(size)])


def row_blocks(block):
    blocks = [block]
    flip = lax.axis_size("row") // 2
    parts = [block] + [swap(block, "row", 2 * step) for step in range(1, flip)]
    blocks = []
    for part in parts:
        blocks += [part, swap(part, "row", 1)]
    return blocks


def dot(left, right, dims):
    return lax.dot_general(left, right, dims, preferred_element_type=F32)


def turn(values, cosine, sine):
    lane = lax.broadcasted_iota(jnp.int32, values.shape, 1)
    swapped = jnp.where(
        lane % HD < HD // 2, pltpu.roll(values, 2 * HD - HD // 2, 1), pltpu.roll(values, HD // 2, 1)
    )
    return values * cosine + swapped * sine


def project_kernel(row_ref, x0, x1, x2, x3, *rest):
    weights = rest[:8]
    cos_ref, sin_ref, bias_ref, tokens, joint, query, keys, values = rest[8:]
    step = pl.program_id(0)
    row = row_ref[0]

    @pl.when(step == 0)
    def _():
        for index, weight in enumerate(weights):
            start = pl.multiple_of((row ^ index) * 128, 128)
            joint[:, pl.ds(start, 128)] = weight[...]

    for index, source in enumerate((x0, x1, x2, x3)):

        @pl.when(step == index)
        def _(source=source):
            tokens[...] = source[...]

    width = joint.shape[0] // 3
    result = dot(tokens[...], joint[...], ROW_DIMS)
    cosine = cos_ref[...]
    sine = sin_ref[...]
    rows = result.shape[0]
    lane = lax.broadcasted_iota(jnp.int32, (rows, 128), 1)
    spare = lane % HD
    one = jnp.ones((rows, 128), F32)
    zero = jnp.zeros((rows, 128), F32)
    key_spare = jnp.where(spare == 0, bias_ref[...] * one, jnp.where(spare <= 3, one, zero))
    query_spare = jnp.where(spare == 0, one, zero)
    for pair in range(width // 128):
        at = pair * 128
        q = turn(result[:, at : at + 128], cosine, sine) * HD**-0.5
        k = turn(result[:, width + at : width + at + 128], cosine, sine)
        v = result[:, 2 * width + at : 2 * width + at + 128]
        for side in range(2):
            mine = (lane < HD) if side == 0 else (lane >= HD)
            query[2 * pair + side] = jnp.where(mine, q, query_spare).astype(BF)
            keys[2 * pair + side] = jnp.where(mine, k, key_spare).astype(BF)
            values[2 * pair + side] = jnp.where(mine, v, one).astype(BF)


def project(row, tokens, weights, cosine, sine, bias):
    rows = tokens[0].shape[0]
    total = rows * len(tokens)
    width = weights[0].shape[0]
    heads = width // 3 // HD
    whole = lambda array: pl.BlockSpec(array.shape, lambda i, r: (0, 0))
    table = pl.BlockSpec((rows, 128), lambda i, r: (i, 0))
    wide = pl.BlockSpec((heads, rows, 128), lambda i, r: (0, i, 0))
    joint_shape = jax.ShapeDtypeStruct((width, D), BF)
    head_shape = jax.ShapeDtypeStruct((heads, total, 128), BF)
    return pl.pallas_call(
        project_kernel,
        out_shape=(
            jax.ShapeDtypeStruct((total, D), BF),
            joint_shape,
            head_shape,
            head_shape,
            head_shape,
        ),
        grid_spec=pltpu.PrefetchScalarGridSpec(
            num_scalar_prefetch=1,
            grid=(len(tokens),),
            in_specs=[whole(t) for t in tokens]
            + [whole(w) for w in weights]
            + [table, table, pl.BlockSpec((rows, 1), lambda i, r: (i, 0))],
            out_specs=(
                pl.BlockSpec((rows, D), lambda i, r: (i, 0)),
                pl.BlockSpec((width, D), lambda i, r: (0, 0)),
                wide,
                wide,
                wide,
            ),
        ),
        name="project",
    )(row, *tokens, *weights, cosine, sine, bias)


def split_three(column):
    high = column.astype(BF).astype(F32)
    rest = column - high
    middle = rest.astype(BF).astype(F32)
    return high, middle, rest - middle


def attend_kernel(query, keys, values, mixed, exact, query_back):
    rows = mixed.shape[0]
    lane = lax.broadcasted_iota(jnp.int32, (rows, 128), 1)
    spare = lane % HD
    outs = []
    for side in range(2):
        q = query[side]
        scores = dot(q, keys[side], ROW_DIMS)
        top = jnp.max(scores, axis=1, keepdims=True)
        weights = jnp.exp(scores - top).astype(BF)
        out = dot(weights, values[side], PLAIN_DIMS)
        at = HD if side == 0 else 0
        total = out[:, at : at + 1]
        outs.append(out / total)
        high, middle, low = split_three(top + jnp.log(total))
        mine = (lane < HD) if side == 0 else (lane >= HD)
        extra = jnp.where(spare == 1, -high, jnp.where(spare == 2, -middle, -low))
        keep = jnp.logical_or(mine, jnp.logical_or(spare == 0, spare > 3))
        query_back[side] = jnp.where(keep, q.astype(F32), extra).astype(BF)
    both = jnp.where(lane < HD, outs[0], outs[1])
    exact[...] = both
    mixed[...] = both.astype(BF)


def attend_pairs(query, keys, values, block):
    heads, rows, _ = query.shape
    part = pl.BlockSpec((2, block, 128), lambda p, i: (p, i, 0))
    whole = pl.BlockSpec((2, rows, 128), lambda p, i: (p, 0, 0))
    out = pl.BlockSpec((block, 128), lambda p, i: (i, p))
    width = heads * HD
    return pl.pallas_call(
        attend_kernel,
        out_shape=(
            jax.ShapeDtypeStruct((rows, width), BF),
            jax.ShapeDtypeStruct((rows, width), F32),
            jax.ShapeDtypeStruct((heads, rows, 128), BF),
        ),
        grid=(heads // 2, rows // block),
        in_specs=[part, whole, whole],
        out_specs=(out, out, part),
        name="attend",
    )(query, keys, values)


def attend_back_kernel(query, grad, exact, keys, values, cos_ref, sin_ref, cos_all, sin_all, out, grad_keys, grad_values, *, chunk):
    pair = pl.program_id(0)
    step = pl.program_id(1)
    rows = grad.shape[0]
    total = keys.shape[1]
    width = out.shape[1] // 3
    lane = lax.broadcasted_iota(jnp.int32, (rows, 128), 1)
    spare = lane % HD

    @pl.when(step == 0)
    def _():
        grad_keys[...] = jnp.zeros_like(grad_keys)
        grad_values[...] = jnp.zeros_like(grad_values)

    product = grad[...].astype(F32) * exact[...]
    sides = []
    for side in range(2):
        q = query[side]
        mine = (lane < HD) if side == 0 else (lane >= HD)
        inner = jnp.sum(jnp.where(mine, product, 0.0), axis=1, keepdims=True)
        high, middle, low = split_three(inner)
        extra = jnp.where(
            spare == 0, -high, jnp.where(spare == 1, -middle, jnp.where(spare == 2, -low, 0.0))
        )
        g = jnp.where(mine, grad[...].astype(F32), extra).astype(BF)
        grad_query = jnp.zeros((128, rows), F32)
        for start in range(0, total, chunk):
            k = keys[side, start : start + chunk]
            v = values[side, start : start + chunk]
            probs = jnp.exp(dot(k, q, ROW_DIMS))
            slope = (probs * dot(v, g, ROW_DIMS)).astype(BF)
            grad_values[side, start : start + chunk] += dot(probs.astype(BF), g, PLAIN_DIMS)
            grad_keys[side, start : start + chunk] += dot(slope, q, PLAIN_DIMS)
            grad_query += dot(k, slope, HEAD_DIMS)
        sides.append(grad_query)
    row = lax.broadcasted_iota(jnp.int32, (128, rows), 0)
    both = jnp.where(row < HD, sides[0], sides[1]).T * HD**-0.5
    at = pl.multiple_of(pair * 128, 128)
    from_row = pl.multiple_of(step * rows, rows)
    out[pl.ds(from_row, rows), pl.ds(at, 128)] = turn(both, cos_ref[...], -sin_ref[...]).astype(BF)

    @pl.when(step == pl.num_programs(1) - 1)
    def _():
        for start in range(0, total, chunk):
            here = slice(start, start + chunk)
            low_half = lax.broadcasted_iota(jnp.int32, (chunk, 128), 1) < HD
            k = jnp.where(low_half, grad_keys[0, here], grad_keys[1, here])
            v = jnp.where(low_half, grad_values[0, here], grad_values[1, here])
            k = turn(k, cos_all[here], -sin_all[here])
            out[here, pl.ds(pl.multiple_of(width + pair * 128, 128), 128)] = k.astype(BF)
            out[here, pl.ds(pl.multiple_of(2 * width + pair * 128, 128), 128)] = v.astype(BF)


def attend_back_pairs(query, grad, exact, keys, values, cosine, sine, block, chunk):
    heads, rows, _ = query.shape
    width = heads * HD
    part = pl.BlockSpec((2, block, 128), lambda p, i: (p, i, 0))
    whole = pl.BlockSpec((2, rows, 128), lambda p, i: (p, 0, 0))
    column = pl.BlockSpec((block, 128), lambda p, i: (i, p))
    table = pl.BlockSpec((block, 128), lambda p, i: (i, 0))
    full = pl.BlockSpec((rows, 128), lambda p, i: (0, 0))
    return pl.pallas_call(
        functools.partial(attend_back_kernel, chunk=chunk),
        out_shape=jax.ShapeDtypeStruct((rows, 3 * width), BF),
        grid=(heads // 2, rows // block),
        in_specs=[part, column, column, whole, whole, table, table, full, full],
        out_specs=pl.BlockSpec((rows, 3 * width), lambda p, i: (0, 0)),
        scratch_shapes=[pltpu.VMEM((2, rows, 128), F32), pltpu.VMEM((2, rows, 128), F32)],
        name="attend_back",
    )(query, grad, exact, keys, values, cosine, sine, cosine, sine)


def feed_kernel(x0, x1, x2, x3, first, second, tokens, act, slope, gelu_out, part):
    step = pl.program_id(0)
    for index, source in enumerate((x0, x1, x2, x3)):

        @pl.when(step == index)
        def _(source=source):
            tokens[...] = source[...]

    x = tokens[...]
    gate = dot(x, first[0], ROW_DIMS)
    upper = dot(x, first[1], ROW_DIMS)
    phi = 0.5 * (1.0 + lax.erf(gate * 2**-0.5))
    gelu = gate * phi
    low = (gelu * upper).astype(BF)
    density = jnp.exp(-0.5 * gate * gate) * 0.3989422804014327
    act[...] = low
    slope[...] = (upper * (phi + gate * density)).astype(BF)
    gelu_out[...] = gelu.astype(BF)
    part[...] = dot(low, second[...], ROW_DIMS)


def feed(tokens, first, second):
    rows = tokens[0].shape[0]
    total = rows * len(tokens)
    hidden = first.shape[1]
    fixed = lambda array: pl.BlockSpec(array.shape, lambda i: (0,) * array.ndim)
    tall = pl.BlockSpec((rows, hidden), lambda i: (i, 0))
    wide = pl.BlockSpec((rows, D), lambda i: (i, 0))
    hidden_shape = jax.ShapeDtypeStruct((total, hidden), BF)
    return pl.pallas_call(
        feed_kernel,
        out_shape=(
            jax.ShapeDtypeStruct((total, D), BF),
            hidden_shape,
            hidden_shape,
            hidden_shape,
            jax.ShapeDtypeStruct((total, D), F32),
        ),
        grid=(len(tokens),),
        in_specs=[fixed(t) for t in tokens] + [fixed(first), fixed(second)],
        out_specs=(wide, tall, tall, tall, wide),
        name="feed",
    )(*tokens, first, second)


def feed_back_kernel(x0, x1, x2, x3, slope, gelu, first, second, grads, out, part):
    step = pl.program_id(0)
    for index, source in enumerate((x0, x1, x2, x3)):

        @pl.when(step == index)
        def _(source=source):
            grads[...] = source[...]

    grad_act = dot(grads[...], second[...], PLAIN_DIMS)
    gate = (grad_act * slope[...].astype(F32)).astype(BF)
    upper = (grad_act * gelu[...].astype(F32)).astype(BF)
    out[0] = gate
    out[1] = upper
    part[...] = dot(gate, first[0], PLAIN_DIMS) + dot(upper, first[1], PLAIN_DIMS)


def feed_back(grads, slope, gelu, first, second):
    rows = grads[0].shape[0]
    total = rows * len(grads)
    hidden = first.shape[1]
    fixed = lambda array: pl.BlockSpec(array.shape, lambda i: (0,) * array.ndim)
    tall = pl.BlockSpec((rows, hidden), lambda i: (i, 0))
    wide = pl.BlockSpec((rows, D), lambda i: (i, 0))
    return pl.pallas_call(
        feed_back_kernel,
        out_shape=(
            jax.ShapeDtypeStruct((total, D), BF),
            jax.ShapeDtypeStruct((2, total, hidden), BF),
            jax.ShapeDtypeStruct((total, D), F32),
        ),
        grid=(len(grads),),
        in_specs=[fixed(t) for t in grads] + [tall, tall, fixed(first), fixed(second)],
        out_specs=(wide, pl.BlockSpec((2, rows, hidden), lambda i: (0, i, 0)), wide),
        name="feed_back",
    )(*grads, slope, gelu, first, second)


def spread(block):
    far = swap(block, "col", 2)
    near = swap(block, "col", 1)
    return [block, near, far, swap(far, "col", 1)]


def collect(part):
    rows = part.shape[0] // 4
    far_near = swap(part[3 * rows :].astype(BF), "col", 1).astype(F32)
    far = (part[2 * rows : 3 * rows] + far_near).astype(BF)
    far = swap(far, "col", 2)
    near = swap(part[rows : 2 * rows].astype(BF), "col", 1).astype(F32)
    return part[:rows] + near + far.astype(F32)


def add_all(values):
    for axis in ("col", "row"):
        flip = 1
        while flip < lax.axis_size(axis):
            values = values + swap(values, axis, flip)
            flip *= 2
    return values


def group_shards(
    hidden_in,
    teacher,
    valid_mask,
    first_gain,
    second_gain,
    attention_in,
    attention_out,
    feed_in,
    feed_out,
):
    own = hidden_in.shape[0]
    column = lax.axis_index("col")
    row = lax.axis_index("row")
    group = own * 4
    group_start = row * group
    total_tokens = group * lax.axis_size("row")
    valid_total = jnp.sum(valid_mask.astype(F32))
    live_group = lax.dynamic_slice_in_dim(valid_mask, group_start, group, 0)
    live_own = lax.dynamic_slice_in_dim(live_group, column * own, own, 0).astype(F32)
    order = jnp.arange(4, dtype=jnp.int32) ^ column
    live = jnp.take(live_group.reshape(4, own), order, axis=0).reshape(group, 1)
    bias = jnp.where(live > 0, 0.0, MASKED).astype(F32)
    place = (order[:, None] * own + jnp.arange(own, dtype=jnp.int32)[None, :]).reshape(group)
    half = HD // 2
    frequency = ROPE_BASE ** (-(jnp.arange(half, dtype=F32) * 2.0) / HD)
    angle = place.astype(F32)[:, None] * jnp.tile(frequency, 4)[None, :]
    sign = jnp.where(jnp.arange(128) % HD < half, -1.0, 1.0)
    cosine = jnp.cos(angle)
    sine = jnp.sin(angle) * sign[None, :]

    inputs = hidden_in.astype(F32)
    normed_one, inverse_one, low_one = layer_norm(inputs, first_gain)
    width = attention_in.shape[1]
    joint_blocks = row_blocks(attention_in.reshape(3 * width, attention_in.shape[2]))
    tokens = spread(low_one)
    attention_rows = lax.all_gather(attention_out, "row", axis=0, tiled=True)
    feed_in_rows = lax.all_gather(feed_in, "row", axis=2, tiled=True)
    feed_out_rows = lax.all_gather(feed_out, "row", axis=0, tiled=True)
    all_low_one, joint, query, keys, values = project(
        row.reshape(1), tokens, joint_blocks, cosine, sine, bias
    )
    mixed, exact, query_back = attend_pairs(query, keys, values, 512)

    attention_twin = swap(attention_rows, "col", 2)
    mixed_twin = swap(mixed[2 * own :], "col", 2)
    mixed_own = mixed[: 2 * own]
    near = dot(mixed_own[own:], attention_rows, ROW_DIMS) + dot(
        mixed_twin[own:], attention_twin, ROW_DIMS
    )
    near = swap(near, "col", 1)
    branch = (
        dot(mixed_own[:own], attention_rows, ROW_DIMS)
        + dot(mixed_twin[:own], attention_twin, ROW_DIMS)
        + near
    )
    middle = inputs + branch
    normed_two, inverse_two, low_two = layer_norm(middle, second_gain)

    chunks = 2
    size = own // chunks
    results = []
    squares = jnp.float32(0.0)
    grad_second = jnp.zeros((D,), F32)
    grad_out = 0.0
    grad_feed = 0.0
    grad_middles = []
    for index in range(chunks):
        here = slice(index * size, (index + 1) * size)
        all_low_two, act, slope, gelu, part = feed(
            spread(low_two[here]), feed_in_rows, feed_out_rows
        )
        result = middle[here] + collect(part)
        error_term = result - teacher[here]
        live_here = live_own[here]
        squares = squares + jnp.sum(live_here * jnp.sum(error_term * error_term, axis=1))
        grad_result = (total_tokens * live_here)[:, None] * error_term / valid_total
        all_grads, grad_hidden, part = feed_back(
            spread(grad_result.astype(BF)), slope, gelu, feed_in_rows, feed_out_rows
        )
        grad_low_two = collect(part)
        grad_norm, grad_gain = norm_back(
            grad_low_two, normed_two[here], inverse_two[here], second_gain
        )
        grad_second = grad_second + grad_gain
        grad_middles.append(grad_result + grad_norm)
        grad_out = grad_out + dot(all_grads, act, HEAD_DIMS)
        grad_feed = grad_feed + jnp.einsum(
            "irf,rd->ifd", grad_hidden, all_low_two, preferred_element_type=F32
        )
        results.append(result)
    result = jnp.concatenate(results, axis=0)
    grad_middle = jnp.concatenate(grad_middles, axis=0)
    grad_branch = grad_middle.astype(BF)

    branch_pair = jnp.concatenate([grad_branch, swap(grad_branch, "col", 1)], axis=0)
    grad_mixed_twin = swap(dot(branch_pair, attention_twin, PLAIN_DIMS).astype(BF), "col", 2)
    grad_mixed = jnp.concatenate(
        [dot(branch_pair, attention_rows, PLAIN_DIMS).astype(BF), grad_mixed_twin], axis=0
    )
    grad_attention_far = swap(dot(branch_pair, mixed_twin, HEAD_DIMS).astype(BF), "col", 2)
    grad_attention = dot(branch_pair, mixed_own, HEAD_DIMS) + grad_attention_far.astype(F32)
    grad_joint = attend_back_pairs(
        query_back, grad_mixed, exact, keys, values, cosine, sine, 512, 512
    )
    grad_low_one = collect(dot(grad_joint, joint, PLAIN_DIMS))
    grad_joint_weight = dot(grad_joint, all_low_one, HEAD_DIMS)
    grad_first = jnp.sum(grad_joint_weight * joint.astype(F32), axis=0) / first_gain
    totals = add_all(
        jnp.concatenate(
            [grad_first.reshape(8, 128), grad_second.reshape(8, 128), jnp.full((8, 128), squares)]
        )
    )
    grad_input_norm, _ = norm_back(grad_low_one, normed_one, inverse_one, first_gain)
    grad_input = grad_middle + grad_input_norm
    grads = (
        lax.psum_scatter(
            grad_joint_weight.astype(BF).reshape(3, width, D),
            "row",
            scatter_dimension=2,
            tiled=True,
        ).astype(F32),
        lax.psum_scatter(
            grad_attention.astype(BF), "row", scatter_dimension=0, tiled=True
        ).astype(F32),
        lax.psum_scatter(grad_feed.astype(BF), "row", scatter_dimension=2, tiled=True).astype(F32),
        lax.psum_scatter(grad_out.astype(BF), "row", scatter_dimension=0, tiled=True).astype(F32),
    )
    loss = totals[16, 0] / (D * valid_total)
    return (
        result.astype(BF),
        loss,
        grad_input,
        totals[:8].reshape(D),
        totals[8:16].reshape(D),
        grads[0],
        grads[1],
        grads[2],
        grads[3],
    )


def shards(hidden_in, teacher, valid_mask, first_gain, second_gain, attention_in, *rest):
    fits = (
        lax.axis_size("col") == 4
        and lax.axis_size("row") == 8
        and hidden_in.shape[0] * 4 == SEQ_LEN
        and attention_in.shape[1] % 128 == 0
    )
    body = group_shards if fits else general_shards
    return body(
        hidden_in, teacher, valid_mask, first_gain, second_gain, attention_in, *rest
    )


def solution(mesh):
    in_specs = (
        P(("row", "col"), None),
        P(("row", "col"), None),
        P(),
        P(),
        P(),
        P(None, "col", "row"),
        P("row", "col"),
        P(None, "col", "row"),
        P("row", "col"),
    )
    out_specs = (
        P(("row", "col"), None),
        P(),
        P(("row", "col"), None),
        P(),
        P(),
        P(None, "col", "row"),
        P("row", "col"),
        P(None, "col", "row"),
        P("row", "col"),
    )
    return jax.shard_map(shards, mesh=mesh, in_specs=in_specs, out_specs=out_specs, check_vma=False)
```

```python
import functools

import jax
import jax.numpy as jnp
from jax import lax
from jax.experimental import pallas as pl
from jax.experimental.pallas import tpu as pltpu
from jax.sharding import PartitionSpec as P

D = 1024
HD = 64
SEQ_LEN = 2048


EPSILON = 1e-05
ROPE_BASE = 160000.0
FLOOR_SCORE = -1e30


def layer_norm(values, gain):
    center = values - jnp.mean(values, axis=1, keepdims=True)
    inverse = lax.rsqrt(jnp.mean(center * center, axis=1, keepdims=True) + EPSILON)
    normed = center * inverse
    return (normed, inverse, (normed * gain).astype(jnp.bfloat16))


def norm_back(grad_low, normed, inverse, gain):
    scaled = grad_low * gain
    inner = jnp.mean(scaled * normed, axis=1, keepdims=True)
    centered = scaled - jnp.mean(scaled, axis=1, keepdims=True)
    return (inverse * (centered - normed * inner), jnp.sum(grad_low * normed, axis=0))


def rotary_tables(rows, width):
    half = width // 2
    frequency = ROPE_BASE ** (-(jnp.arange(half, dtype=jnp.float32) * 2.0) / width)
    place = (jnp.arange(rows, dtype=jnp.int32) % SEQ_LEN).astype(jnp.float32)
    angle = place[:, None] * frequency[None, :]
    angle = jnp.concatenate([angle, angle], axis=1)
    return (jnp.cos(angle), jnp.sin(angle))


def rotate(values, cosine, sine):
    half = values.shape[-1] // 2
    turned = jnp.concatenate([-values[..., half:], values[..., :half]], axis=-1)
    return values * cosine[:, None, :] + turned * sine[:, None, :]


def rotate_back(grads, cosine, sine):
    half = grads.shape[-1] // 2
    moved = grads * sine[:, None, :]
    turned = jnp.concatenate([moved[..., half:], -moved[..., :half]], axis=-1)
    return grads * cosine[:, None, :] + turned


def block_scores(query, keys, live, start, block):
    base = start // SEQ_LEN * SEQ_LEN
    picked = lax.dynamic_slice_in_dim(query, start, block, 0)
    window = lax.dynamic_slice_in_dim(keys, base, SEQ_LEN, 0)
    allowed = lax.dynamic_slice_in_dim(live, base, SEQ_LEN, 0)
    scores = jnp.einsum(
        "qhd,khd->hqk", picked, window, preferred_element_type=jnp.float32
    ) * query.shape[2] ** (-0.5)
    return (jnp.where(allowed[None, None, :] > 0, scores, FLOOR_SCORE), picked, window, base)


def attend(query, keys, values, live):
    rows, heads, width = query.shape
    block = min(512, SEQ_LEN)

    def one_block(index):
        start = index * block
        scores, picked, window, base = block_scores(query, keys, live, start, block)
        seq_values = lax.dynamic_slice_in_dim(values, base, SEQ_LEN, 0)
        top = jnp.max(scores, axis=2, keepdims=True)
        weights = jnp.exp(scores - top)
        total = jnp.sum(weights, axis=2, keepdims=True)
        probs = (weights / total).astype(jnp.bfloat16)
        mixed = jnp.einsum("hqk,khd->qhd", probs, seq_values, preferred_element_type=jnp.float32)
        return (mixed.astype(jnp.bfloat16), (top + jnp.log(total))[:, :, 0])

    mixed, log_total = lax.map(one_block, jnp.arange(rows // block, dtype=jnp.int32))
    return (mixed.reshape(rows, heads * width), log_total)


def attend_back(query, keys, values, live, log_total, grad_mixed):
    rows, heads, width = query.shape
    block = min(512, SEQ_LEN)
    scale = width ** (-0.5)
    zeros = jnp.zeros((rows, heads, width), jnp.float32)

    def one_block(index, carry):
        grad_query, grad_keys, grad_values = carry
        start = index * block
        scores, picked, window, base = block_scores(query, keys, live, start, block)
        probs = jnp.exp(scores - log_total[index][:, :, None])
        seq_values = lax.dynamic_slice_in_dim(values, base, SEQ_LEN, 0)
        grad_block = lax.dynamic_slice_in_dim(grad_mixed, start, block, 0)
        grad_probs = jnp.einsum(
            "qhd,khd->hqk", grad_block, seq_values, preferred_element_type=jnp.float32
        )
        inner = jnp.sum(probs * grad_probs, axis=2, keepdims=True)
        grad_scores = (probs * (grad_probs - inner)).astype(jnp.bfloat16)
        part_query = (
            jnp.einsum("hqk,khd->qhd", grad_scores, window, preferred_element_type=jnp.float32)
            * scale
        )
        part_keys = (
            jnp.einsum("hqk,qhd->khd", grad_scores, picked, preferred_element_type=jnp.float32)
            * scale
        )
        part_values = jnp.einsum(
            "hqk,qhd->khd",
            probs.astype(jnp.bfloat16),
            grad_block,
            preferred_element_type=jnp.float32,
        )
        grad_query = lax.dynamic_update_slice_in_dim(grad_query, part_query, start, 0)
        grad_keys = lax.dynamic_update_slice_in_dim(
            grad_keys, lax.dynamic_slice_in_dim(grad_keys, base, SEQ_LEN, 0) + part_keys, base, 0
        )
        grad_values = lax.dynamic_update_slice_in_dim(
            grad_values,
            lax.dynamic_slice_in_dim(grad_values, base, SEQ_LEN, 0) + part_values,
            base,
            0,
        )
        return (grad_query, grad_keys, grad_values)

    return lax.fori_loop(0, rows // block, one_block, (zeros, zeros, zeros))


def general_shards(
    hidden_in,
    teacher,
    valid_mask,
    first_gain,
    second_gain,
    attention_in,
    attention_out,
    feed_in,
    feed_out,
):
    columns = lax.axis_size("col")
    own_rows = hidden_in.shape[0]
    group = own_rows * columns
    own_start = lax.axis_index("col") * own_rows
    group_start = lax.axis_index("row") * group
    total_tokens = group * lax.axis_size("row")
    live_group = lax.dynamic_slice_in_dim(valid_mask, group_start, group, 0)
    live_own = lax.dynamic_slice_in_dim(live_group, own_start, own_rows, 0).astype(jnp.float32)
    valid_total = jnp.sum(valid_mask.astype(jnp.float32))
    joint_rows, attention_rows, feed_in_rows, feed_out_rows = (
        lax.all_gather(attention_in, "row", axis=2, tiled=True),
        lax.all_gather(attention_out, "row", axis=0, tiled=True),
        lax.all_gather(feed_in, "row", axis=2, tiled=True),
        lax.all_gather(feed_out, "row", axis=0, tiled=True),
    )
    inputs = hidden_in.astype(jnp.float32)
    normed_one, inverse_one, low_one = layer_norm(inputs, first_gain)
    joint = jnp.einsum(
        "rd,icd->ric",
        lax.all_gather(low_one, "col", axis=0, tiled=True),
        joint_rows,
        preferred_element_type=jnp.float32,
    )
    local_width = joint.shape[2]
    split = (group, local_width // HD, HD)
    cosine, sine = rotary_tables(group, HD)
    query = rotate(joint[:, 0].reshape(split), cosine, sine).astype(jnp.bfloat16)
    keys = rotate(joint[:, 1].reshape(split), cosine, sine).astype(jnp.bfloat16)
    values = joint[:, 2].reshape(split).astype(jnp.bfloat16)
    mixed, log_total = attend(query, keys, values, live_group)
    part = mixed
    branch = lax.psum_scatter(
        jnp.einsum("rc,oc->ro", part, attention_rows, preferred_element_type=jnp.float32),
        "col",
        scatter_dimension=0,
        tiled=True,
    )
    middle = inputs + branch
    normed_two, inverse_two, low_two = layer_norm(middle, second_gain)
    projected = jnp.einsum(
        "rd,ifd->rif",
        lax.all_gather(low_two, "col", axis=0, tiled=True),
        feed_in_rows,
        preferred_element_type=jnp.float32,
    )
    gate = projected[:, 0]
    upper = projected[:, 1]
    activated = (jax.nn.gelu(gate, approximate=False) * upper).astype(jnp.bfloat16)
    part = activated
    feed_branch = lax.psum_scatter(
        jnp.einsum("rf,of->ro", part, feed_out_rows, preferred_element_type=jnp.float32),
        "col",
        scatter_dimension=0,
        tiled=True,
    )
    result = middle + feed_branch
    error_term = result - teacher
    squares = jnp.sum(live_own * jnp.sum(error_term * error_term, axis=1))
    grad_result = (total_tokens * live_own)[:, None] * error_term / valid_total
    grad_low = grad_result.astype(jnp.bfloat16)
    piece = lax.all_gather(grad_low, "col", axis=0, tiled=True)
    part = activated
    grad_out = jnp.einsum("ro,rf->of", piece, part, preferred_element_type=jnp.float32)
    rows_grad = jnp.einsum("ro,of->rf", piece, feed_out_rows, preferred_element_type=jnp.float32)
    grad_act = rows_grad

    def geglu(first, second):
        return jax.nn.gelu(first, approximate=False) * second

    unused, pull = jax.vjp(geglu, gate, upper)
    grad_gate, grad_upper = pull(grad_act)
    grad_projected = jnp.stack([grad_gate, grad_upper], axis=1).astype(jnp.bfloat16)
    part = grad_projected
    grad_low_two = lax.psum_scatter(
        jnp.einsum("rif,ifd->rd", part, feed_in_rows, preferred_element_type=jnp.float32),
        "col",
        scatter_dimension=0,
        tiled=True,
    )
    grad_middle_norm, grad_second = norm_back(grad_low_two, normed_two, inverse_two, second_gain)
    grad_middle = grad_result + grad_middle_norm
    grad_branch = grad_middle.astype(jnp.bfloat16)
    piece = lax.all_gather(grad_branch, "col", axis=0, tiled=True)
    part = mixed
    grad_weight = jnp.einsum("ro,rc->oc", piece, part, preferred_element_type=jnp.float32)
    rows_grad = jnp.einsum("ro,oc->rc", piece, attention_rows, preferred_element_type=jnp.float32)
    grad_heads = rows_grad
    grad_attention_rows, grad_heads = (grad_weight, grad_heads)
    grad_mixed = grad_heads.astype(jnp.bfloat16)
    grad_query, grad_keys, grad_values = attend_back(
        query, keys, values, live_group, log_total, grad_mixed.reshape(split)
    )
    grad_joint = jnp.stack(
        [rotate_back(grad_query, cosine, sine), rotate_back(grad_keys, cosine, sine), grad_values],
        axis=1,
    )
    grad_joint = grad_joint.astype(jnp.bfloat16).reshape(group, 3, local_width)
    part = grad_joint
    grad_low_one = lax.psum_scatter(
        jnp.einsum("ric,icd->rd", part, joint_rows, preferred_element_type=jnp.float32).astype(
            jnp.bfloat16
        ),
        "col",
        scatter_dimension=0,
        tiled=True,
    ).astype(jnp.float32)
    grad_input_norm, grad_first = norm_back(grad_low_one, normed_one, inverse_one, first_gain)
    grad_input = grad_middle + grad_input_norm
    grad_joint_weight = jnp.einsum(
        "ric,rd->icd",
        grad_joint,
        lax.all_gather(low_one, "col", axis=0, tiled=True),
        preferred_element_type=jnp.float32,
    )
    grad_feed_weight = jnp.einsum(
        "rif,rd->ifd",
        grad_projected,
        lax.all_gather(low_two, "col", axis=0, tiled=True),
        preferred_element_type=jnp.float32,
    )
    grads = (
        lax.psum_scatter(
            grad_joint_weight.astype(jnp.bfloat16), "row", scatter_dimension=2, tiled=True
        ).astype(jnp.float32),
        lax.psum_scatter(
            grad_attention_rows.astype(jnp.bfloat16), "row", scatter_dimension=0, tiled=True
        ).astype(jnp.float32),
        lax.psum_scatter(
            grad_feed_weight.astype(jnp.bfloat16), "row", scatter_dimension=2, tiled=True
        ).astype(jnp.float32),
        lax.psum_scatter(
            grad_out.astype(jnp.bfloat16), "row", scatter_dimension=0, tiled=True
        ).astype(jnp.float32),
    )
    totals = lax.psum((grad_first, grad_second, squares), ("row", "col"))
    loss = totals[2] / (D * valid_total)
    return (
        result.astype(jnp.bfloat16),
        loss,
        grad_input,
        totals[0],
        totals[1],
        grads[0],
        grads[1],
        grads[2],
        grads[3],
    )


BF = jnp.bfloat16
F32 = jnp.float32
MASKED = -1e30
ROW_DIMS = (((1,), (1,)), ((), ()))
HEAD_DIMS = (((0,), (0,)), ((), ()))
PLAIN_DIMS = (((1,), (0,)), ((), ()))


def swap(values, axis, flip):
    size = lax.axis_size(axis)
    return lax.ppermute(values, axis, [(place, place ^ flip) for place in range(size)])


def row_blocks(block):
    blocks = [block]
    flip = lax.axis_size("row") // 2
    parts = [block] + [swap(block, "row", 2 * step) for step in range(1, flip)]
    blocks = []
    for part in parts:
        blocks += [part, swap(part, "row", 1)]
    return blocks


def dot(left, right, dims):
    return lax.dot_general(left, right, dims, preferred_element_type=F32)


def turn(values, cosine, sine):
    lane = lax.broadcasted_iota(jnp.int32, values.shape, 1)
    swapped = jnp.where(
        lane % HD < HD // 2, pltpu.roll(values, 2 * HD - HD // 2, 1), pltpu.roll(values, HD // 2, 1)
    )
    return values * cosine + swapped * sine


def project_kernel(row_ref, x0, x1, x2, x3, *rest):
    weights = rest[:8]
    cos_ref, sin_ref, bias_ref, tokens, joint, query, keys, values = rest[8:]
    step = pl.program_id(0)
    row = row_ref[0]

    @pl.when(step == 0)
    def _():
        for index, weight in enumerate(weights):
            start = pl.multiple_of((row ^ index) * 128, 128)
            joint[:, pl.ds(start, 128)] = weight[...]

    for index, source in enumerate((x0, x1, x2, x3)):

        @pl.when(step == index)
        def _(source=source):
            tokens[...] = source[...]

    width = joint.shape[0] // 3
    result = dot(tokens[...], joint[...], ROW_DIMS)
    cosine = cos_ref[...]
    sine = sin_ref[...]
    rows = result.shape[0]
    lane = lax.broadcasted_iota(jnp.int32, (rows, 128), 1)
    spare = lane % HD
    one = jnp.ones((rows, 128), F32)
    zero = jnp.zeros((rows, 128), F32)
    key_spare = jnp.where(spare == 0, bias_ref[...] * one, jnp.where(spare <= 3, one, zero))
    query_spare = jnp.where(spare == 0, one, zero)
    for pair in range(width // 128):
        at = pair * 128
        q = turn(result[:, at : at + 128], cosine, sine) * HD**-0.5
        k = turn(result[:, width + at : width + at + 128], cosine, sine)
        v = result[:, 2 * width + at : 2 * width + at + 128]
        for side in range(2):
            mine = (lane < HD) if side == 0 else (lane >= HD)
            query[2 * pair + side] = jnp.where(mine, q, query_spare).astype(BF)
            keys[2 * pair + side] = jnp.where(mine, k, key_spare).astype(BF)
            values[2 * pair + side] = jnp.where(mine, v, one).astype(BF)


def project(row, tokens, weights, cosine, sine, bias):
    rows = tokens[0].shape[0]
    total = rows * len(tokens)
    width = weights[0].shape[0]
    heads = width // 3 // HD
    whole = lambda array: pl.BlockSpec(array.shape, lambda i, r: (0, 0))
    table = pl.BlockSpec((rows, 128), lambda i, r: (i, 0))
    wide = pl.BlockSpec((heads, rows, 128), lambda i, r: (0, i, 0))
    joint_shape = jax.ShapeDtypeStruct((width, D), BF)
    head_shape = jax.ShapeDtypeStruct((heads, total, 128), BF)
    return pl.pallas_call(
        project_kernel,
        out_shape=(
            jax.ShapeDtypeStruct((total, D), BF),
            joint_shape,
            head_shape,
            head_shape,
            head_shape,
        ),
        grid_spec=pltpu.PrefetchScalarGridSpec(
            num_scalar_prefetch=1,
            grid=(len(tokens),),
            in_specs=[whole(t) for t in tokens]
            + [whole(w) for w in weights]
            + [table, table, pl.BlockSpec((rows, 1), lambda i, r: (i, 0))],
            out_specs=(
                pl.BlockSpec((rows, D), lambda i, r: (i, 0)),
                pl.BlockSpec((width, D), lambda i, r: (0, 0)),
                wide,
                wide,
                wide,
            ),
        ),
        cost_estimate=pl.CostEstimate(
            flops=2 * total * width * D, transcendentals=0, bytes_accessed=8 * total * D
        ),
        name="project",
    )(row, *tokens, *weights, cosine, sine, bias)


def split_three(column):
    high = column.astype(BF).astype(F32)
    rest = column - high
    middle = rest.astype(BF).astype(F32)
    return high, middle, rest - middle


def attend_kernel(query, keys, values, mixed, exact, query_back):
    rows = mixed.shape[0]
    lane = lax.broadcasted_iota(jnp.int32, (rows, 128), 1)
    spare = lane % HD
    outs = []
    for side in range(2):
        q = query[side]
        scores = dot(q, keys[side], ROW_DIMS)
        top = jnp.max(scores, axis=1, keepdims=True)
        weights = jnp.exp(scores - top).astype(BF)
        out = dot(weights, values[side], PLAIN_DIMS)
        at = HD if side == 0 else 0
        total = out[:, at : at + 1]
        outs.append(out / total)
        high, middle, low = split_three(top + jnp.log(total))
        mine = (lane < HD) if side == 0 else (lane >= HD)
        extra = jnp.where(spare == 1, -high, jnp.where(spare == 2, -middle, -low))
        keep = jnp.logical_or(mine, jnp.logical_or(spare == 0, spare > 3))
        query_back[side] = jnp.where(keep, q.astype(F32), extra).astype(BF)
    both = jnp.where(lane < HD, outs[0], outs[1])
    exact[...] = both
    mixed[...] = both.astype(BF)


def attend_pairs(query, keys, values, block):
    heads, rows, _ = query.shape
    part = pl.BlockSpec((2, block, 128), lambda p, i: (p, i, 0))
    whole = pl.BlockSpec((2, rows, 128), lambda p, i: (p, 0, 0))
    out = pl.BlockSpec((block, 128), lambda p, i: (i, p))
    width = heads * HD
    return pl.pallas_call(
        attend_kernel,
        out_shape=(
            jax.ShapeDtypeStruct((rows, width), BF),
            jax.ShapeDtypeStruct((rows, width), F32),
            jax.ShapeDtypeStruct((heads, rows, 128), BF),
        ),
        grid=(heads // 2, rows // block),
        in_specs=[part, whole, whole],
        out_specs=(out, out, part),
        cost_estimate=pl.CostEstimate(
            flops=16 * rows * rows * width, transcendentals=0, bytes_accessed=8 * rows * width
        ),
        name="attend",
    )(query, keys, values)


def attend_back_kernel(query, grad, exact, keys, values, cos_ref, sin_ref, cos_all, sin_all, out, grad_keys, grad_values, *, chunk):
    pair = pl.program_id(0)
    step = pl.program_id(1)
    rows = grad.shape[0]
    total = keys.shape[1]
    width = out.shape[1] // 3
    lane = lax.broadcasted_iota(jnp.int32, (rows, 128), 1)
    spare = lane % HD

    @pl.when(step == 0)
    def _():
        grad_keys[...] = jnp.zeros_like(grad_keys)
        grad_values[...] = jnp.zeros_like(grad_values)

    product = grad[...].astype(F32) * exact[...]
    sides = []
    for side in range(2):
        q = query[side]
        mine = (lane < HD) if side == 0 else (lane >= HD)
        inner = jnp.sum(jnp.where(mine, product, 0.0), axis=1, keepdims=True)
        high, middle, low = split_three(inner)
        extra = jnp.where(
            spare == 0, -high, jnp.where(spare == 1, -middle, jnp.where(spare == 2, -low, 0.0))
        )
        g = jnp.where(mine, grad[...].astype(F32), extra).astype(BF)
        grad_query = jnp.zeros((128, rows), F32)
        for start in range(0, total, chunk):
            k = keys[side, start : start + chunk]
            v = values[side, start : start + chunk]
            probs = jnp.exp(dot(k, q, ROW_DIMS))
            slope = (probs * dot(v, g, ROW_DIMS)).astype(BF)
            grad_values[side, start : start + chunk] += dot(probs.astype(BF), g, PLAIN_DIMS)
            grad_keys[side, start : start + chunk] += dot(slope, q, PLAIN_DIMS)
            grad_query += dot(k, slope, HEAD_DIMS)
        sides.append(grad_query)
    row = lax.broadcasted_iota(jnp.int32, (128, rows), 0)
    both = jnp.where(row < HD, sides[0], sides[1]).T * HD**-0.5
    at = pl.multiple_of(pair * 128, 128)
    from_row = pl.multiple_of(step * rows, rows)
    out[pl.ds(from_row, rows), pl.ds(at, 128)] = turn(both, cos_ref[...], -sin_ref[...]).astype(BF)

    @pl.when(step == pl.num_programs(1) - 1)
    def _():
        for start in range(0, total, chunk):
            here = slice(start, start + chunk)
            low_half = lax.broadcasted_iota(jnp.int32, (chunk, 128), 1) < HD
            k = jnp.where(low_half, grad_keys[0, here], grad_keys[1, here])
            v = jnp.where(low_half, grad_values[0, here], grad_values[1, here])
            k = turn(k, cos_all[here], -sin_all[here])
            out[here, pl.ds(pl.multiple_of(width + pair * 128, 128), 128)] = k.astype(BF)
            out[here, pl.ds(pl.multiple_of(2 * width + pair * 128, 128), 128)] = v.astype(BF)


def attend_back_pairs(query, grad, exact, keys, values, cosine, sine, block, chunk):
    heads, rows, _ = query.shape
    width = heads * HD
    part = pl.BlockSpec((2, block, 128), lambda p, i: (p, i, 0))
    whole = pl.BlockSpec((2, rows, 128), lambda p, i: (p, 0, 0))
    column = pl.BlockSpec((block, 128), lambda p, i: (i, p))
    table = pl.BlockSpec((block, 128), lambda p, i: (i, 0))
    full = pl.BlockSpec((rows, 128), lambda p, i: (0, 0))
    return pl.pallas_call(
        functools.partial(attend_back_kernel, chunk=chunk),
        out_shape=jax.ShapeDtypeStruct((rows, 3 * width), BF),
        grid=(heads // 2, rows // block),
        in_specs=[part, column, column, whole, whole, table, table, full, full],
        out_specs=pl.BlockSpec((rows, 3 * width), lambda p, i: (0, 0)),
        scratch_shapes=[pltpu.VMEM((2, rows, 128), F32), pltpu.VMEM((2, rows, 128), F32)],
        cost_estimate=pl.CostEstimate(
            flops=32 * rows * rows * width, transcendentals=0, bytes_accessed=8 * rows * width
        ),
        name="attend_back",
    )(query, grad, exact, keys, values, cosine, sine, cosine, sine)


def pick(step, sources, target):
    for index, source in enumerate(sources):

        @pl.when(step == index)
        def _(source=source):
            target[...] = source[...]


def share(step, part, keep, send):
    @pl.when(step % 2 == 0)
    def _():
        keep[...] = part

    @pl.when(step % 2 == 1)
    def _():
        send[...] = part.astype(BF)


def feed_kernel(*refs, count, held):
    sources, (first, second) = refs[:count], refs[count : count + 2]
    tokens, act, slope, gelu_out, keep, send = refs[count + 2 + held :]
    step = pl.program_id(0)
    pick(step, sources, tokens)
    x = tokens[...]
    gate = dot(x, first[0], ROW_DIMS)
    upper = dot(x, first[1], ROW_DIMS)
    phi = 0.5 * (1.0 + lax.erf(gate * 2**-0.5))
    gelu = gate * phi
    low = (gelu * upper).astype(BF)
    density = jnp.exp(-0.5 * gate * gate) * 0.3989422804014327
    act[...] = low
    slope[...] = (upper * (phi + gate * density)).astype(BF)
    gelu_out[...] = gelu.astype(BF)
    share(step, dot(low, second[...], ROW_DIMS), keep, send)


def feed(tokens, first, second, total, start, held):
    count = len(tokens)
    rows = tokens[0].shape[0]
    hidden = first.shape[1]
    fixed = lambda array: pl.BlockSpec(array.shape, lambda i: (0,) * array.ndim)
    tall = pl.BlockSpec((rows, hidden), lambda i: (i + start, 0))
    wide = pl.BlockSpec((rows, D), lambda i: (i + start, 0))
    half = pl.BlockSpec((rows, D), lambda i: (i // 2, 0))
    hidden_shape = jax.ShapeDtypeStruct((total, hidden), BF)
    size = rows * count
    return pl.pallas_call(
        functools.partial(feed_kernel, count=count, held=len(held)),
        out_shape=(
            jax.ShapeDtypeStruct((total, D), BF),
            hidden_shape,
            hidden_shape,
            hidden_shape,
            jax.ShapeDtypeStruct((size // 2, D), F32),
            jax.ShapeDtypeStruct((size // 2, D), BF),
        ),
        grid=(count,),
        in_specs=[fixed(t) for t in tokens]
        + [fixed(first), fixed(second)]
        + [pl.BlockSpec(memory_space=pl.ANY)] * len(held),
        out_specs=(wide, tall, tall, tall, half, half),
        input_output_aliases={count + 2 + i: i for i in range(len(held))},
        cost_estimate=pl.CostEstimate(
            flops=6 * size * hidden * D, transcendentals=0, bytes_accessed=6 * hidden * D
        ),
        name="feed",
    )(*tokens, first, second, *held)


def feed_back_kernel(*refs, count, held):
    sources, (slope, gelu, first, second) = refs[:count], refs[count : count + 4]
    grads, out, keep, send = refs[count + 4 + held :]
    step = pl.program_id(0)
    pick(step, sources, grads)
    grad_act = dot(grads[...], second[...], PLAIN_DIMS)
    gate = (grad_act * slope[...].astype(F32)).astype(BF)
    upper = (grad_act * gelu[...].astype(F32)).astype(BF)
    out[0] = gate
    out[1] = upper
    part = dot(gate, first[0], PLAIN_DIMS) + dot(upper, first[1], PLAIN_DIMS)
    share(step, part, keep, send)


def feed_back(grads, slope, gelu, first, second, start, held):
    count = len(grads)
    rows = grads[0].shape[0]
    total, hidden = slope.shape
    fixed = lambda array: pl.BlockSpec(array.shape, lambda i: (0,) * array.ndim)
    tall = pl.BlockSpec((rows, hidden), lambda i: (i + start, 0))
    wide = pl.BlockSpec((rows, D), lambda i: (i + start, 0))
    half = pl.BlockSpec((rows, D), lambda i: (i // 2, 0))
    size = rows * count
    return pl.pallas_call(
        functools.partial(feed_back_kernel, count=count, held=len(held)),
        out_shape=(
            jax.ShapeDtypeStruct((total, D), BF),
            jax.ShapeDtypeStruct((2, total, hidden), BF),
            jax.ShapeDtypeStruct((size // 2, D), F32),
            jax.ShapeDtypeStruct((size // 2, D), BF),
        ),
        grid=(count,),
        in_specs=[fixed(t) for t in grads]
        + [tall, tall, fixed(first), fixed(second)]
        + [pl.BlockSpec(memory_space=pl.ANY)] * len(held),
        out_specs=(wide, pl.BlockSpec((2, rows, hidden), lambda i: (0, i + start, 0)), half, half),
        input_output_aliases={count + 4 + i: i for i in range(len(held))},
        cost_estimate=pl.CostEstimate(
            flops=6 * size * hidden * D, transcendentals=0, bytes_accessed=6 * hidden * D
        ),
        name="feed_back",
    )(*grads, slope, gelu, first, second, *held)


def pack_kernel(row_ref, *refs):
    half = len(refs) // 2
    for source, target in zip(refs[:half], refs[half:]):
        target[0] = source[...]


def pack(row, tall, wide):
    ins, in_specs, shapes, out_specs = [], [], [], []
    for array, is_tall in [(a, True) for a in tall] + [(a, False) for a in wide]:
        block = (128, array.shape[1]) if is_tall else (array.shape[0], 128)
        for odd in range(2):
            if is_tall:
                index = lambda j, r, odd=odd: ((2 * j + odd) ^ r[0], 0)
            else:
                index = lambda j, r, odd=odd: (0, (2 * j + odd) ^ r[0])
            ins.append(array)
            in_specs.append(pl.BlockSpec(block, index))
            shapes.append(jax.ShapeDtypeStruct((4, *block), BF))
            out_specs.append(pl.BlockSpec((1, *block), lambda j, r: (j, 0, 0)))
    return pl.pallas_call(
        pack_kernel,
        out_shape=shapes,
        grid_spec=pltpu.PrefetchScalarGridSpec(
            num_scalar_prefetch=1, grid=(4,), in_specs=in_specs, out_specs=out_specs
        ),
        name="pack",
    )(row, *ins)


def stack_kernel(source, target):
    target[0] = source[...]


def stack_wide(array):
    rows, columns = array.shape
    return pl.pallas_call(
        stack_kernel,
        out_shape=jax.ShapeDtypeStruct((columns // 128, rows, 128), array.dtype),
        grid=(columns // 128,),
        in_specs=[pl.BlockSpec((rows, 128), lambda k: (0, k))],
        out_specs=pl.BlockSpec((1, rows, 128), lambda k: (k, 0, 0)),
        name="stack",
    )(array)


def sum_rows(keep, send):
    near = keep.astype(F32) + swap(send, "row", 1).astype(F32)
    total = near[0]
    for step in range(1, 4):
        total = total + swap(near[step].astype(BF), "row", 2 * step).astype(F32)
    return total


def spread(block):
    far = swap(block, "col", 2)
    near = swap(block, "col", 1)
    return [block, near, far, swap(far, "col", 1)]


def collect(part):
    rows = part.shape[0] // 4
    far_near = swap(part[3 * rows :].astype(BF), "col", 1).astype(F32)
    far = (part[2 * rows : 3 * rows] + far_near).astype(BF)
    far = swap(far, "col", 2)
    near = swap(part[rows : 2 * rows].astype(BF), "col", 1).astype(F32)
    return part[:rows] + near + far.astype(F32)


def add_all(values):
    for axis in ("col", "row"):
        flip = 1
        while flip < lax.axis_size(axis):
            values = values + swap(values, axis, flip)
            flip *= 2
    return values


def group_shards(
    hidden_in,
    teacher,
    valid_mask,
    first_gain,
    second_gain,
    attention_in,
    attention_out,
    feed_in,
    feed_out,
):
    own = hidden_in.shape[0]
    column = lax.axis_index("col")
    row = lax.axis_index("row")
    group = own * 4
    group_start = row * group
    total_tokens = group * lax.axis_size("row")
    valid_total = jnp.sum(valid_mask.astype(F32))
    live_group = lax.dynamic_slice_in_dim(valid_mask, group_start, group, 0)
    live_own = lax.dynamic_slice_in_dim(live_group, column * own, own, 0).astype(F32)
    order = jnp.arange(4, dtype=jnp.int32) ^ column
    live = jnp.take(live_group.reshape(4, own), order, axis=0).reshape(group, 1)
    bias = jnp.where(live > 0, 0.0, MASKED).astype(F32)
    spot = (order[:, None] * own + jnp.arange(own, dtype=jnp.int32)[None, :]).reshape(group)
    half = HD // 2
    frequency = ROPE_BASE ** (-(jnp.arange(half, dtype=F32) * 2.0) / HD)
    angle = spot.astype(F32)[:, None] * jnp.tile(frequency, 4)[None, :]
    sign = jnp.where(jnp.arange(128) % HD < half, -1.0, 1.0)
    cosine = jnp.cos(angle)
    sine = jnp.sin(angle) * sign[None, :]

    inputs = hidden_in.astype(F32)
    normed_one, inverse_one, low_one = layer_norm(inputs, first_gain)
    width = attention_in.shape[1]
    joint_blocks = row_blocks(attention_in.reshape(3 * width, attention_in.shape[2]))
    tokens = spread(low_one)
    hidden = feed_in.shape[1]
    out_rows = lax.all_gather(
        jnp.concatenate([attention_out, swap(attention_out, "col", 2), feed_out], axis=1),
        "row",
        axis=0,
        tiled=True,
    )
    feed_in_rows = lax.all_gather(feed_in, "row", axis=2, tiled=True)
    index = row.reshape(1)
    all_low_one, joint, query, keys, values = project(
        index, tokens, joint_blocks, cosine, sine, bias
    )
    mixed, exact, query_back = attend_pairs(query, keys, values, 512)

    attention_rows = out_rows[:, :width]
    attention_twin = out_rows[:, width : 2 * width]
    feed_out_rows = out_rows[:, 2 * width :]
    mixed_twin = swap(mixed[2 * own :], "col", 2)
    mixed_own = mixed[: 2 * own]
    near = dot(mixed_own[own:], attention_rows, ROW_DIMS) + dot(
        mixed_twin[own:], attention_twin, ROW_DIMS
    )
    near = swap(near, "col", 1)
    branch = (
        dot(mixed_own[:own], attention_rows, ROW_DIMS)
        + dot(mixed_twin[:own], attention_twin, ROW_DIMS)
        + near
    )
    middle = inputs + branch
    normed_two, inverse_two, low_two = layer_norm(middle, second_gain)

    chunks = 2
    size = own // chunks
    parts = [slice(i * size, (i + 1) * size) for i in range(chunks)]
    far = [swap(low_two[here], "col", 2) for here in parts]
    near = []
    for here in parts:
        near += [low_two[here], swap(low_two[here], "col", 1)]
    *kept, keep_near, send_near = feed(near, feed_in_rows, feed_out_rows, group, 0, [])
    got_near = swap(send_near, "col", 1)
    sums = []
    gate_to = None
    for i in range(chunks):
        there = far[i]
        if gate_to is not None:
            there, gate_to = lax.optimization_barrier((there, gate_to))
            sums[-1] = gate_to
        there = [there, swap(there, "col", 1)]
        *kept, keep, send = feed(
            there, feed_in_rows, feed_out_rows, group, 2 * chunks + 2 * i, kept
        )
        gate_to = (keep + swap(send, "col", 1).astype(F32)).astype(BF)
        sums.append(gate_to)
    all_low_two, act, slope, gelu = kept
    squares = jnp.float32(0.0)
    results, grad_results, far, held, nears = [], [], [], [], []
    for i, here in enumerate(parts):
        result = (
            middle[here]
            + keep_near[here]
            + got_near[here].astype(F32)
            + swap(sums[i], "col", 2).astype(F32)
        )
        results.append(result)
        error_term = result - teacher[here]
        live_here = live_own[here]
        squares = squares + jnp.sum(live_here * jnp.sum(error_term * error_term, axis=1))
        grad_result = (total_tokens * live_here)[:, None] * error_term / valid_total
        grad_results.append(grad_result)
        low = grad_result.astype(BF)
        far.append(swap(low, "col", 2))
        *held, keep, send = feed_back(
            [low, swap(low, "col", 1)], slope, gelu, feed_in_rows, feed_out_rows, 2 * i, held
        )
        nears.append(keep + swap(send, "col", 1).astype(F32))
    sums = []
    gate_to = None
    for i in range(chunks):
        there = far[i]
        if gate_to is not None:
            there, gate_to = lax.optimization_barrier((there, gate_to))
            sums[-1] = gate_to
        *held, keep, send = feed_back(
            [there, swap(there, "col", 1)],
            slope,
            gelu,
            feed_in_rows,
            feed_out_rows,
            2 * chunks + 2 * i,
            held,
        )
        gate_to = (keep + swap(send, "col", 1).astype(F32)).astype(BF)
        sums.append(gate_to)
    all_grads, grad_hidden = held
    all_grads, grad_hidden, gate_to = lax.optimization_barrier((all_grads, grad_hidden, gate_to))
    sums[-1] = gate_to
    grad_out = dot(all_grads, act, HEAD_DIMS).astype(BF)
    grad_feed = stack_wide(
        jnp.einsum(
            "irf,rd->ifd", grad_hidden, all_low_two, preferred_element_type=F32
        ).astype(BF).reshape(2 * hidden, D)
    )
    grad_second = jnp.zeros((D,), F32)
    grad_middles = []
    for i, here in enumerate(parts):
        grad_low_two = nears[i] + swap(sums[i], "col", 2).astype(F32)
        grad_norm, grad_gain = norm_back(
            grad_low_two, normed_two[here], inverse_two[here], second_gain
        )
        grad_second = grad_second + grad_gain
        grad_middles.append(grad_results[i] + grad_norm)
    result = jnp.concatenate(results, axis=0)
    grad_middle = jnp.concatenate(grad_middles, axis=0)
    grad_branch = grad_middle.astype(BF)

    branch_pair = jnp.concatenate([grad_branch, swap(grad_branch, "col", 1)], axis=0)
    grad_mixed_twin = swap(dot(branch_pair, attention_twin, PLAIN_DIMS).astype(BF), "col", 2)
    grad_mixed = jnp.concatenate(
        [dot(branch_pair, attention_rows, PLAIN_DIMS).astype(BF), grad_mixed_twin], axis=0
    )
    grad_attention_far = swap(dot(branch_pair, mixed_twin, HEAD_DIMS).astype(BF), "col", 2)
    grad_attention = dot(branch_pair, mixed_own, HEAD_DIMS) + grad_attention_far.astype(F32)
    grad_joint = attend_back_pairs(
        query_back, grad_mixed, exact, keys, values, cosine, sine, 512, 512
    )
    grad_low_one = collect(dot(grad_joint, joint, PLAIN_DIMS))
    grad_joint_weight = dot(grad_joint, all_low_one, HEAD_DIMS)
    grad_first = jnp.sum(grad_joint_weight * joint.astype(F32), axis=0) / first_gain
    totals = add_all(
        jnp.concatenate(
            [grad_first.reshape(8, 128), grad_second.reshape(8, 128), jnp.full((8, 128), squares)]
        )
    )
    grad_input_norm, _ = norm_back(grad_low_one, normed_one, inverse_one, first_gain)
    grad_input = grad_middle + grad_input_norm
    attention_keep, attention_send = pack(index, [grad_attention.astype(BF)], [])
    joint_keep, joint_send = pack(index, [], [grad_joint_weight.astype(BF)])
    grads = (
        sum_rows(joint_keep, joint_send).reshape(3, width, 128),
        sum_rows(attention_keep, attention_send),
        lax.psum_scatter(grad_feed, "row", scatter_dimension=0, tiled=True)
        .astype(F32)
        .reshape(2, hidden, 128),
        lax.psum_scatter(grad_out, "row", scatter_dimension=0, tiled=True).astype(F32),
    )
    loss = totals[16, 0] / (D * valid_total)
    return (
        result.astype(BF),
        loss,
        grad_input,
        totals[:8].reshape(D),
        totals[8:16].reshape(D),
        grads[0],
        grads[1],
        grads[2],
        grads[3],
    )


def shards(hidden_in, teacher, valid_mask, first_gain, second_gain, attention_in, *rest):
    fits = (
        lax.axis_size("col") == 4
        and lax.axis_size("row") == 8
        and hidden_in.shape[0] * 4 == SEQ_LEN
        and attention_in.shape[1] % 128 == 0
    )
    body = group_shards if fits else general_shards
    return body(
        hidden_in, teacher, valid_mask, first_gain, second_gain, attention_in, *rest
    )


def solution(mesh):
    in_specs = (
        P(("row", "col"), None),
        P(("row", "col"), None),
        P(),
        P(),
        P(),
        P(None, "col", "row"),
        P("row", "col"),
        P(None, "col", "row"),
        P("row", "col"),
    )
    out_specs = (
        P(("row", "col"), None),
        P(),
        P(("row", "col"), None),
        P(),
        P(),
        P(None, "col", "row"),
        P("row", "col"),
        P(None, "col", "row"),
        P("row", "col"),
    )
    return jax.shard_map(shards, mesh=mesh, in_specs=in_specs, out_specs=out_specs, check_vma=False)
```

```python
import functools

import jax
import jax.numpy as jnp
from jax import lax
from jax.experimental import pallas as pl
from jax.experimental.pallas import tpu as pltpu
from jax.sharding import PartitionSpec as P

D = 1024
HD = 64
SEQ_LEN = 2048


EPSILON = 1e-05
ROPE_BASE = 160000.0
FLOOR_SCORE = -1e30


def layer_norm(values, gain):
    center = values - jnp.mean(values, axis=1, keepdims=True)
    inverse = lax.rsqrt(jnp.mean(center * center, axis=1, keepdims=True) + EPSILON)
    normed = center * inverse
    return (normed, inverse, (normed * gain).astype(jnp.bfloat16))


def norm_back(grad_low, normed, inverse, gain):
    scaled = grad_low * gain
    inner = jnp.mean(scaled * normed, axis=1, keepdims=True)
    centered = scaled - jnp.mean(scaled, axis=1, keepdims=True)
    return (inverse * (centered - normed * inner), jnp.sum(grad_low * normed, axis=0))


def rotary_tables(rows, width):
    half = width // 2
    frequency = ROPE_BASE ** (-(jnp.arange(half, dtype=jnp.float32) * 2.0) / width)
    place = (jnp.arange(rows, dtype=jnp.int32) % SEQ_LEN).astype(jnp.float32)
    angle = place[:, None] * frequency[None, :]
    angle = jnp.concatenate([angle, angle], axis=1)
    return (jnp.cos(angle), jnp.sin(angle))


def rotate(values, cosine, sine):
    half = values.shape[-1] // 2
    turned = jnp.concatenate([-values[..., half:], values[..., :half]], axis=-1)
    return values * cosine[:, None, :] + turned * sine[:, None, :]


def rotate_back(grads, cosine, sine):
    half = grads.shape[-1] // 2
    moved = grads * sine[:, None, :]
    turned = jnp.concatenate([moved[..., half:], -moved[..., :half]], axis=-1)
    return grads * cosine[:, None, :] + turned


def block_scores(query, keys, live, start, block):
    base = start // SEQ_LEN * SEQ_LEN
    picked = lax.dynamic_slice_in_dim(query, start, block, 0)
    window = lax.dynamic_slice_in_dim(keys, base, SEQ_LEN, 0)
    allowed = lax.dynamic_slice_in_dim(live, base, SEQ_LEN, 0)
    scores = jnp.einsum(
        "qhd,khd->hqk", picked, window, preferred_element_type=jnp.float32
    ) * query.shape[2] ** (-0.5)
    return (jnp.where(allowed[None, None, :] > 0, scores, FLOOR_SCORE), picked, window, base)


def attend(query, keys, values, live):
    rows, heads, width = query.shape
    block = min(512, SEQ_LEN)

    def one_block(index):
        start = index * block
        scores, _, _, base = block_scores(query, keys, live, start, block)
        seq_values = lax.dynamic_slice_in_dim(values, base, SEQ_LEN, 0)
        top = jnp.max(scores, axis=2, keepdims=True)
        weights = jnp.exp(scores - top)
        total = jnp.sum(weights, axis=2, keepdims=True)
        probs = (weights / total).astype(jnp.bfloat16)
        mixed = jnp.einsum("hqk,khd->qhd", probs, seq_values, preferred_element_type=jnp.float32)
        return (mixed.astype(jnp.bfloat16), (top + jnp.log(total))[:, :, 0])

    mixed, log_total = lax.map(one_block, jnp.arange(rows // block, dtype=jnp.int32))
    return (mixed.reshape(rows, heads * width), log_total)


def attend_back(query, keys, values, live, log_total, grad_mixed):
    rows, heads, width = query.shape
    block = min(512, SEQ_LEN)
    scale = width ** (-0.5)
    zeros = jnp.zeros((rows, heads, width), jnp.float32)

    def one_block(index, carry):
        grad_query, grad_keys, grad_values = carry
        start = index * block
        scores, picked, window, base = block_scores(query, keys, live, start, block)
        probs = jnp.exp(scores - log_total[index][:, :, None])
        seq_values = lax.dynamic_slice_in_dim(values, base, SEQ_LEN, 0)
        grad_block = lax.dynamic_slice_in_dim(grad_mixed, start, block, 0)
        grad_probs = jnp.einsum(
            "qhd,khd->hqk", grad_block, seq_values, preferred_element_type=jnp.float32
        )
        inner = jnp.sum(probs * grad_probs, axis=2, keepdims=True)
        grad_scores = (probs * (grad_probs - inner)).astype(jnp.bfloat16)
        part_query = (
            jnp.einsum("hqk,khd->qhd", grad_scores, window, preferred_element_type=jnp.float32)
            * scale
        )
        part_keys = (
            jnp.einsum("hqk,qhd->khd", grad_scores, picked, preferred_element_type=jnp.float32)
            * scale
        )
        part_values = jnp.einsum(
            "hqk,qhd->khd",
            probs.astype(jnp.bfloat16),
            grad_block,
            preferred_element_type=jnp.float32,
        )
        grad_query = lax.dynamic_update_slice_in_dim(grad_query, part_query, start, 0)
        grad_keys = lax.dynamic_update_slice_in_dim(
            grad_keys, lax.dynamic_slice_in_dim(grad_keys, base, SEQ_LEN, 0) + part_keys, base, 0
        )
        grad_values = lax.dynamic_update_slice_in_dim(
            grad_values,
            lax.dynamic_slice_in_dim(grad_values, base, SEQ_LEN, 0) + part_values,
            base,
            0,
        )
        return (grad_query, grad_keys, grad_values)

    return lax.fori_loop(0, rows // block, one_block, (zeros, zeros, zeros))


def general_shards(
    hidden_in,
    teacher,
    valid_mask,
    first_gain,
    second_gain,
    attention_in,
    attention_out,
    feed_in,
    feed_out,
):
    columns = lax.axis_size("col")
    own_rows = hidden_in.shape[0]
    group = own_rows * columns
    own_start = lax.axis_index("col") * own_rows
    group_start = lax.axis_index("row") * group
    total_tokens = group * lax.axis_size("row")
    live_group = lax.dynamic_slice_in_dim(valid_mask, group_start, group, 0)
    live_own = lax.dynamic_slice_in_dim(live_group, own_start, own_rows, 0).astype(jnp.float32)
    valid_total = jnp.sum(valid_mask.astype(jnp.float32))
    joint_rows, attention_rows, feed_in_rows, feed_out_rows = (
        lax.all_gather(attention_in, "row", axis=2, tiled=True),
        lax.all_gather(attention_out, "row", axis=0, tiled=True),
        lax.all_gather(feed_in, "row", axis=2, tiled=True),
        lax.all_gather(feed_out, "row", axis=0, tiled=True),
    )
    inputs = hidden_in.astype(jnp.float32)
    normed_one, inverse_one, low_one = layer_norm(inputs, first_gain)
    joint = jnp.einsum(
        "rd,icd->ric",
        lax.all_gather(low_one, "col", axis=0, tiled=True),
        joint_rows,
        preferred_element_type=jnp.float32,
    )
    local_width = joint.shape[2]
    split = (group, local_width // HD, HD)
    cosine, sine = rotary_tables(group, HD)
    query = rotate(joint[:, 0].reshape(split), cosine, sine).astype(jnp.bfloat16)
    keys = rotate(joint[:, 1].reshape(split), cosine, sine).astype(jnp.bfloat16)
    values = joint[:, 2].reshape(split).astype(jnp.bfloat16)
    mixed, log_total = attend(query, keys, values, live_group)
    part = mixed
    branch = lax.psum_scatter(
        jnp.einsum("rc,oc->ro", part, attention_rows, preferred_element_type=jnp.float32),
        "col",
        scatter_dimension=0,
        tiled=True,
    )
    middle = inputs + branch
    normed_two, inverse_two, low_two = layer_norm(middle, second_gain)
    projected = jnp.einsum(
        "rd,ifd->rif",
        lax.all_gather(low_two, "col", axis=0, tiled=True),
        feed_in_rows,
        preferred_element_type=jnp.float32,
    )
    gate = projected[:, 0]
    upper = projected[:, 1]
    activated = (jax.nn.gelu(gate, approximate=False) * upper).astype(jnp.bfloat16)
    part = activated
    feed_branch = lax.psum_scatter(
        jnp.einsum("rf,of->ro", part, feed_out_rows, preferred_element_type=jnp.float32),
        "col",
        scatter_dimension=0,
        tiled=True,
    )
    result = middle + feed_branch
    error_term = result - teacher
    squares = jnp.sum(live_own * jnp.sum(error_term * error_term, axis=1))
    grad_result = (total_tokens * live_own)[:, None] * error_term / valid_total
    grad_low = grad_result.astype(jnp.bfloat16)
    piece = lax.all_gather(grad_low, "col", axis=0, tiled=True)
    part = activated
    grad_out = jnp.einsum("ro,rf->of", piece, part, preferred_element_type=jnp.float32)
    rows_grad = jnp.einsum("ro,of->rf", piece, feed_out_rows, preferred_element_type=jnp.float32)
    grad_act = rows_grad

    def geglu(first, second):
        return jax.nn.gelu(first, approximate=False) * second

    _, pull = jax.vjp(geglu, gate, upper)
    grad_gate, grad_upper = pull(grad_act)
    grad_projected = jnp.stack([grad_gate, grad_upper], axis=1).astype(jnp.bfloat16)
    part = grad_projected
    grad_low_two = lax.psum_scatter(
        jnp.einsum("rif,ifd->rd", part, feed_in_rows, preferred_element_type=jnp.float32),
        "col",
        scatter_dimension=0,
        tiled=True,
    )
    grad_middle_norm, grad_second = norm_back(grad_low_two, normed_two, inverse_two, second_gain)
    grad_middle = grad_result + grad_middle_norm
    grad_branch = grad_middle.astype(jnp.bfloat16)
    piece = lax.all_gather(grad_branch, "col", axis=0, tiled=True)
    part = mixed
    grad_weight = jnp.einsum("ro,rc->oc", piece, part, preferred_element_type=jnp.float32)
    rows_grad = jnp.einsum("ro,oc->rc", piece, attention_rows, preferred_element_type=jnp.float32)
    grad_heads = rows_grad
    grad_attention_rows, grad_heads = (grad_weight, grad_heads)
    grad_mixed = grad_heads.astype(jnp.bfloat16)
    grad_query, grad_keys, grad_values = attend_back(
        query, keys, values, live_group, log_total, grad_mixed.reshape(split)
    )
    grad_joint = jnp.stack(
        [rotate_back(grad_query, cosine, sine), rotate_back(grad_keys, cosine, sine), grad_values],
        axis=1,
    )
    grad_joint = grad_joint.astype(jnp.bfloat16).reshape(group, 3, local_width)
    part = grad_joint
    grad_low_one = lax.psum_scatter(
        jnp.einsum("ric,icd->rd", part, joint_rows, preferred_element_type=jnp.float32).astype(
            jnp.bfloat16
        ),
        "col",
        scatter_dimension=0,
        tiled=True,
    ).astype(jnp.float32)
    grad_input_norm, grad_first = norm_back(grad_low_one, normed_one, inverse_one, first_gain)
    grad_input = grad_middle + grad_input_norm
    grad_joint_weight = jnp.einsum(
        "ric,rd->icd",
        grad_joint,
        lax.all_gather(low_one, "col", axis=0, tiled=True),
        preferred_element_type=jnp.float32,
    )
    grad_feed_weight = jnp.einsum(
        "rif,rd->ifd",
        grad_projected,
        lax.all_gather(low_two, "col", axis=0, tiled=True),
        preferred_element_type=jnp.float32,
    )
    grads = (
        lax.psum_scatter(
            grad_joint_weight.astype(jnp.bfloat16), "row", scatter_dimension=2, tiled=True
        ).astype(jnp.float32),
        lax.psum_scatter(
            grad_attention_rows.astype(jnp.bfloat16), "row", scatter_dimension=0, tiled=True
        ).astype(jnp.float32),
        lax.psum_scatter(
            grad_feed_weight.astype(jnp.bfloat16), "row", scatter_dimension=2, tiled=True
        ).astype(jnp.float32),
        lax.psum_scatter(
            grad_out.astype(jnp.bfloat16), "row", scatter_dimension=0, tiled=True
        ).astype(jnp.float32),
    )
    totals = lax.psum((grad_first, grad_second, squares), ("row", "col"))
    loss = totals[2] / (D * valid_total)
    return (
        result.astype(jnp.bfloat16),
        loss,
        grad_input,
        totals[0],
        totals[1],
        grads[0],
        grads[1],
        grads[2],
        grads[3],
    )


BF = jnp.bfloat16
F32 = jnp.float32
MASKED = -1e30
ROW_DIMS = (((1,), (1,)), ((), ()))
HEAD_DIMS = (((0,), (0,)), ((), ()))
PLAIN_DIMS = (((1,), (0,)), ((), ()))


def swap(values, axis, flip):
    size = lax.axis_size(axis)
    return lax.ppermute(values, axis, [(place, place ^ flip) for place in range(size)])


def row_blocks(block):
    parts = [block] + [swap(block, "row", 2 * step) for step in range(1, 4)]
    blocks = []
    for part in parts:
        blocks += [part, swap(part, "row", 1)]
    return blocks, parts


def dot(left, right, dims):
    return lax.dot_general(left, right, dims, preferred_element_type=F32)


def turn(values, cosine, sine):
    lane = lax.broadcasted_iota(jnp.int32, values.shape, 1)
    swapped = jnp.where(
        lane % HD < HD // 2, pltpu.roll(values, 2 * HD - HD // 2, 1), pltpu.roll(values, HD // 2, 1)
    )
    return values * cosine + swapped * sine


def tables(inner, outer, start):
    cos_in, sin_in = inner[0], inner[1]
    cos_out = outer[0, pl.ds(start, 1)]
    sin_out = outer[1, pl.ds(start, 1)]
    lane = lax.broadcasted_iota(jnp.int32, cos_in.shape, 1)
    sign = jnp.where(lane % HD < HD // 2, -1.0, 1.0)
    cosine = cos_in * cos_out - sin_in * sin_out
    return cosine, (sin_in * cos_out + cos_in * sin_out) * sign


def project_kernel(row_ref, x0, x1, x2, x3, *rest):
    weights = rest[:8]
    inner, outer, bias_ref, tokens, joint, query, keys, values = rest[8:]
    step = pl.program_id(0)
    row = row_ref[0]
    pairs = joint.shape[0] // 384

    @pl.when(step == 0)
    def _():
        for index, weight in enumerate(weights):
            start = pl.multiple_of((row ^ index) * 128, 128)
            for pair in range(pairs):
                for kind in range(3):
                    at = (3 * pair + kind) * 128
                    old = (kind * pairs + pair) * 128
                    joint[at : at + 128, pl.ds(start, 128)] = weight[old : old + 128]

    for index, source in enumerate((x0, x1, x2, x3)):

        @pl.when(step == index)
        def _(source=source):
            tokens[...] = source[...]

    result = dot(tokens[...], joint[...], ROW_DIMS)
    cosine, sine = tables(inner, outer, step)
    rows = result.shape[0]
    lane = lax.broadcasted_iota(jnp.int32, (rows, 128), 1)
    spare = lane % HD
    one = jnp.ones((rows, 128), F32)
    zero = jnp.zeros((rows, 128), F32)
    key_spare = jnp.where(spare == 0, bias_ref[...] * one, jnp.where(spare <= 3, one, zero))
    query_spare = jnp.where(spare == 0, one, zero)
    for pair in range(pairs):
        at = pair * 384
        q = turn(result[:, at : at + 128], cosine, sine) * HD**-0.5
        k = turn(result[:, at + 128 : at + 256], cosine, sine)
        v = result[:, at + 256 : at + 384]
        for side in range(2):
            mine = (lane < HD) if side == 0 else (lane >= HD)
            query[2 * pair + side] = jnp.where(mine, q, query_spare).astype(BF)
            keys[2 * pair + side] = jnp.where(mine, k, key_spare).astype(BF)
            values[2 * pair + side] = jnp.where(mine, v, one).astype(BF)


def project(row, tokens, weights, inner, outer, bias):
    rows = tokens[0].shape[0]
    total = rows * len(tokens)
    width = weights[0].shape[0]
    heads = width // 3 // HD
    whole = lambda array: pl.BlockSpec(array.shape, lambda i, r: (0,) * array.ndim)
    wide = pl.BlockSpec((heads, rows, 128), lambda i, r: (0, i, 0))
    joint_shape = jax.ShapeDtypeStruct((width, D), BF)
    head_shape = jax.ShapeDtypeStruct((heads, total, 128), BF)
    return pl.pallas_call(
        project_kernel,
        out_shape=(
            jax.ShapeDtypeStruct((total, D), BF),
            joint_shape,
            head_shape,
            head_shape,
            head_shape,
        ),
        grid_spec=pltpu.PrefetchScalarGridSpec(
            num_scalar_prefetch=1,
            grid=(len(tokens),),
            in_specs=[whole(t) for t in tokens]
            + [whole(w) for w in weights]
            + [whole(inner), whole(outer), pl.BlockSpec((rows, 1), lambda i, r: (i, 0))],
            out_specs=(
                pl.BlockSpec((rows, D), lambda i, r: (i, 0)),
                pl.BlockSpec((width, D), lambda i, r: (0, 0)),
                wide,
                wide,
                wide,
            ),
        ),
        cost_estimate=pl.CostEstimate(
            flops=2 * total * width * D, transcendentals=0, bytes_accessed=8 * total * D
        ),
        name="project",
    )(row, *tokens, *weights, inner, outer, bias)


def split_three(column):
    high = column.astype(BF).astype(F32)
    rest = column - high
    middle = rest.astype(BF).astype(F32)
    return high, middle, rest - middle


def attend_kernel(query, keys, values, mixed, exact, query_back):
    rows = mixed.shape[0]
    lane = lax.broadcasted_iota(jnp.int32, (rows, 128), 1)
    spare = lane % HD
    outs = []
    for side in range(2):
        q = query[side]
        scores = dot(q, keys[side], ROW_DIMS)
        top = jnp.max(scores, axis=1, keepdims=True)
        weights = jnp.exp(scores - top).astype(BF)
        out = dot(weights, values[side], PLAIN_DIMS)
        at = HD if side == 0 else 0
        total = out[:, at : at + 1]
        outs.append(out / total)
        high, middle, low = split_three(top + jnp.log(total))
        mine = (lane < HD) if side == 0 else (lane >= HD)
        extra = jnp.where(spare == 1, -high, jnp.where(spare == 2, -middle, -low))
        keep = jnp.logical_or(mine, jnp.logical_or(spare == 0, spare > 3))
        query_back[side] = jnp.where(keep, q.astype(F32), extra).astype(BF)
    both = jnp.where(lane < HD, outs[0], outs[1])
    exact[...] = both
    mixed[...] = both.astype(BF)


def attend_pair(pair, query, keys, values, block):
    _, rows, _ = query.shape
    part = pl.BlockSpec((2, block, 128), lambda i: (pair, i, 0))
    whole = pl.BlockSpec((2, rows, 128), lambda i: (pair, 0, 0))
    out = pl.BlockSpec((block, 128), lambda i: (i, 0))
    return pl.pallas_call(
        attend_kernel,
        out_shape=(
            jax.ShapeDtypeStruct((rows, 128), BF),
            jax.ShapeDtypeStruct((rows, 128), F32),
            jax.ShapeDtypeStruct((2, rows, 128), BF),
        ),
        grid=(rows // block,),
        in_specs=[part, whole, whole],
        out_specs=(out, out, pl.BlockSpec((2, block, 128), lambda i: (0, i, 0))),
        cost_estimate=pl.CostEstimate(
            flops=16 * rows * rows * 128, transcendentals=0, bytes_accessed=8 * rows * 128
        ),
        name="attend",
    )(query, keys, values)


def attend_back_kernel(query, grad, exact, keys, values, inner, outer, *refs):
    out, grad_keys, grad_values = refs[-3:]
    step = pl.program_id(0)
    rows = grad.shape[0]
    total = keys.shape[1]
    lane = lax.broadcasted_iota(jnp.int32, (rows, 128), 1)
    spare = lane % HD

    @pl.when(step == 0)
    def _():
        grad_keys[...] = jnp.zeros_like(grad_keys)
        grad_values[...] = jnp.zeros_like(grad_values)

    product = grad[...].astype(F32) * exact[...]
    sides = []
    for side in range(2):
        q = query[side]
        mine = (lane < HD) if side == 0 else (lane >= HD)
        total_grad = jnp.sum(jnp.where(mine, product, 0.0), axis=1, keepdims=True)
        high, middle, low = split_three(total_grad)
        extra = jnp.where(
            spare == 0, -high, jnp.where(spare == 1, -middle, jnp.where(spare == 2, -low, 0.0))
        )
        g = jnp.where(mine, grad[...].astype(F32), extra).astype(BF)
        grad_query = jnp.zeros((128, rows), F32)
        for start in range(0, total, rows):
            k = keys[side, start : start + rows]
            v = values[side, start : start + rows]
            probs = jnp.exp(dot(k, q, ROW_DIMS))
            slope = (probs * dot(v, g, ROW_DIMS)).astype(BF)
            grad_values[side, start : start + rows] += dot(probs.astype(BF), g, PLAIN_DIMS)
            grad_keys[side, start : start + rows] += dot(slope, q, PLAIN_DIMS)
            grad_query += dot(k, slope, HEAD_DIMS)
        sides.append(grad_query)
    row = lax.broadcasted_iota(jnp.int32, (128, rows), 0)
    both = jnp.where(row < HD, sides[0], sides[1]).T * HD**-0.5
    cosine, sine = tables(inner, outer, step)
    from_row = pl.multiple_of(step * rows, rows)
    out[pl.ds(from_row, rows), :128] = turn(both, cosine, -sine).astype(BF)

    @pl.when(step == pl.num_programs(0) - 1)
    def _():
        for block in range(total // rows):
            here = slice(block * rows, (block + 1) * rows)
            k = jnp.where(lane < HD, grad_keys[0, here], grad_keys[1, here])
            v = jnp.where(lane < HD, grad_values[0, here], grad_values[1, here])
            cosine, sine = tables(inner, outer, block)
            out[here, 128:256] = turn(k, cosine, -sine).astype(BF)
            out[here, 256:] = v.astype(BF)


def attend_back_pair(pair, query, grad, exact, keys, values, inner, outer, held):
    heads, rows, _ = keys.shape
    block = inner.shape[1]
    part = pl.BlockSpec((2, block, 128), lambda i: (0, i, 0))
    whole = pl.BlockSpec((2, rows, 128), lambda i: (pair, 0, 0))
    fixed = lambda array: pl.BlockSpec(array.shape, lambda i: (0,) * array.ndim)
    return pl.pallas_call(
        attend_back_kernel,
        out_shape=jax.ShapeDtypeStruct((rows, 3 * heads * HD), BF),
        grid=(rows // block,),
        in_specs=[
            part,
            pl.BlockSpec((block, 128), lambda i: (i, pair)),
            pl.BlockSpec((block, 128), lambda i: (i, 0)),
            whole,
            whole,
            fixed(inner),
            fixed(outer),
        ]
        + [pl.BlockSpec(memory_space=pl.ANY)] * len(held),
        out_specs=pl.BlockSpec((rows, 3 * 128), lambda i: (0, pair)),
        scratch_shapes=[pltpu.VMEM((2, rows, 128), F32), pltpu.VMEM((2, rows, 128), F32)],
        input_output_aliases={7 + i: i for i in range(len(held))},
        cost_estimate=pl.CostEstimate(
            flops=48 * rows * rows * HD, transcendentals=0, bytes_accessed=8 * rows * HD
        ),
        name="attend_back",
    )(query, grad, exact, keys, values, inner, outer, *held)


def pick(step, sources, target):
    for index, source in enumerate(sources):

        @pl.when(step == index)
        def _(source=source):
            target[...] = source[...]


def share(step, part, keep, send):
    @pl.when(step % 2 == 0)
    def _():
        keep[...] = part

    @pl.when(step % 2 == 1)
    def _():
        send[...] = part.astype(BF)


def feed_kernel(row_ref, *refs, count, blocks, held):
    sources, second = refs[:count], refs[count]
    firsts = refs[count + 1 : count + 1 + blocks]
    tokens, act, slope, gelu_out, keep, send = refs[count + 1 + blocks + held :][:6]
    step = pl.program_id(0)
    first = firsts[0] if blocks == 1 else refs[-1]
    if blocks > 1:

        @pl.when(step == 0)
        def _():
            for index, block in enumerate(firsts):
                start = pl.multiple_of((row_ref[0] ^ index) * 128, 128)
                first[:, pl.ds(start, 128)] = block[...]

    hidden = first.shape[0] // 2
    pick(step, sources, tokens)
    x = tokens[...]
    gate = dot(x, first[:hidden], ROW_DIMS)
    upper = dot(x, first[hidden:], ROW_DIMS)
    phi = 0.5 * (1.0 + lax.erf(gate * 2**-0.5))
    gelu = gate * phi
    low = (gelu * upper).astype(BF)
    density = jnp.exp(-0.5 * gate * gate) * 0.3989422804014327
    act[...] = low
    slope[...] = (upper * (phi + gate * density)).astype(BF)
    gelu_out[...] = gelu.astype(BF)
    share(step, dot(low, second[...], ROW_DIMS), keep, send)


def feed(row, tokens, firsts, second, total, start, held):
    count = len(tokens)
    blocks = len(firsts)
    rows = tokens[0].shape[0]
    hidden = second.shape[1]
    fixed = lambda array: pl.BlockSpec(array.shape, lambda i, r: (0,) * array.ndim)
    tall = pl.BlockSpec((rows, hidden), lambda i, r: (i + start, 0))
    wide = pl.BlockSpec((rows, D), lambda i, r: (i + start, 0))
    half = pl.BlockSpec((rows, D), lambda i, r: (i // 2, 0))
    hidden_shape = jax.ShapeDtypeStruct((total, hidden), BF)
    size = rows * count
    first_shape = [jax.ShapeDtypeStruct((2 * hidden, D), BF)] * (blocks > 1)
    return pl.pallas_call(
        functools.partial(feed_kernel, count=count, blocks=blocks, held=len(held)),
        out_shape=(
            jax.ShapeDtypeStruct((total, D), BF),
            hidden_shape,
            hidden_shape,
            hidden_shape,
            jax.ShapeDtypeStruct((size // 2, D), F32),
            jax.ShapeDtypeStruct((size // 2, D), BF),
            *first_shape,
        ),
        grid_spec=pltpu.PrefetchScalarGridSpec(
            num_scalar_prefetch=1,
            grid=(count,),
            in_specs=[fixed(t) for t in tokens]
            + [fixed(second)]
            + [fixed(f) for f in firsts]
            + [pl.BlockSpec(memory_space=pl.ANY)] * len(held),
            out_specs=(wide, tall, tall, tall, half, half, *map(fixed, first_shape)),
        ),
        input_output_aliases={count + 2 + blocks + i: i for i in range(len(held))},
        cost_estimate=pl.CostEstimate(
            flops=6 * size * hidden * D, transcendentals=0, bytes_accessed=6 * hidden * D
        ),
        name="feed",
    )(row, *tokens, second, *firsts, *held)


def feed_back_kernel(*refs, count, held):
    sources, (slope, gelu, first, second) = refs[:count], refs[count : count + 4]
    grads, out, keep, send = refs[count + 4 + held :]
    step = pl.program_id(0)
    pick(step, sources, grads)
    grad_act = dot(grads[...], second[...], PLAIN_DIMS)
    gate = (grad_act * slope[...].astype(F32)).astype(BF)
    upper = (grad_act * gelu[...].astype(F32)).astype(BF)
    out[0] = gate
    out[1] = upper
    hidden = first.shape[0] // 2
    part = dot(gate, first[:hidden], PLAIN_DIMS) + dot(upper, first[hidden:], PLAIN_DIMS)
    share(step, part, keep, send)


def feed_back(grads, slope, gelu, first, second, start, held):
    count = len(grads)
    rows = grads[0].shape[0]
    total, hidden = slope.shape
    fixed = lambda array: pl.BlockSpec(array.shape, lambda i: (0,) * array.ndim)
    tall = pl.BlockSpec((rows, hidden), lambda i: (i + start, 0))
    wide = pl.BlockSpec((rows, D), lambda i: (i + start, 0))
    half = pl.BlockSpec((rows, D), lambda i: (i // 2, 0))
    size = rows * count
    return pl.pallas_call(
        functools.partial(feed_back_kernel, count=count, held=len(held)),
        out_shape=(
            jax.ShapeDtypeStruct((total, D), BF),
            jax.ShapeDtypeStruct((2, total, hidden), BF),
            jax.ShapeDtypeStruct((size // 2, D), F32),
            jax.ShapeDtypeStruct((size // 2, D), BF),
        ),
        grid=(count,),
        in_specs=[fixed(t) for t in grads]
        + [tall, tall, fixed(first), fixed(second)]
        + [pl.BlockSpec(memory_space=pl.ANY)] * len(held),
        out_specs=(wide, pl.BlockSpec((2, rows, hidden), lambda i: (0, i + start, 0)), half, half),
        input_output_aliases={count + 4 + i: i for i in range(len(held))},
        cost_estimate=pl.CostEstimate(
            flops=6 * size * hidden * D, transcendentals=0, bytes_accessed=6 * hidden * D
        ),
        name="feed_back",
    )(*grads, slope, gelu, first, second, *held)


def pack_kernel(row_ref, *refs):
    half = len(refs) // 2
    for source, target in zip(refs[:half], refs[half:]):
        target[0] = source[...]


def pack(row, tall, wide):
    ins, in_specs, shapes, out_specs = [], [], [], []
    for array, is_tall in [(a, True) for a in tall] + [(a, False) for a in wide]:
        block = (128, array.shape[1]) if is_tall else (array.shape[0], 128)
        for odd in range(2):
            if is_tall:
                index = lambda j, r, odd=odd: ((2 * j + odd) ^ r[0], 0)
            else:
                index = lambda j, r, odd=odd: (0, (2 * j + odd) ^ r[0])
            ins.append(array)
            in_specs.append(pl.BlockSpec(block, index))
            shapes.append(jax.ShapeDtypeStruct((4, *block), BF))
            out_specs.append(pl.BlockSpec((1, *block), lambda j, r: (j, 0, 0)))
    return pl.pallas_call(
        pack_kernel,
        out_shape=shapes,
        grid_spec=pltpu.PrefetchScalarGridSpec(
            num_scalar_prefetch=1, grid=(4,), in_specs=in_specs, out_specs=out_specs
        ),
        name="pack",
    )(row, *ins)


def stack_kernel(source, target):
    target[0] = source[...]


def stack_wide(array):
    rows, columns = array.shape
    return pl.pallas_call(
        stack_kernel,
        out_shape=jax.ShapeDtypeStruct((columns // 128, rows, 128), array.dtype),
        grid=(columns // 128,),
        in_specs=[pl.BlockSpec((rows, 128), lambda k: (0, k))],
        out_specs=pl.BlockSpec((1, rows, 128), lambda k: (k, 0, 0)),
        name="stack",
    )(array)


def sum_far(near):
    total = near[0]
    for step in range(1, 4):
        total = total + swap(near[step].astype(BF), "row", 2 * step).astype(F32)
    return total


def add_all(values):
    for axis in ("col", "row"):
        flip = 1
        while flip < lax.axis_size(axis):
            values = values + swap(values, axis, flip)
            flip *= 2
    return values


def group_shards(
    hidden_in,
    teacher,
    valid_mask,
    first_gain,
    second_gain,
    attention_in,
    attention_out,
    feed_in,
    feed_out,
):
    own = hidden_in.shape[0]
    column = lax.axis_index("col")
    row = lax.axis_index("row")
    group = own * 4
    group_start = row * group
    total_tokens = group * lax.axis_size("row")
    valid_total = jnp.sum(valid_mask.astype(F32))
    live_group = lax.dynamic_slice_in_dim(valid_mask, group_start, group, 0)
    live_own = lax.dynamic_slice_in_dim(live_group, column * own, own, 0).astype(F32)
    order = jnp.arange(4, dtype=jnp.int32) ^ column
    live = jnp.take(live_group.reshape(4, own), order, axis=0).reshape(group, 1)
    bias = jnp.where(live > 0, 0.0, MASKED).astype(F32)
    half = HD // 2
    frequency = ROPE_BASE ** (-(jnp.arange(half, dtype=F32) * 2.0) / HD)
    frequency = jnp.tile(frequency, 4)[None, :]
    inner = jnp.arange(own, dtype=F32)[:, None] * frequency
    inner = jnp.stack([jnp.cos(inner), jnp.sin(inner)])
    outer = (order * own).astype(F32)[:, None] * frequency
    outer = jnp.stack([jnp.cos(outer), jnp.sin(outer)])

    inputs = hidden_in.astype(F32)
    normed_one, inverse_one, low_one = layer_norm(inputs, first_gain)
    width = attention_in.shape[1]
    joint_blocks, joint_parts = row_blocks(attention_in.reshape(3 * width, attention_in.shape[2]))
    far = swap(low_one, "col", 2)
    near = swap(low_one, "col", 1)
    out_twin = swap(attention_out, "col", 2)
    hidden = feed_in.shape[1]
    index = row.reshape(1)
    feed_in, feed_out, attention_out, out_twin, *_ = lax.optimization_barrier(
        (feed_in, feed_out, attention_out, out_twin, *joint_parts)
    )
    tokens = [low_one, near, far, swap(far, "col", 1)]
    out_rows = lax.all_gather(
        jnp.concatenate([attention_out, out_twin, feed_out], axis=1), "row", axis=0, tiled=True
    )
    feed_in_blocks, _ = row_blocks(feed_in.reshape(2 * hidden, 128))
    all_low_one, joint, query, keys, values = project(
        index, tokens, joint_blocks, inner, outer, bias
    )
    mixed, exact, query_back, mixed_twin = [], [], [], []
    for pair in range(width // 128):
        pair_mixed, pair_exact, pair_query = attend_pair(pair, query, keys, values, 512)
        mixed.append(pair_mixed)
        exact.append(pair_exact)
        query_back.append(pair_query)
        mixed_twin.append(swap(pair_mixed[2 * own :], "col", 2))
    mixed = jnp.concatenate([m[: 2 * own] for m in mixed], axis=1)
    mixed_twin = jnp.concatenate(mixed_twin, axis=1)
    attention_rows = out_rows[:, :width]
    attention_twin = out_rows[:, width : 2 * width]
    feed_out_rows = out_rows[:, 2 * width :]
    mixed_own = mixed[: 2 * own]
    near = dot(mixed_own[own:], attention_rows, ROW_DIMS) + dot(
        mixed_twin[own:], attention_twin, ROW_DIMS
    )
    near = swap(near, "col", 1)
    branch = (
        dot(mixed_own[:own], attention_rows, ROW_DIMS)
        + dot(mixed_twin[:own], attention_twin, ROW_DIMS)
        + near
    )
    middle = inputs + branch
    normed_two, inverse_two, low_two = layer_norm(middle, second_gain)

    chunks = 2
    size = own // chunks
    parts = [slice(i * size, (i + 1) * size) for i in range(chunks)]
    far = [swap(low_two[here], "col", 2) for here in parts]
    near = []
    for here in parts:
        near += [low_two[here], swap(low_two[here], "col", 1)]
    *kept, keep_near, send_near, feed_in_rows = feed(
        index, near, feed_in_blocks, feed_out_rows, group, 0, []
    )
    far[0], kept[0] = lax.optimization_barrier((far[0], kept[0]))
    got_near = swap(send_near, "col", 1)
    sums = []
    gate_to = None
    for i in range(chunks):
        there = far[i]
        if gate_to is not None:
            there, gate_to = lax.optimization_barrier((there, gate_to))
            sums[-1] = gate_to
        there = [there, swap(there, "col", 1)]
        *kept, keep, send = feed(
            index, there, [feed_in_rows], feed_out_rows, group, 2 * chunks + 2 * i, kept
        )
        gate_to = (keep + swap(send, "col", 1).astype(F32)).astype(BF)
        sums.append(gate_to)
    all_low_two, act, slope, gelu = kept
    squares = jnp.float32(0.0)
    results, grad_results, far, held, nears = [], [], [], [], []
    for i, here in enumerate(parts):
        got_far = swap(sums[i], "col", 2)
        if held:
            got_far, held[0] = lax.optimization_barrier((got_far, held[0]))
        result = (
            middle[here]
            + keep_near[here]
            + got_near[here].astype(F32)
            + got_far.astype(F32)
        )
        results.append(result)
        error_term = result - teacher[here]
        live_here = live_own[here]
        squares = squares + jnp.sum(live_here * jnp.sum(error_term * error_term, axis=1))
        grad_result = (total_tokens * live_here)[:, None] * error_term / valid_total
        grad_results.append(grad_result)
        low = grad_result.astype(BF)
        far.append(swap(low, "col", 2))
        low = [low, swap(low, "col", 1)]
        *held, keep, send = feed_back(low, slope, gelu, feed_in_rows, feed_out_rows, 2 * i, held)
        nears.append(keep + swap(send, "col", 1).astype(F32))
    sums = []
    gate_to = None
    for i in range(chunks):
        there = far[i]
        if gate_to is not None:
            there, gate_to = lax.optimization_barrier((there, gate_to))
            sums[-1] = gate_to
        there = [there, swap(there, "col", 1)]
        *held, keep, send = feed_back(
            there,
            slope,
            gelu,
            feed_in_rows,
            feed_out_rows,
            2 * chunks + 2 * i,
            held,
        )
        gate_to = (keep + swap(send, "col", 1).astype(F32)).astype(BF)
        sums.append(gate_to)
    all_grads, grad_hidden = held
    all_grads, grad_hidden, gate_to = lax.optimization_barrier((all_grads, grad_hidden, gate_to))
    sums[-1] = gate_to
    grad_out = dot(all_grads, act, HEAD_DIMS).astype(BF)
    grad_feed = stack_wide(
        jnp.einsum(
            "irf,rd->ifd", grad_hidden, all_low_two, preferred_element_type=F32
        ).astype(BF).reshape(2 * hidden, D)
    )
    grad_second = jnp.zeros((D,), F32)
    grad_middles = []
    for i, here in enumerate(parts):
        got_far = swap(sums[i], "col", 2)
        if i == chunks - 1:
            got_far, grad_feed, grad_out = lax.optimization_barrier((got_far, grad_feed, grad_out))
        grad_low_two = nears[i] + got_far.astype(F32)
        grad_norm, grad_gain = norm_back(
            grad_low_two, normed_two[here], inverse_two[here], second_gain
        )
        grad_second = grad_second + grad_gain
        grad_middles.append(grad_results[i] + grad_norm)
    result = jnp.concatenate(results, axis=0)
    grad_middle = jnp.concatenate(grad_middles, axis=0)
    grad_branch = grad_middle.astype(BF)

    branch_pair = jnp.concatenate([grad_branch, swap(grad_branch, "col", 1)], axis=0)
    grad_mixed_twin = swap(dot(branch_pair, attention_twin, PLAIN_DIMS).astype(BF), "col", 2)
    grad_mixed = jnp.concatenate(
        [dot(branch_pair, attention_rows, PLAIN_DIMS).astype(BF), grad_mixed_twin], axis=0
    )
    grad_attention_far = swap(dot(branch_pair, mixed_twin, HEAD_DIMS).astype(BF), "col", 2)
    grad_attention = dot(branch_pair, mixed_own, HEAD_DIMS) + grad_attention_far.astype(F32)
    attention_keep, attention_send = pack(index, [grad_attention.astype(BF)], [])
    near_attention = attention_keep.astype(F32) + swap(attention_send, "row", 1).astype(F32)
    held, joint_near = [], []
    grad_first = jnp.zeros((D,), F32)
    for pair in range(width // 128):
        grad_joint = attend_back_pair(
            pair,
            query_back[pair],
            grad_mixed,
            exact[pair],
            keys,
            values,
            inner,
            outer,
            held,
        )
        held = [grad_joint]
        here = slice(pair * 384, (pair + 1) * 384)
        grad_pair = grad_joint[:, here]
        if pair == width // 128 - 1:
            part = dot(grad_joint[2 * own :], joint, PLAIN_DIMS)
            far = part[:own] + swap(part[own:].astype(BF), "col", 1).astype(F32)
            grad_pair, far = lax.optimization_barrier((grad_pair, far.astype(BF)))
        weight = dot(grad_pair, all_low_one, HEAD_DIMS)
        grad_first = grad_first + jnp.sum(weight * joint[here].astype(F32), axis=0)
        keep, send = pack(index, [], [weight.astype(BF)])
        near_sum = keep.astype(F32) + swap(send, "row", 1).astype(F32)
        if pair == 0:
            held, send = lax.optimization_barrier((held, send))
        joint_near.append(near_sum)
    part = dot(grad_joint[: 2 * own], joint, PLAIN_DIMS)
    near = part[:own] + swap(part[own:].astype(BF), "col", 1).astype(F32)
    grad_low_one = near + swap(far, "col", 2).astype(F32)
    grad_first = grad_first / first_gain
    totals = add_all(
        jnp.concatenate(
            [grad_first.reshape(8, 128), grad_second.reshape(8, 128), jnp.full((8, 128), squares)]
        )
    )
    grad_input_norm, _ = norm_back(grad_low_one, normed_one, inverse_one, first_gain)
    grad_input = grad_middle + grad_input_norm
    joint_sums = [sum_far(near).reshape(3, 128, 128) for near in joint_near]
    grads = (
        jnp.concatenate(joint_sums, axis=1),
        sum_far(near_attention),
        lax.psum_scatter(grad_feed, "row", scatter_dimension=0, tiled=True)
        .astype(F32)
        .reshape(2, hidden, 128),
        lax.psum_scatter(grad_out, "row", scatter_dimension=0, tiled=True).astype(F32),
    )
    loss = totals[16, 0] / (D * valid_total)
    return (
        result.astype(BF),
        loss,
        grad_input,
        totals[:8].reshape(D),
        totals[8:16].reshape(D),
        grads[0],
        grads[1],
        grads[2],
        grads[3],
    )


def shards(hidden_in, teacher, valid_mask, first_gain, second_gain, attention_in, *rest):
    fits = (
        lax.axis_size("col") == 4
        and lax.axis_size("row") == 8
        and hidden_in.shape[0] * 4 == SEQ_LEN
        and attention_in.shape[1] % 128 == 0
    )
    body = group_shards if fits else general_shards
    return body(
        hidden_in, teacher, valid_mask, first_gain, second_gain, attention_in, *rest
    )


def solution(mesh):
    in_specs = (
        P(("row", "col"), None),
        P(("row", "col"), None),
        P(),
        P(),
        P(),
        P(None, "col", "row"),
        P("row", "col"),
        P(None, "col", "row"),
        P("row", "col"),
    )
    out_specs = (
        P(("row", "col"), None),
        P(),
        P(("row", "col"), None),
        P(),
        P(),
        P(None, "col", "row"),
        P("row", "col"),
        P(None, "col", "row"),
        P("row", "col"),
    )
    return jax.shard_map(
        shards, mesh=mesh, in_specs=in_specs, out_specs=out_specs, check_vma=False
    )
```

```python
import functools

import jax
import jax.numpy as jnp
from jax import lax
from jax.experimental import pallas as pl
from jax.experimental.pallas import tpu as pltpu
from jax.sharding import PartitionSpec as P

D = 1024
HD = 64
SEQ_LEN = 2048


EPSILON = 1e-05
ROPE_BASE = 160000.0
FLOOR_SCORE = -1e30


def layer_norm(values, gain):
    center = values - jnp.mean(values, axis=1, keepdims=True)
    inverse = lax.rsqrt(jnp.mean(center * center, axis=1, keepdims=True) + EPSILON)
    normed = center * inverse
    return (normed, inverse, (normed * gain).astype(jnp.bfloat16))


def norm_back(grad_low, normed, inverse, gain):
    scaled = grad_low * gain
    inner = jnp.mean(scaled * normed, axis=1, keepdims=True)
    centered = scaled - jnp.mean(scaled, axis=1, keepdims=True)
    return (inverse * (centered - normed * inner), jnp.sum(grad_low * normed, axis=0))


def rotary_tables(rows, width):
    half = width // 2
    frequency = ROPE_BASE ** (-(jnp.arange(half, dtype=jnp.float32) * 2.0) / width)
    place = (jnp.arange(rows, dtype=jnp.int32) % SEQ_LEN).astype(jnp.float32)
    angle = place[:, None] * frequency[None, :]
    angle = jnp.concatenate([angle, angle], axis=1)
    return (jnp.cos(angle), jnp.sin(angle))


def rotate(values, cosine, sine):
    half = values.shape[-1] // 2
    turned = jnp.concatenate([-values[..., half:], values[..., :half]], axis=-1)
    return values * cosine[:, None, :] + turned * sine[:, None, :]


def rotate_back(grads, cosine, sine):
    half = grads.shape[-1] // 2
    moved = grads * sine[:, None, :]
    turned = jnp.concatenate([moved[..., half:], -moved[..., :half]], axis=-1)
    return grads * cosine[:, None, :] + turned


def block_scores(query, keys, live, start, block):
    base = start // SEQ_LEN * SEQ_LEN
    picked = lax.dynamic_slice_in_dim(query, start, block, 0)
    window = lax.dynamic_slice_in_dim(keys, base, SEQ_LEN, 0)
    allowed = lax.dynamic_slice_in_dim(live, base, SEQ_LEN, 0)
    scores = jnp.einsum(
        "qhd,khd->hqk", picked, window, preferred_element_type=jnp.float32
    ) * query.shape[2] ** (-0.5)
    return (jnp.where(allowed[None, None, :] > 0, scores, FLOOR_SCORE), picked, window, base)


def attend(query, keys, values, live):
    rows, heads, width = query.shape
    block = min(512, SEQ_LEN)

    def one_block(index):
        start = index * block
        scores, _, _, base = block_scores(query, keys, live, start, block)
        seq_values = lax.dynamic_slice_in_dim(values, base, SEQ_LEN, 0)
        top = jnp.max(scores, axis=2, keepdims=True)
        weights = jnp.exp(scores - top)
        total = jnp.sum(weights, axis=2, keepdims=True)
        probs = (weights / total).astype(jnp.bfloat16)
        mixed = jnp.einsum("hqk,khd->qhd", probs, seq_values, preferred_element_type=jnp.float32)
        return (mixed.astype(jnp.bfloat16), (top + jnp.log(total))[:, :, 0])

    mixed, log_total = lax.map(one_block, jnp.arange(rows // block, dtype=jnp.int32))
    return (mixed.reshape(rows, heads * width), log_total)


def attend_back(query, keys, values, live, log_total, grad_mixed):
    rows, heads, width = query.shape
    block = min(512, SEQ_LEN)
    scale = width ** (-0.5)
    zeros = jnp.zeros((rows, heads, width), jnp.float32)

    def one_block(index, carry):
        grad_query, grad_keys, grad_values = carry
        start = index * block
        scores, picked, window, base = block_scores(query, keys, live, start, block)
        probs = jnp.exp(scores - log_total[index][:, :, None])
        seq_values = lax.dynamic_slice_in_dim(values, base, SEQ_LEN, 0)
        grad_block = lax.dynamic_slice_in_dim(grad_mixed, start, block, 0)
        grad_probs = jnp.einsum(
            "qhd,khd->hqk", grad_block, seq_values, preferred_element_type=jnp.float32
        )
        inner = jnp.sum(probs * grad_probs, axis=2, keepdims=True)
        grad_scores = (probs * (grad_probs - inner)).astype(jnp.bfloat16)
        part_query = (
            jnp.einsum("hqk,khd->qhd", grad_scores, window, preferred_element_type=jnp.float32)
            * scale
        )
        part_keys = (
            jnp.einsum("hqk,qhd->khd", grad_scores, picked, preferred_element_type=jnp.float32)
            * scale
        )
        part_values = jnp.einsum(
            "hqk,qhd->khd",
            probs.astype(jnp.bfloat16),
            grad_block,
            preferred_element_type=jnp.float32,
        )
        grad_query = lax.dynamic_update_slice_in_dim(grad_query, part_query, start, 0)
        grad_keys = lax.dynamic_update_slice_in_dim(
            grad_keys, lax.dynamic_slice_in_dim(grad_keys, base, SEQ_LEN, 0) + part_keys, base, 0
        )
        grad_values = lax.dynamic_update_slice_in_dim(
            grad_values,
            lax.dynamic_slice_in_dim(grad_values, base, SEQ_LEN, 0) + part_values,
            base,
            0,
        )
        return (grad_query, grad_keys, grad_values)

    return lax.fori_loop(0, rows // block, one_block, (zeros, zeros, zeros))


def general_shards(
    hidden_in,
    teacher,
    valid_mask,
    first_gain,
    second_gain,
    attention_in,
    attention_out,
    feed_in,
    feed_out,
):
    columns = lax.axis_size("col")
    own_rows = hidden_in.shape[0]
    group = own_rows * columns
    own_start = lax.axis_index("col") * own_rows
    group_start = lax.axis_index("row") * group
    total_tokens = group * lax.axis_size("row")
    live_group = lax.dynamic_slice_in_dim(valid_mask, group_start, group, 0)
    live_own = lax.dynamic_slice_in_dim(live_group, own_start, own_rows, 0).astype(jnp.float32)
    valid_total = jnp.sum(valid_mask.astype(jnp.float32))
    joint_rows, attention_rows, feed_in_rows, feed_out_rows = (
        lax.all_gather(attention_in, "row", axis=2, tiled=True),
        lax.all_gather(attention_out, "row", axis=0, tiled=True),
        lax.all_gather(feed_in, "row", axis=2, tiled=True),
        lax.all_gather(feed_out, "row", axis=0, tiled=True),
    )
    inputs = hidden_in.astype(jnp.float32)
    normed_one, inverse_one, low_one = layer_norm(inputs, first_gain)
    joint = jnp.einsum(
        "rd,icd->ric",
        lax.all_gather(low_one, "col", axis=0, tiled=True),
        joint_rows,
        preferred_element_type=jnp.float32,
    )
    local_width = joint.shape[2]
    split = (group, local_width // HD, HD)
    cosine, sine = rotary_tables(group, HD)
    query = rotate(joint[:, 0].reshape(split), cosine, sine).astype(jnp.bfloat16)
    keys = rotate(joint[:, 1].reshape(split), cosine, sine).astype(jnp.bfloat16)
    values = joint[:, 2].reshape(split).astype(jnp.bfloat16)
    mixed, log_total = attend(query, keys, values, live_group)
    part = mixed
    branch = lax.psum_scatter(
        jnp.einsum("rc,oc->ro", part, attention_rows, preferred_element_type=jnp.float32),
        "col",
        scatter_dimension=0,
        tiled=True,
    )
    middle = inputs + branch
    normed_two, inverse_two, low_two = layer_norm(middle, second_gain)
    projected = jnp.einsum(
        "rd,ifd->rif",
        lax.all_gather(low_two, "col", axis=0, tiled=True),
        feed_in_rows,
        preferred_element_type=jnp.float32,
    )
    gate = projected[:, 0]
    upper = projected[:, 1]
    activated = (jax.nn.gelu(gate, approximate=False) * upper).astype(jnp.bfloat16)
    part = activated
    feed_branch = lax.psum_scatter(
        jnp.einsum("rf,of->ro", part, feed_out_rows, preferred_element_type=jnp.float32),
        "col",
        scatter_dimension=0,
        tiled=True,
    )
    result = middle + feed_branch
    error_term = result - teacher
    squares = jnp.sum(live_own * jnp.sum(error_term * error_term, axis=1))
    grad_result = (total_tokens * live_own)[:, None] * error_term / valid_total
    grad_low = grad_result.astype(jnp.bfloat16)
    piece = lax.all_gather(grad_low, "col", axis=0, tiled=True)
    part = activated
    grad_out = jnp.einsum("ro,rf->of", piece, part, preferred_element_type=jnp.float32)
    rows_grad = jnp.einsum("ro,of->rf", piece, feed_out_rows, preferred_element_type=jnp.float32)
    grad_act = rows_grad

    def geglu(first, second):
        return jax.nn.gelu(first, approximate=False) * second

    _, pull = jax.vjp(geglu, gate, upper)
    grad_gate, grad_upper = pull(grad_act)
    grad_projected = jnp.stack([grad_gate, grad_upper], axis=1).astype(jnp.bfloat16)
    part = grad_projected
    grad_low_two = lax.psum_scatter(
        jnp.einsum("rif,ifd->rd", part, feed_in_rows, preferred_element_type=jnp.float32),
        "col",
        scatter_dimension=0,
        tiled=True,
    )
    grad_middle_norm, grad_second = norm_back(grad_low_two, normed_two, inverse_two, second_gain)
    grad_middle = grad_result + grad_middle_norm
    grad_branch = grad_middle.astype(jnp.bfloat16)
    piece = lax.all_gather(grad_branch, "col", axis=0, tiled=True)
    part = mixed
    grad_weight = jnp.einsum("ro,rc->oc", piece, part, preferred_element_type=jnp.float32)
    rows_grad = jnp.einsum("ro,oc->rc", piece, attention_rows, preferred_element_type=jnp.float32)
    grad_heads = rows_grad
    grad_attention_rows, grad_heads = (grad_weight, grad_heads)
    grad_mixed = grad_heads.astype(jnp.bfloat16)
    grad_query, grad_keys, grad_values = attend_back(
        query, keys, values, live_group, log_total, grad_mixed.reshape(split)
    )
    grad_joint = jnp.stack(
        [rotate_back(grad_query, cosine, sine), rotate_back(grad_keys, cosine, sine), grad_values],
        axis=1,
    )
    grad_joint = grad_joint.astype(jnp.bfloat16).reshape(group, 3, local_width)
    part = grad_joint
    grad_low_one = lax.psum_scatter(
        jnp.einsum("ric,icd->rd", part, joint_rows, preferred_element_type=jnp.float32).astype(
            jnp.bfloat16
        ),
        "col",
        scatter_dimension=0,
        tiled=True,
    ).astype(jnp.float32)
    grad_input_norm, grad_first = norm_back(grad_low_one, normed_one, inverse_one, first_gain)
    grad_input = grad_middle + grad_input_norm
    grad_joint_weight = jnp.einsum(
        "ric,rd->icd",
        grad_joint,
        lax.all_gather(low_one, "col", axis=0, tiled=True),
        preferred_element_type=jnp.float32,
    )
    grad_feed_weight = jnp.einsum(
        "rif,rd->ifd",
        grad_projected,
        lax.all_gather(low_two, "col", axis=0, tiled=True),
        preferred_element_type=jnp.float32,
    )
    grads = (
        lax.psum_scatter(
            grad_joint_weight.astype(jnp.bfloat16), "row", scatter_dimension=2, tiled=True
        ).astype(jnp.float32),
        lax.psum_scatter(
            grad_attention_rows.astype(jnp.bfloat16), "row", scatter_dimension=0, tiled=True
        ).astype(jnp.float32),
        lax.psum_scatter(
            grad_feed_weight.astype(jnp.bfloat16), "row", scatter_dimension=2, tiled=True
        ).astype(jnp.float32),
        lax.psum_scatter(
            grad_out.astype(jnp.bfloat16), "row", scatter_dimension=0, tiled=True
        ).astype(jnp.float32),
    )
    totals = lax.psum((grad_first, grad_second, squares), ("row", "col"))
    loss = totals[2] / (D * valid_total)
    return (
        result.astype(jnp.bfloat16),
        loss,
        grad_input,
        totals[0],
        totals[1],
        grads[0],
        grads[1],
        grads[2],
        grads[3],
    )


BF = jnp.bfloat16
F32 = jnp.float32
MASKED = -1e30
ROW_DIMS = (((1,), (1,)), ((), ()))
HEAD_DIMS = (((0,), (0,)), ((), ()))
PLAIN_DIMS = (((1,), (0,)), ((), ()))


def swap(values, axis, flip):
    size = lax.axis_size(axis)
    return lax.ppermute(values, axis, [(place, place ^ flip) for place in range(size)])


def row_blocks(block):
    parts = [block] + [swap(block, "row", 2 * step) for step in range(1, 4)]
    blocks = []
    for part in parts:
        blocks += [part, swap(part, "row", 1)]
    return blocks, parts


def dot(left, right, dims):
    return lax.dot_general(left, right, dims, preferred_element_type=F32)


def turn(values, cosine, sine):
    lane = lax.broadcasted_iota(jnp.int32, values.shape, 1)
    swapped = jnp.where(
        lane % HD < HD // 2, pltpu.roll(values, 2 * HD - HD // 2, 1), pltpu.roll(values, HD // 2, 1)
    )
    return values * cosine + swapped * sine


def tables(inner, outer, start):
    cos_in, sin_in = inner[0], inner[1]
    cos_out = outer[0, pl.ds(start, 1)]
    sin_out = outer[1, pl.ds(start, 1)]
    lane = lax.broadcasted_iota(jnp.int32, cos_in.shape, 1)
    sign = jnp.where(lane % HD < HD // 2, -1.0, 1.0)
    cosine = cos_in * cos_out - sin_in * sin_out
    return cosine, (sin_in * cos_out + cos_in * sin_out) * sign


def project_kernel(row_ref, x0, x1, x2, x3, *rest):
    weights = rest[:8]
    inner, outer, bias_ref, tokens, joint, query, keys, values = rest[8:]
    step = pl.program_id(0)
    row = row_ref[0]
    pairs = joint.shape[0] // 384

    @pl.when(step == 0)
    def _():
        for index, weight in enumerate(weights):
            start = pl.multiple_of((row ^ index) * 128, 128)
            for pair in range(pairs):
                for kind in range(3):
                    at = (3 * pair + kind) * 128
                    old = (kind * pairs + pair) * 128
                    joint[at : at + 128, pl.ds(start, 128)] = weight[old : old + 128]

    for index, source in enumerate((x0, x1, x2, x3)):

        @pl.when(step == index)
        def _(source=source):
            tokens[...] = source[...]

    result = dot(tokens[...], joint[...], ROW_DIMS)
    cosine, sine = tables(inner, outer, step)
    rows = result.shape[0]
    lane = lax.broadcasted_iota(jnp.int32, (rows, 128), 1)
    spare = lane % HD
    one = jnp.ones((rows, 128), F32)
    zero = jnp.zeros((rows, 128), F32)
    key_spare = jnp.where(spare == 0, bias_ref[...] * one, jnp.where(spare <= 3, one, zero))
    query_spare = jnp.where(spare == 0, one, zero)
    for pair in range(pairs):
        at = pair * 384
        q = turn(result[:, at : at + 128], cosine, sine) * HD**-0.5
        k = turn(result[:, at + 128 : at + 256], cosine, sine)
        v = result[:, at + 256 : at + 384]
        for side in range(2):
            mine = (lane < HD) if side == 0 else (lane >= HD)
            query[2 * pair + side] = jnp.where(mine, q, query_spare).astype(BF)
            keys[2 * pair + side] = jnp.where(mine, k, key_spare).astype(BF)
            values[2 * pair + side] = jnp.where(mine, v, one).astype(BF)


def project(row, tokens, weights, inner, outer, bias):
    rows = tokens[0].shape[0]
    total = rows * len(tokens)
    width = weights[0].shape[0]
    heads = width // 3 // HD
    whole = lambda array: pl.BlockSpec(array.shape, lambda i, r: (0,) * array.ndim)
    wide = pl.BlockSpec((heads, rows, 128), lambda i, r: (0, i, 0))
    joint_shape = jax.ShapeDtypeStruct((width, D), BF)
    head_shape = jax.ShapeDtypeStruct((heads, total, 128), BF)
    return pl.pallas_call(
        project_kernel,
        out_shape=(
            jax.ShapeDtypeStruct((total, D), BF),
            joint_shape,
            head_shape,
            head_shape,
            head_shape,
        ),
        grid_spec=pltpu.PrefetchScalarGridSpec(
            num_scalar_prefetch=1,
            grid=(len(tokens),),
            in_specs=[whole(t) for t in tokens]
            + [whole(w) for w in weights]
            + [whole(inner), whole(outer), pl.BlockSpec((rows, 1), lambda i, r: (i, 0))],
            out_specs=(
                pl.BlockSpec((rows, D), lambda i, r: (i, 0)),
                pl.BlockSpec((width, D), lambda i, r: (0, 0)),
                wide,
                wide,
                wide,
            ),
        ),
        cost_estimate=pl.CostEstimate(
            flops=2 * total * width * D, transcendentals=0, bytes_accessed=8 * total * D
        ),
        name="project",
    )(row, *tokens, *weights, inner, outer, bias)


def split_three(column):
    high = column.astype(BF).astype(F32)
    rest = column - high
    middle = rest.astype(BF).astype(F32)
    return high, middle, rest - middle


def attend_kernel(query, keys, values, mixed, exact, query_back):
    rows = mixed.shape[0]
    lane = lax.broadcasted_iota(jnp.int32, (rows, 128), 1)
    spare = lane % HD
    outs = []
    for side in range(2):
        q = query[side]
        scores = dot(q, keys[side], ROW_DIMS)
        top = jnp.max(scores, axis=1, keepdims=True)
        weights = jnp.exp(scores - top).astype(BF)
        out = dot(weights, values[side], PLAIN_DIMS)
        at = HD if side == 0 else 0
        total = out[:, at : at + 1]
        outs.append(out / total)
        high, middle, low = split_three(top + jnp.log(total))
        mine = (lane < HD) if side == 0 else (lane >= HD)
        extra = jnp.where(spare == 1, -high, jnp.where(spare == 2, -middle, -low))
        keep = jnp.logical_or(mine, jnp.logical_or(spare == 0, spare > 3))
        query_back[side] = jnp.where(keep, q.astype(F32), extra).astype(BF)
    both = jnp.where(lane < HD, outs[0], outs[1])
    exact[...] = both
    mixed[...] = both.astype(BF)


def attend_pair(pair, query, keys, values, block):
    _, rows, _ = query.shape
    part = pl.BlockSpec((2, block, 128), lambda i: (pair, i, 0))
    whole = pl.BlockSpec((2, rows, 128), lambda i: (pair, 0, 0))
    out = pl.BlockSpec((block, 128), lambda i: (i, 0))
    return pl.pallas_call(
        attend_kernel,
        out_shape=(
            jax.ShapeDtypeStruct((rows, 128), BF),
            jax.ShapeDtypeStruct((rows, 128), F32),
            jax.ShapeDtypeStruct((2, rows, 128), BF),
        ),
        grid=(rows // block,),
        in_specs=[part, whole, whole],
        out_specs=(out, out, pl.BlockSpec((2, block, 128), lambda i: (0, i, 0))),
        cost_estimate=pl.CostEstimate(
            flops=16 * rows * rows * 128, transcendentals=0, bytes_accessed=8 * rows * 128
        ),
        name="attend",
    )(query, keys, values)


def attend_back_kernel(query, grad, exact, keys, values, inner, outer, *refs):
    out, grad_keys, grad_values = refs[-3:]
    step = pl.program_id(0)
    rows = grad.shape[0]
    total = keys.shape[1]
    lane = lax.broadcasted_iota(jnp.int32, (rows, 128), 1)
    spare = lane % HD

    @pl.when(step == 0)
    def _():
        grad_keys[...] = jnp.zeros_like(grad_keys)
        grad_values[...] = jnp.zeros_like(grad_values)

    product = grad[...].astype(F32) * exact[...]
    sides = []
    for side in range(2):
        q = query[side]
        mine = (lane < HD) if side == 0 else (lane >= HD)
        total_grad = jnp.sum(jnp.where(mine, product, 0.0), axis=1, keepdims=True)
        high, middle, low = split_three(total_grad)
        extra = jnp.where(
            spare == 0, -high, jnp.where(spare == 1, -middle, jnp.where(spare == 2, -low, 0.0))
        )
        g = jnp.where(mine, grad[...].astype(F32), extra).astype(BF)
        grad_query = jnp.zeros((128, rows), F32)
        for start in range(0, total, rows):
            k = keys[side, start : start + rows]
            v = values[side, start : start + rows]
            probs = jnp.exp(dot(k, q, ROW_DIMS))
            slope = (probs * dot(v, g, ROW_DIMS)).astype(BF)
            grad_values[side, start : start + rows] += dot(probs.astype(BF), g, PLAIN_DIMS)
            grad_keys[side, start : start + rows] += dot(slope, q, PLAIN_DIMS)
            grad_query += dot(k, slope, HEAD_DIMS)
        sides.append(grad_query)
    row = lax.broadcasted_iota(jnp.int32, (128, rows), 0)
    both = jnp.where(row < HD, sides[0], sides[1]).T * HD**-0.5
    cosine, sine = tables(inner, outer, step)
    from_row = pl.multiple_of(step * rows, rows)
    out[pl.ds(from_row, rows), :128] = turn(both, cosine, -sine).astype(BF)

    @pl.when(step == pl.num_programs(0) - 1)
    def _():
        for block in range(total // rows):
            here = slice(block * rows, (block + 1) * rows)
            k = jnp.where(lane < HD, grad_keys[0, here], grad_keys[1, here])
            v = jnp.where(lane < HD, grad_values[0, here], grad_values[1, here])
            cosine, sine = tables(inner, outer, block)
            out[here, 128:256] = turn(k, cosine, -sine).astype(BF)
            out[here, 256:] = v.astype(BF)


def attend_back_pair(pair, query, grad, exact, keys, values, inner, outer, held):
    heads, rows, _ = keys.shape
    block = inner.shape[1]
    part = pl.BlockSpec((2, block, 128), lambda i: (0, i, 0))
    whole = pl.BlockSpec((2, rows, 128), lambda i: (pair, 0, 0))
    fixed = lambda array: pl.BlockSpec(array.shape, lambda i: (0,) * array.ndim)
    return pl.pallas_call(
        attend_back_kernel,
        out_shape=jax.ShapeDtypeStruct((rows, 3 * heads * HD), BF),
        grid=(rows // block,),
        in_specs=[
            part,
            pl.BlockSpec((block, 128), lambda i: (i, pair)),
            pl.BlockSpec((block, 128), lambda i: (i, 0)),
            whole,
            whole,
            fixed(inner),
            fixed(outer),
        ]
        + [pl.BlockSpec(memory_space=pl.ANY)] * len(held),
        out_specs=pl.BlockSpec((rows, 3 * 128), lambda i: (0, pair)),
        scratch_shapes=[pltpu.VMEM((2, rows, 128), F32), pltpu.VMEM((2, rows, 128), F32)],
        input_output_aliases={7 + i: i for i in range(len(held))},
        cost_estimate=pl.CostEstimate(
            flops=48 * rows * rows * HD, transcendentals=0, bytes_accessed=8 * rows * HD
        ),
        name="attend_back",
    )(query, grad, exact, keys, values, inner, outer, *held)


def pick(step, sources, target):
    for index, source in enumerate(sources):

        @pl.when(step == index)
        def _(source=source):
            target[...] = source[...]


def share(step, part, keep, send):
    @pl.when(step % 2 == 0)
    def _():
        keep[...] = part

    @pl.when(step % 2 == 1)
    def _():
        send[...] = part.astype(BF)


def feed_kernel(row_ref, *refs, count, blocks, held):
    sources, second = refs[:count], refs[count]
    firsts = refs[count + 1 : count + 1 + blocks]
    tokens, act, slope, gelu_out, keep, send = refs[count + 1 + blocks + held :][:6]
    step = pl.program_id(0)
    first = firsts[0] if blocks == 1 else refs[-1]
    if blocks > 1:

        @pl.when(step == 0)
        def _():
            for index, block in enumerate(firsts):
                start = pl.multiple_of((row_ref[0] ^ index) * 128, 128)
                first[:, pl.ds(start, 128)] = block[...]

    hidden = first.shape[0] // 2
    pick(step, sources, tokens)
    x = tokens[...]
    gate = dot(x, first[:hidden], ROW_DIMS)
    upper = dot(x, first[hidden:], ROW_DIMS)
    phi = 0.5 * (1.0 + lax.erf(gate * 2**-0.5))
    gelu = gate * phi
    low = (gelu * upper).astype(BF)
    density = jnp.exp(-0.5 * gate * gate) * 0.3989422804014327
    act[...] = low
    slope[...] = (upper * (phi + gate * density)).astype(BF)
    gelu_out[...] = gelu.astype(BF)
    share(step, dot(low, second[...], ROW_DIMS), keep, send)


def feed(row, tokens, firsts, second, total, start, held):
    count = len(tokens)
    blocks = len(firsts)
    rows = tokens[0].shape[0]
    hidden = second.shape[1]
    fixed = lambda array: pl.BlockSpec(array.shape, lambda i, r: (0,) * array.ndim)
    tall = pl.BlockSpec((rows, hidden), lambda i, r: (i + start, 0))
    wide = pl.BlockSpec((rows, D), lambda i, r: (i + start, 0))
    half = pl.BlockSpec((rows, D), lambda i, r: (i // 2, 0))
    hidden_shape = jax.ShapeDtypeStruct((total, hidden), BF)
    size = rows * count
    first_shape = [jax.ShapeDtypeStruct((2 * hidden, D), BF)] * (blocks > 1)
    return pl.pallas_call(
        functools.partial(feed_kernel, count=count, blocks=blocks, held=len(held)),
        out_shape=(
            jax.ShapeDtypeStruct((total, D), BF),
            hidden_shape,
            hidden_shape,
            hidden_shape,
            jax.ShapeDtypeStruct((size // 2, D), F32),
            jax.ShapeDtypeStruct((size // 2, D), BF),
            *first_shape,
        ),
        grid_spec=pltpu.PrefetchScalarGridSpec(
            num_scalar_prefetch=1,
            grid=(count,),
            in_specs=[fixed(t) for t in tokens]
            + [fixed(second)]
            + [fixed(f) for f in firsts]
            + [pl.BlockSpec(memory_space=pl.ANY)] * len(held),
            out_specs=(wide, tall, tall, tall, half, half, *map(fixed, first_shape)),
        ),
        input_output_aliases={count + 2 + blocks + i: i for i in range(len(held))},
        cost_estimate=pl.CostEstimate(
            flops=6 * size * hidden * D, transcendentals=0, bytes_accessed=6 * hidden * D
        ),
        name="feed",
    )(row, *tokens, second, *firsts, *held)


def feed_back_kernel(*refs, count, held):
    sources, (slope, gelu, first, second) = refs[:count], refs[count : count + 4]
    grads, out, keep, send = refs[count + 4 + held :]
    step = pl.program_id(0)
    pick(step, sources, grads)
    grad_act = dot(grads[...], second[...], PLAIN_DIMS)
    gate = (grad_act * slope[...].astype(F32)).astype(BF)
    upper = (grad_act * gelu[...].astype(F32)).astype(BF)
    out[0] = gate
    out[1] = upper
    hidden = first.shape[0] // 2
    part = dot(gate, first[:hidden], PLAIN_DIMS) + dot(upper, first[hidden:], PLAIN_DIMS)
    share(step, part, keep, send)


def feed_back(grads, slope, gelu, first, second, start, held):
    count = len(grads)
    rows = grads[0].shape[0]
    total, hidden = slope.shape
    fixed = lambda array: pl.BlockSpec(array.shape, lambda i: (0,) * array.ndim)
    tall = pl.BlockSpec((rows, hidden), lambda i: (i + start, 0))
    wide = pl.BlockSpec((rows, D), lambda i: (i + start, 0))
    half = pl.BlockSpec((rows, D), lambda i: (i // 2, 0))
    size = rows * count
    return pl.pallas_call(
        functools.partial(feed_back_kernel, count=count, held=len(held)),
        out_shape=(
            jax.ShapeDtypeStruct((total, D), BF),
            jax.ShapeDtypeStruct((2, total, hidden), BF),
            jax.ShapeDtypeStruct((size // 2, D), F32),
            jax.ShapeDtypeStruct((size // 2, D), BF),
        ),
        grid=(count,),
        in_specs=[fixed(t) for t in grads]
        + [tall, tall, fixed(first), fixed(second)]
        + [pl.BlockSpec(memory_space=pl.ANY)] * len(held),
        out_specs=(wide, pl.BlockSpec((2, rows, hidden), lambda i: (0, i + start, 0)), half, half),
        input_output_aliases={count + 4 + i: i for i in range(len(held))},
        cost_estimate=pl.CostEstimate(
            flops=6 * size * hidden * D, transcendentals=0, bytes_accessed=6 * hidden * D
        ),
        name="feed_back",
    )(*grads, slope, gelu, first, second, *held)


def pack_kernel(row_ref, *refs):
    half = len(refs) // 2
    for source, target in zip(refs[:half], refs[half:]):
        target[0] = source[...]


def pack(row, tall, wide):
    ins, in_specs, shapes, out_specs = [], [], [], []
    for array, is_tall in [(a, True) for a in tall] + [(a, False) for a in wide]:
        block = (128, array.shape[1]) if is_tall else (array.shape[0], 128)
        for odd in range(2):
            if is_tall:
                index = lambda j, r, odd=odd: ((2 * j + odd) ^ r[0], 0)
            else:
                index = lambda j, r, odd=odd: (0, (2 * j + odd) ^ r[0])
            ins.append(array)
            in_specs.append(pl.BlockSpec(block, index))
            shapes.append(jax.ShapeDtypeStruct((4, *block), BF))
            out_specs.append(pl.BlockSpec((1, *block), lambda j, r: (j, 0, 0)))
    return pl.pallas_call(
        pack_kernel,
        out_shape=shapes,
        grid_spec=pltpu.PrefetchScalarGridSpec(
            num_scalar_prefetch=1, grid=(4,), in_specs=in_specs, out_specs=out_specs
        ),
        name="pack",
    )(row, *ins)


def stack_kernel(*refs):
    at = 0
    for source in refs[:-1]:
        rows = source.shape[0]
        refs[-1][0, at : at + rows] = source[...]
        at += rows


def stack_wide(arrays):
    rows = sum(array.shape[0] for array in arrays)
    blocks = arrays[0].shape[1] // 128
    return pl.pallas_call(
        stack_kernel,
        out_shape=jax.ShapeDtypeStruct((blocks, rows, 128), BF),
        grid=(blocks,),
        in_specs=[pl.BlockSpec((array.shape[0], 128), lambda k: (0, k)) for array in arrays],
        out_specs=pl.BlockSpec((1, rows, 128), lambda k: (k, 0, 0)),
        name="stack",
    )(*arrays)


def sum_far(near):
    total = near[0]
    for step in range(1, 4):
        total = total + swap(near[step].astype(BF), "row", 2 * step).astype(F32)
    return total


def add_all(values):
    for axis in ("col", "row"):
        flip = 1
        while flip < lax.axis_size(axis):
            values = values + swap(values, axis, flip)
            flip *= 2
    return values


def group_shards(
    hidden_in,
    teacher,
    valid_mask,
    first_gain,
    second_gain,
    attention_in,
    attention_out,
    feed_in,
    feed_out,
):
    own = hidden_in.shape[0]
    column = lax.axis_index("col")
    row = lax.axis_index("row")
    group = own * 4
    group_start = row * group
    total_tokens = group * lax.axis_size("row")
    valid_total = jnp.sum(valid_mask.astype(F32))
    live_group = lax.dynamic_slice_in_dim(valid_mask, group_start, group, 0)
    live_own = lax.dynamic_slice_in_dim(live_group, column * own, own, 0).astype(F32)
    order = jnp.arange(4, dtype=jnp.int32) ^ column
    live = jnp.take(live_group.reshape(4, own), order, axis=0).reshape(group, 1)
    bias = jnp.where(live > 0, 0.0, MASKED).astype(F32)
    half = HD // 2
    frequency = ROPE_BASE ** (-(jnp.arange(half, dtype=F32) * 2.0) / HD)
    frequency = jnp.tile(frequency, 4)[None, :]
    inner = jnp.arange(own, dtype=F32)[:, None] * frequency
    inner = jnp.stack([jnp.cos(inner), jnp.sin(inner)])
    outer = (order * own).astype(F32)[:, None] * frequency
    outer = jnp.stack([jnp.cos(outer), jnp.sin(outer)])

    inputs = hidden_in.astype(F32)
    normed_one, inverse_one, low_one = layer_norm(inputs, first_gain)
    width = attention_in.shape[1]
    out_twin = swap(attention_out, "col", 2)
    joint_blocks, joint_parts = row_blocks(attention_in.reshape(3 * width, attention_in.shape[2]))
    far = swap(low_one, "col", 2)
    near = swap(low_one, "col", 1)
    hidden = feed_in.shape[1]
    index = row.reshape(1)
    feed_in, feed_out, attention_out, out_twin, *_ = lax.optimization_barrier(
        (feed_in, feed_out, attention_out, out_twin, *joint_parts)
    )
    tokens = [low_one, near, far, swap(far, "col", 1)]
    out_rows = lax.all_gather(
        jnp.concatenate([attention_out, out_twin, feed_out], axis=1), "row", axis=0, tiled=True
    )
    feed_in_blocks, _ = row_blocks(feed_in.reshape(2 * hidden, 128))
    all_low_one, joint, query, keys, values = project(
        index, tokens, joint_blocks, inner, outer, bias
    )
    mixed, exact, query_back, mixed_twin = [], [], [], []
    for pair in range(width // 128):
        pair_mixed, pair_exact, pair_query = attend_pair(pair, query, keys, values, 512)
        mixed.append(pair_mixed)
        exact.append(pair_exact)
        query_back.append(pair_query)
        mixed_twin.append(swap(pair_mixed[2 * own :], "col", 2))
    mixed = jnp.concatenate([m[: 2 * own] for m in mixed], axis=1)
    mixed_twin = jnp.concatenate(mixed_twin, axis=1)
    attention_rows = out_rows[:, :width]
    attention_twin = out_rows[:, width : 2 * width]
    feed_out_rows = out_rows[:, 2 * width :]
    mixed_own = mixed[: 2 * own]
    near = dot(mixed_own[own:], attention_rows, ROW_DIMS) + dot(
        mixed_twin[own:], attention_twin, ROW_DIMS
    )
    near = swap(near, "col", 1)
    branch = (
        dot(mixed_own[:own], attention_rows, ROW_DIMS)
        + dot(mixed_twin[:own], attention_twin, ROW_DIMS)
        + near
    )
    middle = inputs + branch
    normed_two, inverse_two, low_two = layer_norm(middle, second_gain)

    chunks = 2
    size = own // chunks
    parts = [slice(i * size, (i + 1) * size) for i in range(chunks)]
    far = [swap(low_two[here], "col", 2) for here in parts]
    near = []
    for here in parts:
        near += [low_two[here], swap(low_two[here], "col", 1)]
    *kept, keep_near, send_near, feed_in_rows = feed(
        index, near, feed_in_blocks, feed_out_rows, group, 0, []
    )
    far[0], kept[0] = lax.optimization_barrier((far[0], kept[0]))
    got_near = swap(send_near, "col", 1)
    sums = []
    gate_to = None
    for i in range(chunks):
        there = far[i]
        if gate_to is not None:
            there, gate_to = lax.optimization_barrier((there, gate_to))
            sums[-1] = gate_to
        there = [there, swap(there, "col", 1)]
        *kept, keep, send = feed(
            index, there, [feed_in_rows], feed_out_rows, group, 2 * chunks + 2 * i, kept
        )
        gate_to = (keep + swap(send, "col", 1).astype(F32)).astype(BF)
        sums.append(gate_to)
    all_low_two, act, slope, gelu = kept
    squares = jnp.float32(0.0)
    results, grad_results, far, held, nears = [], [], [], [], []
    for i, here in enumerate(parts):
        got_far = swap(sums[i], "col", 2)
        if held:
            got_far, held[0] = lax.optimization_barrier((got_far, held[0]))
        result = (
            middle[here]
            + keep_near[here]
            + got_near[here].astype(F32)
            + got_far.astype(F32)
        )
        results.append(result)
        error_term = result - teacher[here]
        live_here = live_own[here]
        squares = squares + jnp.sum(live_here * jnp.sum(error_term * error_term, axis=1))
        grad_result = (total_tokens * live_here)[:, None] * error_term / valid_total
        grad_results.append(grad_result)
        low = grad_result.astype(BF)
        far.append(swap(low, "col", 2))
        low = [low, swap(low, "col", 1)]
        *held, keep, send = feed_back(low, slope, gelu, feed_in_rows, feed_out_rows, 2 * i, held)
        nears.append(keep + swap(send, "col", 1).astype(F32))
    sums = []
    gate_to = None
    for i in range(chunks):
        there = far[i]
        if gate_to is not None:
            there, gate_to = lax.optimization_barrier((there, gate_to))
            sums[-1] = gate_to
        there = [there, swap(there, "col", 1)]
        *held, keep, send = feed_back(
            there,
            slope,
            gelu,
            feed_in_rows,
            feed_out_rows,
            2 * chunks + 2 * i,
            held,
        )
        gate_to = (keep + swap(send, "col", 1).astype(F32)).astype(BF)
        sums.append(gate_to)
    all_grads, grad_hidden = held
    all_grads, grad_hidden, gate_to = lax.optimization_barrier((all_grads, grad_hidden, gate_to))
    sums[-1] = gate_to
    grad_out = dot(act, all_grads, HEAD_DIMS).astype(BF)
    grad_feed = jnp.einsum("irf,rd->ifd", grad_hidden, all_low_two, preferred_element_type=F32)
    grad_feed = stack_wide([grad_feed.astype(BF).reshape(2 * hidden, D), grad_out])
    grad_second = jnp.zeros((D,), F32)
    grad_middles = []
    for i, here in enumerate(parts):
        got_far = swap(sums[i], "col", 2)
        if i == chunks - 1:
            got_far, grad_feed = lax.optimization_barrier((got_far, grad_feed))
        grad_low_two = nears[i] + got_far.astype(F32)
        grad_norm, grad_gain = norm_back(
            grad_low_two, normed_two[here], inverse_two[here], second_gain
        )
        grad_second = grad_second + grad_gain
        grad_middles.append(grad_results[i] + grad_norm)
    result = jnp.concatenate(results, axis=0)
    grad_middle = jnp.concatenate(grad_middles, axis=0)
    grad_branch = grad_middle.astype(BF)

    branch_pair = jnp.concatenate([grad_branch, swap(grad_branch, "col", 1)], axis=0)
    grad_mixed_twin = swap(dot(branch_pair, attention_twin, PLAIN_DIMS).astype(BF), "col", 2)
    grad_mixed = jnp.concatenate(
        [dot(branch_pair, attention_rows, PLAIN_DIMS).astype(BF), grad_mixed_twin], axis=0
    )
    grad_attention_far = swap(dot(branch_pair, mixed_twin, HEAD_DIMS).astype(BF), "col", 2)
    grad_attention = dot(branch_pair, mixed_own, HEAD_DIMS) + grad_attention_far.astype(F32)
    attention_keep, attention_send = pack(index, [grad_attention.astype(BF)], [])
    near_attention = attention_keep.astype(F32) + swap(attention_send, "row", 1).astype(F32)
    held, joint_near = [], []
    grad_first = jnp.zeros((D,), F32)
    for pair in range(width // 128):
        grad_joint = attend_back_pair(
            pair,
            query_back[pair],
            grad_mixed,
            exact[pair],
            keys,
            values,
            inner,
            outer,
            held,
        )
        held = [grad_joint]
        here = slice(pair * 384, (pair + 1) * 384)
        grad_pair = grad_joint[:, here]
        if pair == width // 128 - 1:
            part = dot(grad_joint[2 * own :], joint, PLAIN_DIMS)
            far = part[:own] + swap(part[own:].astype(BF), "col", 1).astype(F32)
            grad_pair, far = lax.optimization_barrier((grad_pair, far.astype(BF)))
        weight = dot(grad_pair, all_low_one, HEAD_DIMS)
        grad_first = grad_first + jnp.sum(weight * joint[here].astype(F32), axis=0)
        keep, send = pack(index, [], [weight.astype(BF)])
        near_sum = keep.astype(F32) + swap(send, "row", 1).astype(F32)
        if pair == 0:
            held, send = lax.optimization_barrier((held, send))
        joint_near.append(near_sum)
    part = dot(grad_joint[: 2 * own], joint, PLAIN_DIMS)
    near = part[:own] + swap(part[own:].astype(BF), "col", 1).astype(F32)
    grad_low_one = near + swap(far, "col", 2).astype(F32)
    grad_first = grad_first / first_gain
    totals = add_all(
        jnp.concatenate(
            [grad_first.reshape(8, 128), grad_second.reshape(8, 128), jnp.full((8, 128), squares)]
        )
    )
    grad_input_norm, _ = norm_back(grad_low_one, normed_one, inverse_one, first_gain)
    grad_input = grad_middle + grad_input_norm
    feed_sum = lax.psum_scatter(grad_feed, "row", scatter_dimension=0, tiled=True)
    feed_sum = feed_sum.astype(F32).reshape(3 * hidden, 128)
    joint_sums = [sum_far(near).reshape(3, 128, 128) for near in joint_near]
    grads = (
        jnp.concatenate(joint_sums, axis=1),
        sum_far(near_attention),
        feed_sum[: 2 * hidden].reshape(2, hidden, 128),
        feed_sum[2 * hidden :].T,
    )
    loss = totals[16, 0] / (D * valid_total)
    return (
        result.astype(BF),
        loss,
        grad_input,
        totals[:8].reshape(D),
        totals[8:16].reshape(D),
        grads[0],
        grads[1],
        grads[2],
        grads[3],
    )


def shards(hidden_in, teacher, valid_mask, first_gain, second_gain, attention_in, *rest):
    fits = (
        lax.axis_size("col") == 4
        and lax.axis_size("row") == 8
        and hidden_in.shape[0] * 4 == SEQ_LEN
        and attention_in.shape[1] % 128 == 0
    )
    body = group_shards if fits else general_shards
    return body(
        hidden_in, teacher, valid_mask, first_gain, second_gain, attention_in, *rest
    )


def solution(mesh):
    in_specs = (
        P(("row", "col"), None),
        P(("row", "col"), None),
        P(),
        P(),
        P(),
        P(None, "col", "row"),
        P("row", "col"),
        P(None, "col", "row"),
        P("row", "col"),
    )
    out_specs = (
        P(("row", "col"), None),
        P(),
        P(("row", "col"), None),
        P(),
        P(),
        P(None, "col", "row"),
        P("row", "col"),
        P(None, "col", "row"),
        P("row", "col"),
    )
    return jax.shard_map(
        shards, mesh=mesh, in_specs=in_specs, out_specs=out_specs, check_vma=False
    )
```

```python
import functools

import jax
import jax.numpy as jnp
from jax import lax
from jax.experimental import pallas as pl
from jax.experimental.pallas import tpu as pltpu
from jax.sharding import PartitionSpec as P

D = 1024
HD = 64
SEQ_LEN = 2048


EPSILON = 1e-05
ROPE_BASE = 160000.0
FLOOR_SCORE = -1e30


def layer_norm(values, gain):
    center = values - jnp.mean(values, axis=1, keepdims=True)
    inverse = lax.rsqrt(jnp.mean(center * center, axis=1, keepdims=True) + EPSILON)
    normed = center * inverse
    return (normed, inverse, (normed * gain).astype(jnp.bfloat16))


def norm_back(grad_low, normed, inverse, gain):
    scaled = grad_low * gain
    inner = jnp.mean(scaled * normed, axis=1, keepdims=True)
    centered = scaled - jnp.mean(scaled, axis=1, keepdims=True)
    return (inverse * (centered - normed * inner), jnp.sum(grad_low * normed, axis=0))


def rotary_tables(rows, width):
    half = width // 2
    frequency = ROPE_BASE ** (-(jnp.arange(half, dtype=jnp.float32) * 2.0) / width)
    place = (jnp.arange(rows, dtype=jnp.int32) % SEQ_LEN).astype(jnp.float32)
    angle = place[:, None] * frequency[None, :]
    angle = jnp.concatenate([angle, angle], axis=1)
    return (jnp.cos(angle), jnp.sin(angle))


def rotate(values, cosine, sine):
    half = values.shape[-1] // 2
    turned = jnp.concatenate([-values[..., half:], values[..., :half]], axis=-1)
    return values * cosine[:, None, :] + turned * sine[:, None, :]


def rotate_back(grads, cosine, sine):
    half = grads.shape[-1] // 2
    moved = grads * sine[:, None, :]
    turned = jnp.concatenate([moved[..., half:], -moved[..., :half]], axis=-1)
    return grads * cosine[:, None, :] + turned


def block_scores(query, keys, live, start, block):
    base = start // SEQ_LEN * SEQ_LEN
    picked = lax.dynamic_slice_in_dim(query, start, block, 0)
    window = lax.dynamic_slice_in_dim(keys, base, SEQ_LEN, 0)
    allowed = lax.dynamic_slice_in_dim(live, base, SEQ_LEN, 0)
    scores = jnp.einsum(
        "qhd,khd->hqk", picked, window, preferred_element_type=jnp.float32
    ) * query.shape[2] ** (-0.5)
    return (jnp.where(allowed[None, None, :] > 0, scores, FLOOR_SCORE), picked, window, base)


def attend(query, keys, values, live):
    rows, heads, width = query.shape
    block = min(512, SEQ_LEN)

    def one_block(index):
        start = index * block
        scores, _, _, base = block_scores(query, keys, live, start, block)
        seq_values = lax.dynamic_slice_in_dim(values, base, SEQ_LEN, 0)
        top = jnp.max(scores, axis=2, keepdims=True)
        weights = jnp.exp(scores - top)
        total = jnp.sum(weights, axis=2, keepdims=True)
        probs = (weights / total).astype(jnp.bfloat16)
        mixed = jnp.einsum("hqk,khd->qhd", probs, seq_values, preferred_element_type=jnp.float32)
        return (mixed.astype(jnp.bfloat16), (top + jnp.log(total))[:, :, 0])

    mixed, log_total = lax.map(one_block, jnp.arange(rows // block, dtype=jnp.int32))
    return (mixed.reshape(rows, heads * width), log_total)


def attend_back(query, keys, values, live, log_total, grad_mixed):
    rows, heads, width = query.shape
    block = min(512, SEQ_LEN)
    scale = width ** (-0.5)
    zeros = jnp.zeros((rows, heads, width), jnp.float32)

    def one_block(index, carry):
        grad_query, grad_keys, grad_values = carry
        start = index * block
        scores, picked, window, base = block_scores(query, keys, live, start, block)
        probs = jnp.exp(scores - log_total[index][:, :, None])
        seq_values = lax.dynamic_slice_in_dim(values, base, SEQ_LEN, 0)
        grad_block = lax.dynamic_slice_in_dim(grad_mixed, start, block, 0)
        grad_probs = jnp.einsum(
            "qhd,khd->hqk", grad_block, seq_values, preferred_element_type=jnp.float32
        )
        inner = jnp.sum(probs * grad_probs, axis=2, keepdims=True)
        grad_scores = (probs * (grad_probs - inner)).astype(jnp.bfloat16)
        part_query = (
            jnp.einsum("hqk,khd->qhd", grad_scores, window, preferred_element_type=jnp.float32)
            * scale
        )
        part_keys = (
            jnp.einsum("hqk,qhd->khd", grad_scores, picked, preferred_element_type=jnp.float32)
            * scale
        )
        part_values = jnp.einsum(
            "hqk,qhd->khd",
            probs.astype(jnp.bfloat16),
            grad_block,
            preferred_element_type=jnp.float32,
        )
        grad_query = lax.dynamic_update_slice_in_dim(grad_query, part_query, start, 0)
        grad_keys = lax.dynamic_update_slice_in_dim(
            grad_keys, lax.dynamic_slice_in_dim(grad_keys, base, SEQ_LEN, 0) + part_keys, base, 0
        )
        grad_values = lax.dynamic_update_slice_in_dim(
            grad_values,
            lax.dynamic_slice_in_dim(grad_values, base, SEQ_LEN, 0) + part_values,
            base,
            0,
        )
        return (grad_query, grad_keys, grad_values)

    return lax.fori_loop(0, rows // block, one_block, (zeros, zeros, zeros))


def general_shards(
    hidden_in,
    teacher,
    valid_mask,
    first_gain,
    second_gain,
    attention_in,
    attention_out,
    feed_in,
    feed_out,
):
    columns = lax.axis_size("col")
    own_rows = hidden_in.shape[0]
    group = own_rows * columns
    own_start = lax.axis_index("col") * own_rows
    group_start = lax.axis_index("row") * group
    total_tokens = group * lax.axis_size("row")
    live_group = lax.dynamic_slice_in_dim(valid_mask, group_start, group, 0)
    live_own = lax.dynamic_slice_in_dim(live_group, own_start, own_rows, 0).astype(jnp.float32)
    valid_total = jnp.sum(valid_mask.astype(jnp.float32))
    joint_rows, attention_rows, feed_in_rows, feed_out_rows = (
        lax.all_gather(attention_in, "row", axis=2, tiled=True),
        lax.all_gather(attention_out, "row", axis=0, tiled=True),
        lax.all_gather(feed_in, "row", axis=2, tiled=True),
        lax.all_gather(feed_out, "row", axis=0, tiled=True),
    )
    inputs = hidden_in.astype(jnp.float32)
    normed_one, inverse_one, low_one = layer_norm(inputs, first_gain)
    joint = jnp.einsum(
        "rd,icd->ric",
        lax.all_gather(low_one, "col", axis=0, tiled=True),
        joint_rows,
        preferred_element_type=jnp.float32,
    )
    local_width = joint.shape[2]
    split = (group, local_width // HD, HD)
    cosine, sine = rotary_tables(group, HD)
    query = rotate(joint[:, 0].reshape(split), cosine, sine).astype(jnp.bfloat16)
    keys = rotate(joint[:, 1].reshape(split), cosine, sine).astype(jnp.bfloat16)
    values = joint[:, 2].reshape(split).astype(jnp.bfloat16)
    mixed, log_total = attend(query, keys, values, live_group)
    part = mixed
    branch = lax.psum_scatter(
        jnp.einsum("rc,oc->ro", part, attention_rows, preferred_element_type=jnp.float32),
        "col",
        scatter_dimension=0,
        tiled=True,
    )
    middle = inputs + branch
    normed_two, inverse_two, low_two = layer_norm(middle, second_gain)
    projected = jnp.einsum(
        "rd,ifd->rif",
        lax.all_gather(low_two, "col", axis=0, tiled=True),
        feed_in_rows,
        preferred_element_type=jnp.float32,
    )
    gate = projected[:, 0]
    upper = projected[:, 1]
    activated = (jax.nn.gelu(gate, approximate=False) * upper).astype(jnp.bfloat16)
    part = activated
    feed_branch = lax.psum_scatter(
        jnp.einsum("rf,of->ro", part, feed_out_rows, preferred_element_type=jnp.float32),
        "col",
        scatter_dimension=0,
        tiled=True,
    )
    result = middle + feed_branch
    error_term = result - teacher
    squares = jnp.sum(live_own * jnp.sum(error_term * error_term, axis=1))
    grad_result = (total_tokens * live_own)[:, None] * error_term / valid_total
    grad_low = grad_result.astype(jnp.bfloat16)
    piece = lax.all_gather(grad_low, "col", axis=0, tiled=True)
    part = activated
    grad_out = jnp.einsum("ro,rf->of", piece, part, preferred_element_type=jnp.float32)
    rows_grad = jnp.einsum("ro,of->rf", piece, feed_out_rows, preferred_element_type=jnp.float32)
    grad_act = rows_grad

    def geglu(first, second):
        return jax.nn.gelu(first, approximate=False) * second

    _, pull = jax.vjp(geglu, gate, upper)
    grad_gate, grad_upper = pull(grad_act)
    grad_projected = jnp.stack([grad_gate, grad_upper], axis=1).astype(jnp.bfloat16)
    part = grad_projected
    grad_low_two = lax.psum_scatter(
        jnp.einsum("rif,ifd->rd", part, feed_in_rows, preferred_element_type=jnp.float32),
        "col",
        scatter_dimension=0,
        tiled=True,
    )
    grad_middle_norm, grad_second = norm_back(grad_low_two, normed_two, inverse_two, second_gain)
    grad_middle = grad_result + grad_middle_norm
    grad_branch = grad_middle.astype(jnp.bfloat16)
    piece = lax.all_gather(grad_branch, "col", axis=0, tiled=True)
    part = mixed
    grad_weight = jnp.einsum("ro,rc->oc", piece, part, preferred_element_type=jnp.float32)
    rows_grad = jnp.einsum("ro,oc->rc", piece, attention_rows, preferred_element_type=jnp.float32)
    grad_heads = rows_grad
    grad_attention_rows, grad_heads = (grad_weight, grad_heads)
    grad_mixed = grad_heads.astype(jnp.bfloat16)
    grad_query, grad_keys, grad_values = attend_back(
        query, keys, values, live_group, log_total, grad_mixed.reshape(split)
    )
    grad_joint = jnp.stack(
        [rotate_back(grad_query, cosine, sine), rotate_back(grad_keys, cosine, sine), grad_values],
        axis=1,
    )
    grad_joint = grad_joint.astype(jnp.bfloat16).reshape(group, 3, local_width)
    part = grad_joint
    grad_low_one = lax.psum_scatter(
        jnp.einsum("ric,icd->rd", part, joint_rows, preferred_element_type=jnp.float32).astype(
            jnp.bfloat16
        ),
        "col",
        scatter_dimension=0,
        tiled=True,
    ).astype(jnp.float32)
    grad_input_norm, grad_first = norm_back(grad_low_one, normed_one, inverse_one, first_gain)
    grad_input = grad_middle + grad_input_norm
    grad_joint_weight = jnp.einsum(
        "ric,rd->icd",
        grad_joint,
        lax.all_gather(low_one, "col", axis=0, tiled=True),
        preferred_element_type=jnp.float32,
    )
    grad_feed_weight = jnp.einsum(
        "rif,rd->ifd",
        grad_projected,
        lax.all_gather(low_two, "col", axis=0, tiled=True),
        preferred_element_type=jnp.float32,
    )
    grads = (
        lax.psum_scatter(
            grad_joint_weight.astype(jnp.bfloat16), "row", scatter_dimension=2, tiled=True
        ).astype(jnp.float32),
        lax.psum_scatter(
            grad_attention_rows.astype(jnp.bfloat16), "row", scatter_dimension=0, tiled=True
        ).astype(jnp.float32),
        lax.psum_scatter(
            grad_feed_weight.astype(jnp.bfloat16), "row", scatter_dimension=2, tiled=True
        ).astype(jnp.float32),
        lax.psum_scatter(
            grad_out.astype(jnp.bfloat16), "row", scatter_dimension=0, tiled=True
        ).astype(jnp.float32),
    )
    totals = lax.psum((grad_first, grad_second, squares), ("row", "col"))
    loss = totals[2] / (D * valid_total)
    return (
        result.astype(jnp.bfloat16),
        loss,
        grad_input,
        totals[0],
        totals[1],
        grads[0],
        grads[1],
        grads[2],
        grads[3],
    )


ROW, COL = "row", "col"
BF = jnp.bfloat16
F32 = jnp.float32
MASKED = -1e30
ROW_DIMS = (((1,), (1,)), ((), ()))
HEAD_DIMS = (((0,), (0,)), ((), ()))
PLAIN_DIMS = (((1,), (0,)), ((), ()))


def swap(values, axis, flip):
    size = lax.axis_size(axis)
    return lax.ppermute(values, axis, [(place, place ^ flip) for place in range(size)])


def row_blocks(block):
    parts = [block] + [swap(block, ROW, 2 * step) for step in range(1, 4)]
    blocks = []
    for part in parts:
        blocks += [part, swap(part, ROW, 1)]
    return blocks, parts


def dot(left, right, dims):
    return lax.dot_general(left, right, dims, preferred_element_type=F32)


def turn(values, cosine, sine):
    lane = lax.broadcasted_iota(jnp.int32, values.shape, 1)
    swapped = jnp.where(
        lane % HD < HD // 2, pltpu.roll(values, 2 * HD - HD // 2, 1), pltpu.roll(values, HD // 2, 1)
    )
    return values * cosine + swapped * sine


def tables(inner, outer, start):
    cos_in, sin_in = inner[0], inner[1]
    cos_out = outer[0, pl.ds(start, 1)]
    sin_out = outer[1, pl.ds(start, 1)]
    lane = lax.broadcasted_iota(jnp.int32, cos_in.shape, 1)
    sign = jnp.where(lane % HD < HD // 2, -1.0, 1.0)
    cosine = cos_in * cos_out - sin_in * sin_out
    return cosine, (sin_in * cos_out + cos_in * sin_out) * sign


def project_kernel(row_ref, x0, x1, x2, x3, *rest):
    weights = rest[:8]
    inner, outer, bias_ref, tokens, joint, query, keys, values = rest[8:]
    step = pl.program_id(0)
    row = row_ref[0]
    pairs = joint.shape[0] // 384

    @pl.when(step == 0)
    def _():
        for index, weight in enumerate(weights):
            start = pl.multiple_of((row ^ index) * 128, 128)
            for pair in range(pairs):
                for kind in range(3):
                    at = (3 * pair + kind) * 128
                    old = (kind * pairs + pair) * 128
                    joint[at : at + 128, pl.ds(start, 128)] = weight[old : old + 128]

    for index, source in enumerate((x0, x1, x2, x3)):

        @pl.when(step == index)
        def _(source=source):
            tokens[...] = source[...]

    result = dot(tokens[...], joint[...], ROW_DIMS)
    cosine, sine = tables(inner, outer, step)
    rows = result.shape[0]
    lane = lax.broadcasted_iota(jnp.int32, (rows, 128), 1)
    spare = lane % HD
    one = jnp.ones((rows, 128), F32)
    zero = jnp.zeros((rows, 128), F32)
    key_spare = jnp.where(spare == 0, bias_ref[...] * one, jnp.where(spare <= 3, one, zero))
    query_spare = jnp.where(spare == 0, one, zero)
    for pair in range(pairs):
        at = pair * 384
        q = turn(result[:, at : at + 128], cosine, sine) * HD**-0.5
        k = turn(result[:, at + 128 : at + 256], cosine, sine)
        v = result[:, at + 256 : at + 384]
        for side in range(2):
            mine = (lane < HD) if side == 0 else (lane >= HD)
            query[2 * pair + side] = jnp.where(mine, q, query_spare).astype(BF)
            keys[2 * pair + side] = jnp.where(mine, k, key_spare).astype(BF)
            values[2 * pair + side] = jnp.where(mine, v, one).astype(BF)


def project(row, tokens, weights, inner, outer, bias):
    rows = tokens[0].shape[0]
    total = rows * len(tokens)
    width = weights[0].shape[0]
    heads = width // 3 // HD
    whole = lambda array: pl.BlockSpec(array.shape, lambda i, r: (0,) * array.ndim)
    wide = pl.BlockSpec((heads, rows, 128), lambda i, r: (0, i, 0))
    joint_shape = jax.ShapeDtypeStruct((width, D), BF)
    head_shape = jax.ShapeDtypeStruct((heads, total, 128), BF)
    return pl.pallas_call(
        project_kernel,
        out_shape=(
            jax.ShapeDtypeStruct((total, D), BF),
            joint_shape,
            head_shape,
            head_shape,
            head_shape,
        ),
        grid_spec=pltpu.PrefetchScalarGridSpec(
            num_scalar_prefetch=1,
            grid=(len(tokens),),
            in_specs=[whole(t) for t in tokens]
            + [whole(w) for w in weights]
            + [whole(inner), whole(outer), pl.BlockSpec((rows, 1), lambda i, r: (i, 0))],
            out_specs=(
                pl.BlockSpec((rows, D), lambda i, r: (i, 0)),
                pl.BlockSpec((width, D), lambda i, r: (0, 0)),
                wide,
                wide,
                wide,
            ),
        ),
        cost_estimate=pl.CostEstimate(
            flops=2 * total * width * D, transcendentals=0, bytes_accessed=8 * total * D
        ),
    )(row, *tokens, *weights, inner, outer, bias)


def split_three(column):
    high = column.astype(BF).astype(F32)
    rest = column - high
    middle = rest.astype(BF).astype(F32)
    return high, middle, rest - middle


def attend_kernel(query, keys, values, mixed, exact, query_back):
    rows = mixed.shape[0]
    lane = lax.broadcasted_iota(jnp.int32, (rows, 128), 1)
    spare = lane % HD
    outs = []
    for side in range(2):
        q = query[side]
        scores = dot(q, keys[side], ROW_DIMS)
        top = jnp.max(scores, axis=1, keepdims=True)
        weights = jnp.exp(scores - top).astype(BF)
        out = dot(weights, values[side], PLAIN_DIMS)
        at = HD if side == 0 else 0
        total = out[:, at : at + 1]
        outs.append(out / total)
        high, middle, low = split_three(top + jnp.log(total))
        mine = (lane < HD) if side == 0 else (lane >= HD)
        extra = jnp.where(spare == 1, -high, jnp.where(spare == 2, -middle, -low))
        keep = jnp.logical_or(mine, jnp.logical_or(spare == 0, spare > 3))
        query_back[side] = jnp.where(keep, q.astype(F32), extra).astype(BF)
    both = jnp.where(lane < HD, outs[0], outs[1])
    exact[...] = both
    mixed[...] = both.astype(BF)


def attend_pair(pair, query, keys, values, block):
    _, rows, _ = query.shape
    part = pl.BlockSpec((2, block, 128), lambda i: (pair, i, 0))
    whole = pl.BlockSpec((2, rows, 128), lambda i: (pair, 0, 0))
    out = pl.BlockSpec((block, 128), lambda i: (i, 0))
    return pl.pallas_call(
        attend_kernel,
        out_shape=(
            jax.ShapeDtypeStruct((rows, 128), BF),
            jax.ShapeDtypeStruct((rows, 128), F32),
            jax.ShapeDtypeStruct((2, rows, 128), BF),
        ),
        grid=(rows // block,),
        in_specs=[part, whole, whole],
        out_specs=(out, out, pl.BlockSpec((2, block, 128), lambda i: (0, i, 0))),
        cost_estimate=pl.CostEstimate(
            flops=16 * rows * rows * 128, transcendentals=0, bytes_accessed=8 * rows * 128
        ),
    )(query, keys, values)


def attend_back_kernel(query, grad, exact, keys, values, inner, outer, *refs):
    out, grad_keys, grad_values = refs[-3:]
    step = pl.program_id(0)
    rows = grad.shape[0]
    total = keys.shape[1]
    lane = lax.broadcasted_iota(jnp.int32, (rows, 128), 1)
    spare = lane % HD

    @pl.when(step == 0)
    def _():
        grad_keys[...] = jnp.zeros_like(grad_keys)
        grad_values[...] = jnp.zeros_like(grad_values)

    product = grad[...].astype(F32) * exact[...]
    sides = []
    for side in range(2):
        q = query[side]
        mine = (lane < HD) if side == 0 else (lane >= HD)
        total_grad = jnp.sum(jnp.where(mine, product, 0.0), axis=1, keepdims=True)
        high, middle, low = split_three(total_grad)
        extra = jnp.where(
            spare == 0, -high, jnp.where(spare == 1, -middle, jnp.where(spare == 2, -low, 0.0))
        )
        g = jnp.where(mine, grad[...].astype(F32), extra).astype(BF)
        grad_query = jnp.zeros((128, rows), F32)
        for start in range(0, total, rows):
            k = keys[side, start : start + rows]
            v = values[side, start : start + rows]
            probs = jnp.exp(dot(k, q, ROW_DIMS))
            slope = (probs * dot(v, g, ROW_DIMS)).astype(BF)
            grad_values[side, start : start + rows] += dot(probs.astype(BF), g, PLAIN_DIMS)
            grad_keys[side, start : start + rows] += dot(slope, q, PLAIN_DIMS)
            grad_query += dot(k, slope, HEAD_DIMS)
        sides.append(grad_query)
    row = lax.broadcasted_iota(jnp.int32, (128, rows), 0)
    both = jnp.where(row < HD, sides[0], sides[1]).T * HD**-0.5
    cosine, sine = tables(inner, outer, step)
    from_row = pl.multiple_of(step * rows, rows)
    out[pl.ds(from_row, rows), :128] = turn(both, cosine, -sine).astype(BF)

    @pl.when(step == pl.num_programs(0) - 1)
    def _():
        for block in range(total // rows):
            here = slice(block * rows, (block + 1) * rows)
            k = jnp.where(lane < HD, grad_keys[0, here], grad_keys[1, here])
            v = jnp.where(lane < HD, grad_values[0, here], grad_values[1, here])
            cosine, sine = tables(inner, outer, block)
            out[here, 128:256] = turn(k, cosine, -sine).astype(BF)
            out[here, 256:] = v.astype(BF)


def attend_back_pair(pair, query, grad, exact, keys, values, inner, outer, held):
    heads, rows, _ = keys.shape
    block = inner.shape[1]
    part = pl.BlockSpec((2, block, 128), lambda i: (0, i, 0))
    whole = pl.BlockSpec((2, rows, 128), lambda i: (pair, 0, 0))
    fixed = lambda array: pl.BlockSpec(array.shape, lambda i: (0,) * array.ndim)
    return pl.pallas_call(
        attend_back_kernel,
        out_shape=jax.ShapeDtypeStruct((rows, 3 * heads * HD), BF),
        grid=(rows // block,),
        in_specs=[
            part,
            pl.BlockSpec((block, 128), lambda i: (i, pair)),
            pl.BlockSpec((block, 128), lambda i: (i, 0)),
            whole,
            whole,
            fixed(inner),
            fixed(outer),
        ]
        + [pl.BlockSpec(memory_space=pl.ANY)] * len(held),
        out_specs=pl.BlockSpec((rows, 3 * 128), lambda i: (0, pair)),
        scratch_shapes=[pltpu.VMEM((2, rows, 128), F32), pltpu.VMEM((2, rows, 128), F32)],
        input_output_aliases={7 + i: i for i in range(len(held))},
        cost_estimate=pl.CostEstimate(
            flops=48 * rows * rows * HD, transcendentals=0, bytes_accessed=8 * rows * HD
        ),
    )(query, grad, exact, keys, values, inner, outer, *held)


def pick(step, sources, target):
    for index, source in enumerate(sources):

        @pl.when(step == index)
        def _(source=source):
            target[...] = source[...]


def share(step, part, keep, send):
    @pl.when(step % 2 == 0)
    def _():
        keep[...] = part

    @pl.when(step % 2 == 1)
    def _():
        send[...] = part.astype(BF)


def feed_kernel(row_ref, *refs, count, blocks, held):
    sources, second = refs[:count], refs[count]
    firsts = refs[count + 1 : count + 1 + blocks]
    tokens, act, slope, gelu_out, keep, send = refs[count + 1 + blocks + held :][:6]
    step = pl.program_id(0)
    first = firsts[0] if blocks == 1 else refs[-1]
    if blocks > 1:

        @pl.when(step == 0)
        def _():
            for index, block in enumerate(firsts):
                start = pl.multiple_of((row_ref[0] ^ index) * 128, 128)
                first[:, pl.ds(start, 128)] = block[...]

    hidden = first.shape[0] // 2
    pick(step, sources, tokens)
    x = tokens[...]
    gate = dot(x, first[:hidden], ROW_DIMS)
    upper = dot(x, first[hidden:], ROW_DIMS)
    phi = 0.5 * (1.0 + lax.erf(gate * 2**-0.5))
    gelu = gate * phi
    low = (gelu * upper).astype(BF)
    density = jnp.exp(-0.5 * gate * gate) * 0.3989422804014327
    act[...] = low
    slope[...] = (upper * (phi + gate * density)).astype(BF)
    gelu_out[...] = gelu.astype(BF)
    share(step, dot(low, second[...], ROW_DIMS), keep, send)


def feed(row, tokens, firsts, second, total, start, held):
    count = len(tokens)
    blocks = len(firsts)
    rows = tokens[0].shape[0]
    hidden = second.shape[1]
    fixed = lambda array: pl.BlockSpec(array.shape, lambda i, r: (0,) * array.ndim)
    tall = pl.BlockSpec((rows, hidden), lambda i, r: (i + start, 0))
    wide = pl.BlockSpec((rows, D), lambda i, r: (i + start, 0))
    half = pl.BlockSpec((rows, D), lambda i, r: (i // 2, 0))
    hidden_shape = jax.ShapeDtypeStruct((total, hidden), BF)
    size = rows * count
    first_shape = [jax.ShapeDtypeStruct((2 * hidden, D), BF)] * (blocks > 1)
    return pl.pallas_call(
        functools.partial(feed_kernel, count=count, blocks=blocks, held=len(held)),
        out_shape=(
            jax.ShapeDtypeStruct((total, D), BF),
            hidden_shape,
            hidden_shape,
            hidden_shape,
            jax.ShapeDtypeStruct((size // 2, D), F32),
            jax.ShapeDtypeStruct((size // 2, D), BF),
            *first_shape,
        ),
        grid_spec=pltpu.PrefetchScalarGridSpec(
            num_scalar_prefetch=1,
            grid=(count,),
            in_specs=[fixed(t) for t in tokens]
            + [fixed(second)]
            + [fixed(f) for f in firsts]
            + [pl.BlockSpec(memory_space=pl.ANY)] * len(held),
            out_specs=(wide, tall, tall, tall, half, half, *map(fixed, first_shape)),
        ),
        input_output_aliases={count + 2 + blocks + i: i for i in range(len(held))},
        cost_estimate=pl.CostEstimate(
            flops=6 * size * hidden * D, transcendentals=0, bytes_accessed=6 * hidden * D
        ),
    )(row, *tokens, second, *firsts, *held)


def feed_back_kernel(*refs, count, held):
    sources, (slope, gelu, first, second) = refs[:count], refs[count : count + 4]
    grads, out, keep, send = refs[count + 4 + held :]
    step = pl.program_id(0)
    pick(step, sources, grads)
    grad_act = dot(grads[...], second[...], PLAIN_DIMS)
    gate = (grad_act * slope[...].astype(F32)).astype(BF)
    upper = (grad_act * gelu[...].astype(F32)).astype(BF)
    out[0] = gate
    out[1] = upper
    hidden = first.shape[0] // 2
    part = dot(gate, first[:hidden], PLAIN_DIMS) + dot(upper, first[hidden:], PLAIN_DIMS)
    share(step, part, keep, send)


def feed_back(grads, slope, gelu, first, second, start, held):
    count = len(grads)
    rows = grads[0].shape[0]
    total, hidden = slope.shape
    fixed = lambda array: pl.BlockSpec(array.shape, lambda i: (0,) * array.ndim)
    tall = pl.BlockSpec((rows, hidden), lambda i: (i + start, 0))
    wide = pl.BlockSpec((rows, D), lambda i: (i + start, 0))
    half = pl.BlockSpec((rows, D), lambda i: (i // 2, 0))
    size = rows * count
    return pl.pallas_call(
        functools.partial(feed_back_kernel, count=count, held=len(held)),
        out_shape=(
            jax.ShapeDtypeStruct((total, D), BF),
            jax.ShapeDtypeStruct((2, total, hidden), BF),
            jax.ShapeDtypeStruct((size // 2, D), F32),
            jax.ShapeDtypeStruct((size // 2, D), BF),
        ),
        grid=(count,),
        in_specs=[fixed(t) for t in grads]
        + [tall, tall, fixed(first), fixed(second)]
        + [pl.BlockSpec(memory_space=pl.ANY)] * len(held),
        out_specs=(wide, pl.BlockSpec((2, rows, hidden), lambda i: (0, i + start, 0)), half, half),
        input_output_aliases={count + 4 + i: i for i in range(len(held))},
        cost_estimate=pl.CostEstimate(
            flops=6 * size * hidden * D, transcendentals=0, bytes_accessed=6 * hidden * D
        ),
    )(*grads, slope, gelu, first, second, *held)


def pack_kernel(row_ref, *refs):
    half = len(refs) // 2
    for source, target in zip(refs[:half], refs[half:]):
        target[0] = source[...]


def pack(row, tall, wide):
    ins, in_specs, shapes, out_specs = [], [], [], []
    for array, is_tall in [(a, True) for a in tall] + [(a, False) for a in wide]:
        block = (128, array.shape[1]) if is_tall else (array.shape[0], 128)
        for odd in range(2):
            if is_tall:
                index = lambda j, r, odd=odd: ((2 * j + odd) ^ r[0], 0)
            else:
                index = lambda j, r, odd=odd: (0, (2 * j + odd) ^ r[0])
            ins.append(array)
            in_specs.append(pl.BlockSpec(block, index))
            shapes.append(jax.ShapeDtypeStruct((4, *block), BF))
            out_specs.append(pl.BlockSpec((1, *block), lambda j, r: (j, 0, 0)))
    return pl.pallas_call(
        pack_kernel,
        out_shape=shapes,
        grid_spec=pltpu.PrefetchScalarGridSpec(
            num_scalar_prefetch=1, grid=(4,), in_specs=in_specs, out_specs=out_specs
        ),
    )(row, *ins)


def stack_kernel(*refs):
    at = 0
    for source in refs[:-1]:
        rows = source.shape[0]
        refs[-1][0, at : at + rows] = source[...]
        at += rows


def stack_wide(arrays):
    rows = sum(array.shape[0] for array in arrays)
    blocks = arrays[0].shape[1] // 128
    return pl.pallas_call(
        stack_kernel,
        out_shape=jax.ShapeDtypeStruct((blocks, rows, 128), BF),
        grid=(blocks,),
        in_specs=[pl.BlockSpec((array.shape[0], 128), lambda k: (0, k)) for array in arrays],
        out_specs=pl.BlockSpec((1, rows, 128), lambda k: (k, 0, 0)),
    )(*arrays)


def sum_far(near):
    total = near[0]
    for step in range(1, 4):
        total = total + swap(near[step].astype(BF), ROW, 2 * step).astype(F32)
    return total


def add_all(values):
    for axis, flip in ((ROW, 2), (ROW, 4), (COL, 1), (ROW, 1), (COL, 2)):
        values = values + swap(values, axis, flip)
    return values


def group_shards(
    hidden_in,
    teacher,
    valid_mask,
    first_gain,
    second_gain,
    attention_in,
    attention_out,
    feed_in,
    feed_out,
):
    own = hidden_in.shape[0]
    column = lax.axis_index(COL)
    row = lax.axis_index(ROW)
    group = own * 4
    group_start = row * group
    total_tokens = group * lax.axis_size(ROW)
    valid_total = jnp.sum(valid_mask.astype(F32))
    live_group = lax.dynamic_slice_in_dim(valid_mask, group_start, group, 0)
    live_own = lax.dynamic_slice_in_dim(live_group, column * own, own, 0).astype(F32)
    order = jnp.arange(4, dtype=jnp.int32) ^ column
    live = jnp.take(live_group.reshape(4, own), order, axis=0).reshape(group, 1)
    bias = jnp.where(live > 0, 0.0, MASKED).astype(F32)
    half = HD // 2
    frequency = ROPE_BASE ** (-(jnp.arange(half, dtype=F32) * 2.0) / HD)
    frequency = jnp.tile(frequency, 4)[None, :]
    inner = jnp.arange(own, dtype=F32)[:, None] * frequency
    inner = jnp.stack([jnp.cos(inner), jnp.sin(inner)])
    outer = (order * own).astype(F32)[:, None] * frequency
    outer = jnp.stack([jnp.cos(outer), jnp.sin(outer)])

    inputs = hidden_in.astype(F32)
    normed_one, inverse_one, low_one = layer_norm(inputs, first_gain)
    width = attention_in.shape[1]
    out_twin = swap(attention_out, COL, 2)
    joint_blocks, joint_parts = row_blocks(attention_in.reshape(3 * width, attention_in.shape[2]))
    far = swap(low_one, COL, 2)
    near = swap(low_one, COL, 1)
    hidden = feed_in.shape[1]
    index = row.reshape(1)
    feed_in, feed_out, attention_out, out_twin, *_ = lax.optimization_barrier(
        (feed_in, feed_out, attention_out, out_twin, *joint_parts)
    )
    tokens = [low_one, near, far, swap(far, COL, 1)]
    out_rows = lax.all_gather(
        jnp.concatenate([attention_out, out_twin, feed_out], axis=1), ROW, axis=0, tiled=True
    )
    feed_in_blocks, _ = row_blocks(feed_in.reshape(2 * hidden, 128))
    all_low_one, joint, query, keys, values = project(
        index, tokens, joint_blocks, inner, outer, bias
    )
    mixed, exact, query_back, mixed_twin = [], [], [], []
    for pair in range(width // 128):
        pair_mixed, pair_exact, pair_query = attend_pair(pair, query, keys, values, 512)
        mixed.append(pair_mixed)
        exact.append(pair_exact)
        query_back.append(pair_query)
        mixed_twin.append(swap(pair_mixed[2 * own :], COL, 2))
    mixed = jnp.concatenate([m[: 2 * own] for m in mixed], axis=1)
    mixed_twin = jnp.concatenate(mixed_twin, axis=1)
    attention_rows = out_rows[:, :width]
    attention_twin = out_rows[:, width : 2 * width]
    feed_out_rows = out_rows[:, 2 * width :]
    mixed_own = mixed[: 2 * own]
    near = dot(mixed_own[own:], attention_rows, ROW_DIMS) + dot(
        mixed_twin[own:], attention_twin, ROW_DIMS
    )
    near = swap(near, COL, 1)
    branch = (
        dot(mixed_own[:own], attention_rows, ROW_DIMS)
        + dot(mixed_twin[:own], attention_twin, ROW_DIMS)
        + near
    )
    middle = inputs + branch
    normed_two, inverse_two, low_two = layer_norm(middle, second_gain)

    chunks = 2
    size = own // chunks
    parts = [slice(i * size, (i + 1) * size) for i in range(chunks)]
    far = [swap(low_two[here], COL, 2) for here in parts]
    near = []
    for here in parts:
        near += [low_two[here], swap(low_two[here], COL, 1)]
    *kept, keep_near, send_near, feed_in_rows = feed(
        index, near, feed_in_blocks, feed_out_rows, group, 0, []
    )
    far[0], kept[0] = lax.optimization_barrier((far[0], kept[0]))
    got_near = swap(send_near, COL, 1)
    sums = []
    gate_to = None
    for i in range(chunks):
        there = far[i]
        if gate_to is not None:
            there, gate_to = lax.optimization_barrier((there, gate_to))
            sums[-1] = gate_to
        there = [there, swap(there, COL, 1)]
        *kept, keep, send = feed(
            index, there, [feed_in_rows], feed_out_rows, group, 2 * chunks + 2 * i, kept
        )
        gate_to = (keep + swap(send, COL, 1).astype(F32)).astype(BF)
        sums.append(gate_to)
    all_low_two, act, slope, gelu = kept
    squares = jnp.float32(0.0)
    results, grad_results, far, held, nears = [], [], [], [], []
    for i, here in enumerate(parts):
        got_far = swap(sums[i], COL, 2)
        if held:
            got_far, held[0] = lax.optimization_barrier((got_far, held[0]))
        result = (
            middle[here]
            + keep_near[here]
            + got_near[here].astype(F32)
            + got_far.astype(F32)
        )
        results.append(result)
        error_term = result - teacher[here]
        live_here = live_own[here]
        squares = squares + jnp.sum(live_here * jnp.sum(error_term * error_term, axis=1))
        grad_result = (total_tokens * live_here)[:, None] * error_term / valid_total
        grad_results.append(grad_result)
        low = grad_result.astype(BF)
        far.append(swap(low, COL, 2))
        low = [low, swap(low, COL, 1)]
        *held, keep, send = feed_back(low, slope, gelu, feed_in_rows, feed_out_rows, 2 * i, held)
        nears.append(keep + swap(send, COL, 1).astype(F32))
    sums = []
    gate_to = None
    for i in range(chunks):
        there = far[i]
        if gate_to is not None:
            there, gate_to = lax.optimization_barrier((there, gate_to))
            sums[-1] = gate_to
        there = [there, swap(there, COL, 1)]
        *held, keep, send = feed_back(
            there,
            slope,
            gelu,
            feed_in_rows,
            feed_out_rows,
            2 * chunks + 2 * i,
            held,
        )
        gate_to = (keep + swap(send, COL, 1).astype(F32)).astype(BF)
        sums.append(gate_to)
    all_grads, grad_hidden = held
    all_grads, grad_hidden, gate_to = lax.optimization_barrier((all_grads, grad_hidden, gate_to))
    sums[-1] = gate_to
    grad_feed = jnp.einsum("irf,rd->ifd", grad_hidden, all_low_two, preferred_element_type=F32)
    grad_feed = grad_feed.astype(BF).reshape(2 * hidden, D)
    grad_second = jnp.zeros((D,), F32)
    grad_middles = []
    for i, here in enumerate(parts):
        got_far = swap(sums[i], COL, 2)
        if i == chunks - 1:
            got_far, grad_feed = lax.optimization_barrier((got_far, grad_feed))
        grad_low_two = nears[i] + got_far.astype(F32)
        grad_norm, grad_gain = norm_back(
            grad_low_two, normed_two[here], inverse_two[here], second_gain
        )
        grad_second = grad_second + grad_gain
        grad_middles.append(grad_results[i] + grad_norm)
    result = jnp.concatenate(results, axis=0)
    grad_middle = jnp.concatenate(grad_middles, axis=0)
    grad_branch = grad_middle.astype(BF)

    grad_branch, all_grads = lax.optimization_barrier((grad_branch, all_grads))
    grad_out = dot(act, all_grads, HEAD_DIMS).astype(BF)
    branch_pair = jnp.concatenate([grad_branch, swap(grad_branch, COL, 1)], axis=0)
    grad_mixed_twin = swap(dot(branch_pair, attention_twin, PLAIN_DIMS).astype(BF), COL, 2)
    grad_feed = stack_wide([grad_feed, grad_out])
    grad_mixed = jnp.concatenate(
        [dot(branch_pair, attention_rows, PLAIN_DIMS).astype(BF), grad_mixed_twin], axis=0
    )
    grad_attention_far = swap(dot(branch_pair, mixed_twin, HEAD_DIMS).astype(BF), COL, 2)
    grad_attention = dot(branch_pair, mixed_own, HEAD_DIMS) + grad_attention_far.astype(F32)
    attention_keep, attention_send = pack(index, [grad_attention.astype(BF)], [])
    near_attention = attention_keep.astype(F32) + swap(attention_send, ROW, 1).astype(F32)
    held, joint_near = [], []
    grad_first = jnp.zeros((D,), F32)
    for pair in range(width // 128):
        grad_joint = attend_back_pair(
            pair,
            query_back[pair],
            grad_mixed,
            exact[pair],
            keys,
            values,
            inner,
            outer,
            held,
        )
        held = [grad_joint]
        here = slice(pair * 384, (pair + 1) * 384)
        grad_pair = grad_joint[:, here]
        last = pair == width // 128 - 1
        if last:
            far = swap(dot(grad_joint[3 * own :], joint, PLAIN_DIMS).astype(BF), COL, 1)
            far = dot(grad_joint[2 * own : 3 * own], joint, PLAIN_DIMS) + far.astype(F32)
            grad_pair, far = lax.optimization_barrier((grad_pair, far.astype(BF)))
        weight = dot(grad_pair, all_low_one, HEAD_DIMS)
        grad_first = grad_first + jnp.sum(weight * joint[here].astype(F32), axis=0)
        weight = weight.astype(BF)
        keep, send = pack(index, [], [weight])
        if last:
            send, grad_joint, grad_first, joint_near[0] = lax.optimization_barrier(
                (send, grad_joint, grad_first, joint_near[0])
            )
        near_sum = keep.astype(F32) + swap(send, ROW, 1).astype(F32)
        if pair == 0:
            held, send = lax.optimization_barrier((held, send))
        joint_near.append(near_sum)
    near = swap(dot(grad_joint[own : 2 * own], joint, PLAIN_DIMS).astype(BF), COL, 1)
    near = dot(grad_joint[:own], joint, PLAIN_DIMS) + near.astype(F32)
    grad_low_one = near + swap(far, COL, 2).astype(F32)
    grad_first = grad_first / first_gain
    totals = add_all(
        jnp.concatenate(
            [grad_first.reshape(8, 128), grad_second.reshape(8, 128), jnp.full((8, 128), squares)]
        )
    )
    grad_input_norm, _ = norm_back(grad_low_one, normed_one, inverse_one, first_gain)
    grad_input = grad_middle + grad_input_norm
    feed_sum = lax.psum_scatter(grad_feed, ROW, scatter_dimension=0, tiled=True)
    feed_sum = feed_sum.astype(F32).reshape(3 * hidden, 128)
    joint_sums = [sum_far(near).reshape(3, 128, 128) for near in joint_near]
    grads = (
        jnp.concatenate(joint_sums, axis=1),
        sum_far(near_attention),
        feed_sum[: 2 * hidden].reshape(2, hidden, 128),
        feed_sum[2 * hidden :].T,
    )
    loss = totals[16, 0] / (D * valid_total)
    return (
        result.astype(BF),
        loss,
        grad_input,
        totals[:8].reshape(D),
        totals[8:16].reshape(D),
        grads[0],
        grads[1],
        grads[2],
        grads[3],
    )


def shards(hidden_in, teacher, valid_mask, first_gain, second_gain, attention_in, *rest):
    fits = (
        lax.axis_size(COL) == 4
        and lax.axis_size(ROW) == 8
        and hidden_in.shape[0] * 4 == SEQ_LEN
        and attention_in.shape[1] % 128 == 0
    )
    body = group_shards if fits else general_shards
    return body(
        hidden_in, teacher, valid_mask, first_gain, second_gain, attention_in, *rest
    )


def solution(mesh):
    in_specs = (
        P(("row", "col"), None),
        P(("row", "col"), None),
        P(),
        P(),
        P(),
        P(None, "col", "row"),
        P("row", "col"),
        P(None, "col", "row"),
        P("row", "col"),
    )
    out_specs = (
        P(("row", "col"), None),
        P(),
        P(("row", "col"), None),
        P(),
        P(),
        P(None, "col", "row"),
        P("row", "col"),
        P(None, "col", "row"),
        P("row", "col"),
    )
    return jax.shard_map(
        shards, mesh=mesh, in_specs=in_specs, out_specs=out_specs, check_vma=False
    )
```
